32 devices in a mesh: dp: 4 (over y, core), ctx: 8 (over z, x).
Axes of the slice: x: 2, y: 2, z: 4, core: 2. Of those that a mesh axis runs over, the one named last changes fastest.
Arguments:
- features: bfloat16 [4, 8, 248, 12288], P('dp', 'ctx'), may hold values from -6 to 6
- counts: int32 [4, 8], P('dp', 'ctx'), may hold values from 8 to 248, as said below
- short_taps: float32 [7, 3, 4096], P(None, None, 'ctx'), may hold values from -2 to 2
- residue: float32 [16, 256], P(None, 'ctx'), may hold values from -0.25 to 0.25
- decay_rate: float32 [16, 256], P(None, 'ctx'), may hold values from 1.953125e-05 to 0.05
- skip_gain: float32 [4096], P('ctx'), may hold values from -4 to 4
- cotangent: bfloat16 [4, 8, 248, 4096], P('dp', 'ctx'), may hold values from -6 to 6
Outputs:
- output: bfloat16 [4, 8, 248, 4096], P('dp', 'ctx')
- grad_features: bfloat16 [4, 8, 248, 12288], P('dp', 'ctx')
- grad_taps: float32 [7, 3, 4096], P(None, None, 'ctx')
- grad_residue: float32 [16, 256], P(None, 'ctx')
- grad_skip: float32 [4096], P('ctx')
The draws below stay inside these ranges and needn't reach their ends.
Inputs may be any that keep to these rules, and one draw needn't show every extreme that they name: Along ctx the loader shards come in pairs 2m, 2m + 1 whose counts sum to 256; each replica has a shard holding exactly 248 rows; the counts of a replica sum to 1024.
All inputs are finite; a program needn't handle non-finite values.
Results may differ from the reference program's by a relative error of at most 0.0069.
Values may be sent and summed in bfloat16 or wider, within the bound.
A program may use at most 128 MiB of HBM per device.

```python
import math
import jax
import jax.numpy as jnp
from jax import lax

D = 4096
GROUP = 16
FILTERS = 256
POLES = 16
TAPS = 7
TOK_DEV = 128
CAP = 248
N_DP = 4
N_CTX = 8


def draw_counts(key, part):
    pair_count = N_CTX // 2
    first_key, second_key, third_key = jax.random.split(key, 3)
    reach = TOK_DEV - 8
    offsets_pair = jax.random.randint(first_key, (N_DP, pair_count), -reach, reach + 1)
    chosen = jax.random.randint(second_key, (N_DP, 1), 0, pair_count)
    sign_draw = jax.random.randint(third_key, (N_DP, 1), 0, 2) * 2 - 1
    pair_ids = jnp.arange(pair_count)[None, :]
    offsets_pair = jnp.where(pair_ids == chosen, sign_draw * reach, offsets_pair)
    paired = jnp.stack([TOK_DEV + offsets_pair, TOK_DEV - offsets_pair], axis=-1)
    return paired.reshape(N_DP, N_CTX).astype(jnp.int32)


def level_of(rng, dims, cuts, low, largest):
    level = 1.0
    for position, blocks in cuts:
        heights = jax.random.uniform(jax.random.fold_in(jax.random.fold_in(rng, 6), position), (blocks,), jnp.float32, low / len(cuts), largest / len(cuts))
        level = level * jnp.repeat(jnp.exp(heights), dims[position] // blocks).reshape((-1,) + (1,) * (len(dims) - 1 - position))
    return level


def noise(key, shape, scale, most, shards=(), kind=jnp.bfloat16):
    values = jax.random.normal(key, shape, jnp.float32) * scale
    if len(shards) > 0:
        values = level_of(key, shape, shards, -0.22, 0.18) * values
    return jnp.clip(values, min=-most, max=most).astype(kind)


def setup_inputs(seed: int = 0) -> dict:
    keys = jax.random.split(jax.random.key(seed), 8)
    return {
        "features": noise(keys[0], (N_DP, N_CTX, CAP, 3 * D), 1.0, 6.0, ((0, 4), (1, 8))),
        "counts": draw_counts(jax.random.fold_in(keys[7], 71), 0),
        "short_taps": noise(keys[2], (TAPS, 3, D), TAPS ** -0.5, 2.0, ((2, 8),), jnp.float32),
        "residue": noise(keys[3], (POLES, FILTERS), (2.0 / (POLES * TOK_DEV * N_CTX) ** 0.5), 0.25, ((1, 8),), jnp.float32),
        "decay_rate": jnp.clip(jnp.exp(math.log(0.05) - 7.8477626 * jax.random.uniform(keys[4], (POLES, FILTERS), jnp.float32) ** level_of(keys[4], (POLES, FILTERS), ((1, 8),), -0.2, 0.2)), 1.9531249563442543e-05, 0.05),
        "skip_gain": noise(keys[5], (D,), 1.0, 4.0, ((0, 8),), jnp.float32),
        "cotangent": noise(keys[6], (N_DP, N_CTX, CAP, D), 1.0, 6.0, ((0, 4), (1, 8))),
    }


def causal(filt, signal):
    size = 2 * signal.shape[0]
    spec = jnp.fft.rfft(filt, n=size, axis=0) * jnp.fft.rfft(signal, n=size, axis=0)
    return jnp.fft.irfft(spec, n=size, axis=0)[: signal.shape[0]]


def correlate(later, earlier):
    size = 2 * later.shape[0]
    spec = jnp.fft.rfft(later, n=size, axis=0) * jnp.conj(jnp.fft.rfft(earlier, n=size, axis=0))
    return jnp.fft.irfft(spec, n=size, axis=0)[: later.shape[0]]


def reference(features, counts, short_taps, residue, decay_rate, skip_gain, cotangent):
    window_len = TOK_DEV * N_CTX
    positions = jnp.arange(window_len, dtype=jnp.int32)
    times = jnp.arange(window_len, dtype=jnp.float32)
    basis = jnp.exp(-decay_rate[:, None, :] * times[None, :, None])
    filt = jnp.sum(residue[:, None, :] * basis, axis=0)
    filt_chan = jnp.repeat(filt, GROUP, axis=1)
    slot_rows = jnp.arange(CAP, dtype=jnp.int32)

    def replica(inputs):
        feats_b, counts_b, cot_b = inputs
        shard_ends = jnp.cumsum(counts_b).astype(jnp.int32)
        shard_starts = (shard_ends - counts_b).astype(jnp.int32)
        passed = shard_ends[None, :] <= positions[:, None]
        shard_of = jnp.sum(passed.astype(jnp.int32), axis=1).astype(jnp.int32)
        before = jnp.sum(jnp.where(passed, counts_b[None, :], 0), axis=1).astype(jnp.int32)
        take_index = (shard_of * CAP + positions - before).astype(jnp.int32)
        window = feats_b.reshape(N_CTX * CAP, 3, D)[take_index]
        padded = jnp.pad(window, ((TAPS - 1, 0), (0, 0), (0, 0)))
        short_out = jnp.zeros((window_len, 3, D), jnp.float32)
        for tap_index in range(TAPS):
            piece = padded[TAPS - 1 - tap_index: TAPS - 1 - tap_index + window_len].astype(jnp.float32)
            short_out = short_out + short_taps[tap_index] * piece
        short_b = short_out.astype(jnp.bfloat16)
        query_f = short_b[:, 0].astype(jnp.float32)
        key_f = short_b[:, 1].astype(jnp.float32)
        value_f = short_b[:, 2].astype(jnp.float32)
        mixed = (key_f * value_f).astype(jnp.bfloat16).astype(jnp.float32)
        long_out = causal(filt_chan, mixed) + skip_gain * mixed
        gated = (query_f * long_out).astype(jnp.bfloat16)
        back_index = jnp.clip(shard_starts[:, None] + slot_rows[None, :], 0, window_len - 1).astype(jnp.int32)
        back_valid = slot_rows[None, :] < counts_b[:, None]
        out_rows = jnp.where(back_valid[:, :, None], gated[back_index], jnp.zeros((), jnp.bfloat16))
        grad_f = cot_b.reshape(N_CTX * CAP, D)[take_index].astype(jnp.float32)
        d_query = grad_f * long_out
        d_long = grad_f * query_f
        d_mixed = jnp.flip(causal(filt_chan, jnp.flip(d_long, axis=0)), axis=0) + skip_gain * d_long
        d_short = jnp.stack([d_query, d_mixed * value_f, d_mixed * key_f], axis=1)
        tail = jnp.pad(d_short, ((0, TAPS - 1), (0, 0), (0, 0)))
        d_window = jnp.zeros((window_len, 3, D), jnp.float32)
        tap_grads = []
        for tap_index in range(TAPS):
            d_window = d_window + short_taps[tap_index] * tail[tap_index: tap_index + window_len]
            piece = padded[TAPS - 1 - tap_index: TAPS - 1 - tap_index + window_len].astype(jnp.float32)
            tap_grads.append(jnp.sum(d_short * piece, axis=0))
        d_window = d_window.astype(jnp.bfloat16)
        d_rows = jnp.where(back_valid[:, :, None, None], d_window[back_index], jnp.zeros((), jnp.bfloat16))
        d_rows = d_rows.reshape(N_CTX, CAP, 3 * D)
        lag_grad = correlate(d_long, mixed).reshape(window_len, FILTERS, GROUP).sum(axis=2)
        d_res = jnp.sum(basis * lag_grad[None], axis=1)
        d_skip = jnp.sum(d_long * mixed, axis=0)
        return out_rows, d_rows, jnp.stack(tap_grads, axis=0), d_res, d_skip

    outs = lax.map(replica, (features, counts, cotangent))
    return outs[0], outs[1], jnp.sum(outs[2], axis=0), jnp.sum(outs[3], axis=0), jnp.sum(outs[4], axis=0)
```

```python
import functools

import jax
import jax.numpy as jnp
from jax import lax
from jax.experimental import pallas as pl
from jax.experimental.pallas import tpu as pltpu
from jax.sharding import PartitionSpec as P

TAPS = 7
HALO = 8
REACH = TAPS - 1
ROWS = 256
BLK = 128
POLES = 16
GROUP = 16
LANES = 128
PER = LANES // GROUP
F32 = jnp.float32
BF16 = jnp.bfloat16
SKIP_ROW = 3 * TAPS
RES_ROW = SKIP_ROW + 1
DEC_ROW = SKIP_ROW + 2
CNT_ROW = SKIP_ROW + 3
PARAM_ROWS = 32
GRAD_ROWS = 24
CHUNK = 64
VMEM_LIMIT = 56 << 20
MESH = pl.DeviceIdType.MESH


def iota(shape, axis):
    return lax.broadcasted_iota(jnp.int32, shape, axis)


def same_filter():
    return (iota((LANES, LANES), 0) // POLES) == (iota((LANES, LANES), 1) // GROUP)


def lane_filter(shape):
    return (iota(shape, 1) % LANES) // GROUP


def column_of(row):
    return jnp.transpose(jnp.broadcast_to(row, (LANES, LANES)))


def pick(full):
    fil = lane_filter((POLES, LANES))
    out = full[0:POLES]
    for f in range(1, PER):
        out = jnp.where(fil == f, full[f * POLES : (f + 1) * POLES], out)
    return out


def spread_rows(x):
    fil = lane_filter(x.shape)
    zero = jnp.zeros_like(x)
    return jnp.concatenate([jnp.where(fil == f, x, zero) for f in range(PER)], axis=0)


def side(x):
    return jnp.concatenate([x[0:BLK], x[BLK:ROWS]], axis=1)


def group_lanes(k):
    return pl.ds(pl.multiple_of(k * LANES, LANES), LANES)


def row_mask(shape, low, high):
    row = iota(shape, 0)
    keep = jnp.logical_and(row >= low, row < high)
    return jnp.where(keep, 1.0, 0.0).astype(BF16)


def fill(scratch, rows_bf, left, right, sc, own):
    count = sc[0]
    capacity = rows_bf.shape[0]
    if left is not None:
        scratch[0:HALO, :] = jnp.where(sc[1] > 0, left.astype(F32), 0.0)
    scratch[HALO : HALO + capacity, :] = (rows_bf * own).astype(F32)
    tail_rows = scratch.shape[0] - HALO - capacity
    scratch[HALO + capacity :, :] = jnp.zeros((tail_rows, LANES), F32)
    scratch[pl.ds(HALO + count, HALO), :] = jnp.where(sc[2] > 0, right.astype(F32), 0.0)


def front_kernel(
    groups, sc, fq, fk, fv, cot, tq, tk, tv, hq, hk, hv, hc, param,
    q_out, k_out, v_out, m_out, g_out, d_out, states, skips, win, masks,
):
    count = sc[0]
    capacity = cot.shape[0]

    @pl.when(pl.program_id(0) == 0)
    def _():
        masks[0] = row_mask((ROWS, LANES), 0, count)
        masks[1] = row_mask((ROWS, LANES), 0, count + REACH)
        masks[2] = row_mask((ROWS, LANES), REACH, count + REACH)

    def group(k, carry):
        lanes = group_lanes(k)
        own = masks[0, 0:capacity]
        for m, (rows, left, right) in enumerate(((fq, tq, hq), (fk, tk, hk), (fv, tv, hv))):
            fill(win.at[m], rows[:, lanes], left[:, lanes], right[:, lanes], sc, own)
        fill(win.at[3], cot[:, lanes], None, hc[:, lanes], sc, own)
        for r in range(0, ROWS, CHUNK):
            rows = slice(r, r + CHUNK)
            keep = masks[1, rows]
            shorts = []
            for m in range(3):
                total = param[0, m : m + 1, lanes] * win[m, HALO + r : HALO + r + CHUNK, :]
                for tap in range(1, TAPS):
                    weight = param[0, 3 * tap + m : 3 * tap + m + 1, lanes]
                    at = HALO + r - tap
                    total = total + weight * win[m, at : at + CHUNK, :]
                shorts.append(total.astype(BF16) * keep)
            query, key, value = shorts
            grad = win[3, HALO + r : HALO + r + CHUNK, :].astype(BF16) * keep
            q_out[rows, lanes] = query
            k_out[rows, lanes] = key
            v_out[rows, lanes] = value
            m_out[rows, lanes] = key * value
            g_out[rows, lanes] = grad
            d_out[rows, lanes] = grad * query

        dec = column_of(param[0, DEC_ROW : DEC_ROW + 1, lanes])
        lane_f = iota((LANES, LANES), 1).astype(F32)
        tab_l = jnp.exp(-dec * lane_f).astype(BF16)
        tab_r = jnp.exp(-dec * (BLK - 1.0 - lane_f)).astype(BF16)
        d_long = d_out[:, lanes]
        m_own = m_out[:, lanes] * masks[0]
        fwd = jnp.dot(tab_r, side(m_own), preferred_element_type=F32)
        bwd = jnp.dot(tab_l, side(d_long * masks[2]), preferred_element_type=F32)
        rate = pick(dec)
        first = (count - BLK).astype(F32)
        states[0, :, lanes] = jnp.exp(-rate * first) * pick(fwd[:, 0:LANES]) + jnp.exp(
            -rate * (first - BLK)
        ) * pick(fwd[:, LANES:])
        states[1, :, lanes] = jnp.exp(rate * REACH) * pick(bwd[:, 0:LANES]) + jnp.exp(
            -rate * (BLK - REACH)
        ) * pick(bwd[:, LANES:])
        states[2, :, lanes] = rate
        skips[:, lanes] = jnp.dot(
            jnp.ones((HALO, ROWS), BF16), d_long * m_own, preferred_element_type=F32
        )
        return carry

    lax.fori_loop(0, groups, group, 0)


def local_group(k, m_ref, d_ref, param, masks, yf, yb, res_out, seen_out):
    lanes = group_lanes(k)
    mixed = m_ref[:, lanes]
    d_long = d_ref[:, lanes]
    res_row = param[0, RES_ROW : RES_ROW + 1, lanes]
    dec_row = param[0, DEC_ROW : DEC_ROW + 1, lanes]
    res = column_of(res_row)
    dec = column_of(dec_row)
    lane_f = iota((LANES, LANES), 1).astype(F32)
    sub_f = iota((LANES, LANES), 0).astype(F32)
    tab_l = jnp.exp(-dec * lane_f)
    tab_r = jnp.exp(-dec * (BLK - 1.0 - lane_f))
    k_lag = jnp.sum((res * tab_l).reshape(PER, POLES, LANES), axis=1)
    k_rest = jnp.sum((res * tab_r).reshape(PER, POLES, LANES), axis=1)
    k_turn = pltpu.roll(k_rest, 1, 1)
    lower = iota((BLK, BLK), 0) >= iota((BLK, BLK), 1)
    upper = iota((BLK, BLK), 0) <= iota((BLK, BLK), 1)

    def toeplitz(rows, keep):
        parts = []
        for f in range(PER):
            wide = jnp.broadcast_to(rows[f : f + 1, :], (BLK, LANES))
            wide = pltpu.roll(wide, 0, 1, stride=1, stride_axis=0)
            parts.append(jnp.where(keep, wide, 0.0).astype(BF16))
        return jnp.concatenate(parts, axis=1)

    own_side = side(d_long * masks[...])
    mirror = iota((BLK, BLK), 0) + iota((BLK, BLK), 1)
    flip = jnp.where(mirror == BLK - 1, 1.0, 0.0).astype(BF16)
    own_flip = jnp.dot(flip, own_side, preferred_element_type=F32).astype(BF16)
    m_stack = spread_rows(side(mixed))
    pair = lax.dot_general(
        own_flip, m_stack, (((1,), (1,)), ((), ())), preferred_element_type=F32
    )
    same = same_filter()
    tab_lb = tab_l.astype(BF16)
    s_first = jnp.dot(tab_r.astype(BF16), mixed[0:BLK], preferred_element_type=F32)
    s_first = jnp.where(same, s_first, 0.0)
    e_second = jnp.dot(tab_lb, d_long[BLK:ROWS], preferred_element_type=F32)
    e_second = jnp.where(same, e_second, 0.0).astype(BF16)
    seen = jnp.dot(tab_lb, own_side, preferred_element_type=F32)
    out_t = (res_row * jnp.exp(-dec_row * (sub_f + 1.0))).astype(BF16)
    in_t = (res_row * jnp.exp(-dec_row * (BLK - sub_f))).astype(BF16)
    y_next = jnp.dot(out_t, s_first.astype(BF16), preferred_element_type=F32)
    y_near = jnp.dot(in_t, e_second, preferred_element_type=F32)
    y_fwd = jnp.dot(toeplitz(k_turn, lower), m_stack, preferred_element_type=F32)
    yf[0:BLK, lanes] = y_fwd[:, 0:LANES]
    yf[BLK:ROWS, lanes] = y_fwd[:, LANES:] + y_next
    d_stack = spread_rows(side(d_long))
    y_bwd = jnp.dot(toeplitz(k_lag, upper), d_stack, preferred_element_type=F32)
    yb[0:BLK, lanes] = y_bwd[:, 0:LANES] + y_near
    yb[BLK:ROWS, lanes] = y_bwd[:, LANES:]

    lag_rows = []
    for f in range(PER):
        piece = jnp.where(mirror < BLK, pair[:, f * LANES : (f + 1) * LANES], 0.0)
        piece = pltpu.roll(piece, 0, 1, stride=1, stride_axis=0)
        lag_rows.append(jnp.broadcast_to(jnp.sum(piece, axis=0, keepdims=True), (POLES, LANES)))
    lag_sums = jnp.concatenate(lag_rows, axis=0)
    res_grad = lag_sums * tab_r + jnp.exp(-dec) * seen[:, LANES:] * s_first
    row = jnp.sum(jnp.transpose(res_grad), axis=0, keepdims=True)
    res_out[:, lanes] = jnp.broadcast_to(row, (HALO, LANES))
    rate = pick(dec)
    seen_out[:, lanes] = jnp.exp(-rate) * pick(seen[:, 0:LANES]) + jnp.exp(
        -rate * (BLK + 1.0)
    ) * pick(seen[:, LANES:])


def local_kernel(
    groups, shards, rounds, sc, decays, m_ref, d_ref, param, states,
    yf, yb, res_out, seen_out, carries, masks, total, outbox, inbox, send, recv,
):
    step = pl.program_id(0)
    dp, me = lax.axis_index("dp"), lax.axis_index("ctx")
    pieces = total.shape[2] // (LANES * 4)

    def peer(gap):
        return (dp, lax.rem(me + gap + shards, shards))

    def copy(j, way):
        gap = (1 << j) if way == 0 else -(1 << j)
        return pltpu.make_async_remote_copy(
            src_ref=outbox.at[j, way], dst_ref=inbox.at[j, way], send_sem=send.at[j, way],
            recv_sem=recv.at[j, way], device_id=peer(gap), device_id_type=MESH,
        )

    def sends(j, way):
        return me + (1 << j) < shards if way == 0 else me >= (1 << j)

    def start(j):
        for way in range(2):
            @pl.when(sends(j, way))
            def _(way=way):
                outbox[j, way] = total[way].astype(BF16)
                copy(j, way).start()

    def finish(j):
        for way in range(2):
            @pl.when(sends(j, 1 - way))
            def _(way=way):
                copy(j, way).wait_recv()

                def piece(p, c):
                    lanes = pl.ds(pl.multiple_of(p * LANES * 4, LANES), LANES * 4)
                    rate = states[2, :, lanes]
                    there = inbox[j, way, :, lanes].astype(F32)
                    near = jnp.exp(-rate * decays[4 * j + 2 + way]) * there
                    carries[way, :, lanes] = carries[way, :, lanes] + near
                    if j < rounds - 1:
                        far = jnp.exp(-rate * decays[4 * j + way]) * there
                        total[way, :, lanes] = total[way, :, lanes] + far
                    return c

                lax.fori_loop(0, pieces, piece, 0)

            @pl.when(sends(j, way))
            def _(way=way):
                copy(j, way).wait_send()

    @pl.when(step == 0)
    def _():
        barrier = pltpu.get_barrier_semaphore()
        greeted = 0
        for j in range(rounds):
            for way in range(2):
                there = sends(j, way)
                greeted = greeted + there.astype(jnp.int32)

                @pl.when(there)
                def _(j=j, way=way):
                    gap = (1 << j) if way == 0 else -(1 << j)
                    pl.semaphore_signal(
                        barrier, inc=1, device_id=peer(gap), device_id_type=MESH
                    )
        pl.semaphore_wait(barrier, greeted)
        masks[...] = row_mask((ROWS, LANES), 0, sc[0])
        carries[...] = jnp.zeros_like(carries)
        total[...] = states[0:2]
        start(0)

    for j in range(1, rounds):
        @pl.when(step == (j * shards) // rounds)
        def _(j=j):
            finish(j - 1)
            start(j)

    def group(k, carry):
        local_group(k, m_ref, d_ref, param, masks, yf, yb, res_out, seen_out)
        return carry

    lax.fori_loop(0, groups, group, 0)

    @pl.when(step == shards - 1)
    def _():
        finish(rounds - 1)


def final_kernel(
    groups, shards, sc, fq, fk, fv, q_ref, k_ref, v_ref, m_ref, g_ref, yf, yb, param,
    carries, rates, seen, res_in, skips, out, dfeat, dparam,
    own, dshort, prods, dwin, sems,
):
    count = sc[0]
    step = pl.program_id(0)
    capacity = fq.shape[0]
    chan = fq.shape[1]
    slot = lax.rem(step, 2)

    def writes(at, place):
        made = []
        for m in range(3):
            lanes = pl.ds(pl.multiple_of((m * shards + at) * chan, LANES), chan)
            made.append(
                pltpu.make_async_copy(dwin.at[place, m], dfeat.at[:, lanes], sems.at[place, m])
            )
        return made

    @pl.when(step == 0)
    def _():
        own[...] = row_mask((ROWS, LANES), 0, count)
        dshort[:, ROWS:, :] = jnp.zeros((3, dshort.shape[1] - ROWS, LANES), F32)
        prods[...] = jnp.zeros_like(prods)

    @pl.when(step >= 2)
    def _():
        for copy in writes(step - 2, slot):
            copy.wait()

    dparam[GRAD_ROWS - 1 : GRAD_ROWS, :] = jnp.zeros((1, chan), F32)

    def group(k, carry):
        lanes = group_lanes(k)
        res_row = param[0, RES_ROW : RES_ROW + 1, lanes]
        dec_row = param[0, DEC_ROW : DEC_ROW + 1, lanes]
        skip = param[0, SKIP_ROW : SKIP_ROW + 1, lanes]
        sub_f = iota((LANES, LANES), 0).astype(F32)
        out_t = (res_row * jnp.exp(-dec_row * (sub_f + 1.0))).astype(BF16)
        in_t = (res_row * jnp.exp(-dec_row * (BLK - 1.0 - sub_f))).astype(BF16)
        rate = rates[0, :, lanes]
        from_left = carries[0, :, lanes]
        from_right = carries[1, :, lanes]

        def pair(a, b):
            both = jnp.concatenate([a.astype(BF16), b.astype(BF16)], axis=1)
            return spread_rows(both)

        until = (count + (REACH + 1 - BLK)).astype(F32)
        y_left = jnp.dot(
            out_t, pair(from_left, from_left * jnp.exp(-rate * float(BLK))),
            preferred_element_type=F32,
        )
        y_right = jnp.dot(
            in_t,
            pair(from_right * jnp.exp(-rate * until), from_right * jnp.exp(-rate * (until - BLK))),
            preferred_element_type=F32,
        )
        for r in range(0, ROWS, CHUNK):
            rows = slice(r, r + CHUNK)
            at = slice(r % BLK, r % BLK + CHUNK)
            cols = slice((r // BLK) * LANES, (r // BLK + 1) * LANES)
            kept = min(r + CHUNK, capacity) - r
            query = q_ref[rows, lanes].astype(F32)
            grad = g_ref[rows, lanes].astype(F32)
            mixed = m_ref[rows, lanes].astype(F32)
            long_out = yf[rows, lanes] + y_left[at, cols] + skip * mixed
            gated = (query * long_out).astype(BF16) * own[rows]
            out[r : r + kept, lanes] = gated[0:kept]
            dshort[0, rows, :] = grad * long_out
            d_mixed = yb[rows, lanes] + y_right[at, cols] + skip * (grad * query)
            dshort[1, rows, :] = d_mixed * v_ref[rows, lanes].astype(F32)
            dshort[2, rows, :] = d_mixed * k_ref[rows, lanes].astype(F32)

        for m, feat in enumerate((fq, fk, fv)):
            for r in range(0, ROWS, CHUNK):
                kept = min(r + CHUNK, capacity) - r
                rows = slice(r, r + kept)
                keep = own[rows]
                window = feat[rows, lanes] * keep
                total = None
                for tap in range(TAPS):
                    weight = param[0, 3 * tap + m : 3 * tap + m + 1, lanes]
                    shifted = dshort[m, r + tap : r + tap + kept, :]
                    term = weight * shifted
                    total = term if total is None else total + term
                    prods[rows, tap * LANES : (tap + 1) * LANES] = shifted.astype(BF16) * window
                dwin[slot, m, rows, lanes] = total.astype(BF16) * keep
            sums = jnp.dot(jnp.ones((HALO, ROWS), BF16), prods[...], preferred_element_type=F32)
            for tap in range(TAPS):
                dparam[3 * tap + m : 3 * tap + m + 1, lanes] = sums[
                    0:1, tap * LANES : (tap + 1) * LANES
                ]

        crossed = seen[:, lanes] * from_left
        high = crossed.astype(BF16)
        low = (crossed - high.astype(F32)).astype(BF16)
        gather = (iota((LANES, LANES), 0) // GROUP) == (iota((LANES, LANES), 1) // GROUP)
        gather = jnp.where(gather, 1.0, 0.0).astype(BF16)
        sums = jnp.dot(high, gather, preferred_element_type=F32)
        sums = sums + jnp.dot(low, gather, preferred_element_type=F32)
        mine = iota((POLES, LANES), 0) == iota((POLES, LANES), 1) % POLES
        row = jnp.sum(jnp.where(mine, sums, 0.0), axis=0, keepdims=True)
        dparam[RES_ROW : RES_ROW + 1, lanes] = res_in[0:1, lanes] + row
        dparam[SKIP_ROW : SKIP_ROW + 1, lanes] = skips[0:1, lanes]
        return carry

    lax.fori_loop(0, groups, group, 0)
    for copy in writes(step, slot):
        copy.start()

    @pl.when(step == shards - 1)
    def _():
        for copy in writes(step - 1, 1 - slot) + writes(step, slot):
            copy.wait()


def meet(peers):
    barrier = pltpu.get_barrier_semaphore()
    for peer in peers:
        pl.semaphore_signal(barrier, inc=1, device_id=peer, device_id_type=MESH)
    pl.semaphore_wait(barrier, len(peers))


def params_kernel(shards, packed, tail, head, params, tail_in, head_in, send, recv, own):
    dp, me = lax.axis_index("dp"), lax.axis_index("ctx")
    peers = [(dp, lax.rem(me + d, shards)) for d in range(1, shards)]
    meet(peers)
    local = pltpu.make_async_copy(packed, params.at[me], own)
    local.start()
    jobs = [(tail, tail_in, peers[0]), (head, head_in, peers[-1])]
    jobs += [(packed, params.at[me], peer) for peer in peers]
    copies = []
    for n, (src, dst, peer) in enumerate(jobs):
        copies.append(
            pltpu.make_async_remote_copy(
                src_ref=src, dst_ref=dst, send_sem=send.at[n], recv_sem=recv.at[n],
                device_id=peer, device_id_type=MESH,
            )
        )
        copies[-1].start()
    local.wait()
    for copy in copies:
        copy.wait()


def reduce_kernel(shards, replicas, part, out, by_ctx, by_dp, send, recv, send_dp, recv_dp):
    dp, me = lax.axis_index("dp"), lax.axis_index("ctx")
    chan = out.shape[1]
    peers = [(dp, lax.rem(me + d, shards)) for d in range(1, shards)]
    others = [(lax.rem(dp + d, replicas), me) for d in range(1, replicas)]
    meet(peers + others)
    copies = []
    for n, peer in enumerate(peers):
        lanes = pl.ds(pl.multiple_of(peer[1] * chan, LANES), chan)
        copies.append(
            pltpu.make_async_remote_copy(
                src_ref=part.at[:, lanes], dst_ref=by_ctx.at[n], send_sem=send.at[n],
                recv_sem=recv.at[n], device_id=peer, device_id_type=MESH,
            )
        )
        copies[-1].start()
    total = part[:, pl.ds(pl.multiple_of(me * chan, LANES), chan)]
    for n, copy in enumerate(copies):
        copy.wait()
        total = total + by_ctx[n]
    by_dp[dp] = total
    copies = []
    for n, peer in enumerate(others):
        copies.append(
            pltpu.make_async_remote_copy(
                src_ref=by_dp.at[dp], dst_ref=by_dp.at[dp], send_sem=send_dp.at[n],
                recv_sem=recv_dp.at[n], device_id=peer, device_id_type=MESH,
            )
        )
        copies[-1].start()
    for copy in copies:
        copy.wait()
    total = by_dp[0]
    for n in range(1, replicas):
        total = total + by_dp[n]
    out[...] = total


def remote(ident):
    return pltpu.CompilerParams(
        collective_id=ident, has_side_effects=True, vmem_limit_bytes=VMEM_LIMIT
    )


def per_device(features, counts, short_taps, residue, decay_rate, skip_gain, cotangent):
    shards = lax.axis_size("ctx")
    me = lax.axis_index("ctx")
    capacity = features.shape[2]
    width = cotangent.shape[3]
    chan = short_taps.shape[2]
    groups = chan // LANES
    feats = features[0, 0]
    cot = cotangent[0, 0]
    count = counts[0, 0]

    packed = jnp.concatenate(
        [
            short_taps.reshape(3 * TAPS, chan),
            skip_gain.reshape(1, chan),
            residue.T.reshape(1, chan),
            decay_rate.T.reshape(1, chan),
            jnp.broadcast_to(count.astype(F32), (PARAM_ROWS - CNT_ROW, chan)),
        ],
        axis=0,
    )
    tail = lax.dynamic_slice(feats, (count - HALO, 0), (HALO, 3 * width))
    head = jnp.concatenate([feats[0:HALO], cot[0:HALO]], axis=1)
    anywhere = pl.BlockSpec(memory_space=pl.ANY)
    params, tail, head = pl.pallas_call(
        functools.partial(params_kernel, shards),
        in_specs=[anywhere] * 3,
        out_specs=[anywhere] * 3,
        out_shape=[
            jax.ShapeDtypeStruct((shards,) + packed.shape, F32),
            jax.ShapeDtypeStruct(tail.shape, BF16),
            jax.ShapeDtypeStruct(head.shape, BF16),
        ],
        scratch_shapes=[
            pltpu.SemaphoreType.DMA((shards + 1,)),
            pltpu.SemaphoreType.DMA((shards + 1,)),
            pltpu.SemaphoreType.DMA,
        ],
        compiler_params=remote(0),
        name="params",
    )(packed, tail, head)

    all_counts = params[:, CNT_ROW, 0]
    ids = jnp.arange(shards, dtype=jnp.int32)
    rounds = (shards - 1).bit_length()
    spans = []
    for j in range(rounds):
        gap = 1 << j
        left, right = ids > me - gap, ids < me + gap
        spans += [left & (ids <= me), right & (ids >= me), left & (ids < me), right & (ids > me)]
    decays = jnp.sum(jnp.where(jnp.stack(spans), all_counts[None, :], 0.0), axis=1)
    edges = jnp.stack([me > 0, me < shards - 1]).astype(jnp.int32)
    scalars = jnp.concatenate([count[None], edges]).astype(jnp.int32)

    def cols(rows, offset):
        return pl.BlockSpec((rows, chan), lambda g, *_: (0, offset * shards + g))

    def planes(lead, rows, first=0):
        return pl.BlockSpec((lead, rows, chan), lambda g, *_: (first, 0, g))

    def shape(*dims, dtype=F32):
        return jax.ShapeDtypeStruct(dims, dtype)

    plain = pltpu.CompilerParams(vmem_limit_bytes=VMEM_LIMIT)
    smem = pl.BlockSpec(memory_space=pltpu.SMEM)
    param_spec = pl.BlockSpec((1, PARAM_ROWS, chan), lambda g, *_: (g, 0, 0))
    feat_specs = [cols(capacity, m) for m in range(3)]
    rows_spec = cols(ROWS, 0)
    rows_shape = shape(ROWS, width, dtype=BF16)
    query, key, value, mixed, grad, d_long, states, skips = pl.pallas_call(
        functools.partial(front_kernel, groups),
        grid=(shards,),
        in_specs=[smem] + feat_specs + [cols(capacity, 0)]
        + [cols(HALO, m) for m in range(3)] + [cols(HALO, m) for m in range(4)] + [param_spec],
        out_specs=[rows_spec] * 6 + [planes(3, POLES), cols(HALO, 0)],
        out_shape=[rows_shape] * 6 + [shape(3, POLES, width), shape(HALO, width)],
        scratch_shapes=[
            pltpu.VMEM((4, HALO + ROWS + HALO, LANES), F32),
            pltpu.VMEM((3, ROWS, LANES), BF16),
        ],
        compiler_params=plain,
        name="front",
    )(scalars, feats, feats, feats, cot, tail, tail, tail, head, head, head, head, params)

    whole = pl.BlockSpec((3, POLES, width), lambda g: (0, 0, 0))
    y_fwd, y_bwd, res_local, seen, carries = pl.pallas_call(
        functools.partial(local_kernel, groups, shards, rounds),
        grid=(shards,),
        in_specs=[smem, smem, rows_spec, rows_spec, param_spec, whole],
        out_specs=[rows_spec, rows_spec, cols(HALO, 0), cols(POLES, 0),
                   pl.BlockSpec((2, POLES, width), lambda g: (0, 0, 0))],
        out_shape=[shape(ROWS, width), shape(ROWS, width), shape(HALO, width),
                   shape(POLES, width), shape(2, POLES, width)],
        scratch_shapes=[
            pltpu.VMEM((ROWS, LANES), BF16),
            pltpu.VMEM((2, POLES, width), F32),
            pltpu.VMEM((rounds, 2, POLES, width), BF16),
            pltpu.VMEM((rounds, 2, POLES, width), BF16),
            pltpu.SemaphoreType.DMA((rounds, 2)),
            pltpu.SemaphoreType.DMA((rounds, 2)),
        ],
        compiler_params=remote(1),
        name="local",
    )(scalars, decays, mixed, d_long, params, states)

    out, dfeat, dparam = pl.pallas_call(
        functools.partial(final_kernel, groups, shards),
        grid=(shards,),
        in_specs=[smem] + feat_specs + [rows_spec] * 7
        + [param_spec, planes(2, POLES), planes(1, POLES, 2), cols(POLES, 0),
           cols(HALO, 0), cols(HALO, 0)],
        out_specs=[cols(capacity, 0), anywhere, cols(GRAD_ROWS, 0)],
        out_shape=[
            shape(capacity, width, dtype=BF16),
            shape(capacity, 3 * width, dtype=BF16),
            shape(GRAD_ROWS, width),
        ],
        scratch_shapes=[
            pltpu.VMEM((ROWS, LANES), BF16),
            pltpu.VMEM((3, ROWS + HALO, LANES), F32),
            pltpu.VMEM((ROWS, TAPS * LANES), BF16),
            pltpu.VMEM((2, 3, capacity, chan), BF16),
            pltpu.SemaphoreType.DMA((2, 3)),
        ],
        compiler_params=plain,
        name="final",
    )(scalars, feats, feats, feats, query, key, value, mixed, grad, y_fwd, y_bwd, params,
      carries, states, seen, res_local, skips)
    replicas = lax.axis_size("dp")
    vmem = pl.BlockSpec(memory_space=pltpu.VMEM)
    grads = pl.pallas_call(
        functools.partial(reduce_kernel, shards, replicas),
        in_specs=[vmem],
        out_specs=vmem,
        out_shape=jax.ShapeDtypeStruct((GRAD_ROWS, chan), F32),
        scratch_shapes=[
            pltpu.VMEM((shards - 1, GRAD_ROWS, chan), F32),
            pltpu.VMEM((replicas, GRAD_ROWS, chan), F32),
            pltpu.SemaphoreType.DMA((shards - 1,)),
            pltpu.SemaphoreType.DMA((shards - 1,)),
            pltpu.SemaphoreType.DMA((replicas - 1,)),
            pltpu.SemaphoreType.DMA((replicas - 1,)),
        ],
        compiler_params=remote(2),
        name="reduce",
    )(dparam)
    return (
        out[None, None],
        dfeat[None, None],
        grads[0 : 3 * TAPS].reshape(TAPS, 3, chan),
        grads[RES_ROW].reshape(chan // GROUP, POLES).T,
        grads[SKIP_ROW],
    )


def solution(mesh):
    in_specs = (
        P("dp", "ctx", None, None),
        P("dp", "ctx"),
        P(None, None, "ctx"),
        P(None, "ctx"),
        P(None, "ctx"),
        P("ctx"),
        P("dp", "ctx", None, None),
    )
    out_specs = (
        P("dp", "ctx", None, None),
        P("dp", "ctx", None, None),
        P(None, None, "ctx"),
        P(None, "ctx"),
        P("ctx"),
    )
    return jax.shard_map(
        per_device, mesh=mesh, in_specs=in_specs, out_specs=out_specs, check_vma=False
    )
```

```python
import functools

import jax
import jax.numpy as jnp
from jax import lax
from jax.experimental import pallas as pl
from jax.experimental.pallas import tpu as pltpu
from jax.sharding import PartitionSpec as P

TAPS = 7
HALO = 8
REACH = TAPS - 1
ROWS = 256
BLK = 128
POLES = 16
GROUP = 16
LANES = 128
PER = LANES // GROUP
F32 = jnp.float32
BF16 = jnp.bfloat16
SKIP_ROW = 3 * TAPS
RES_ROW = SKIP_ROW + 1
DEC_ROW = SKIP_ROW + 2
LOW_ROW = SKIP_ROW + 3
CNT_ROW = LOW_ROW + SKIP_ROW
PARAM_ROWS = 2 * LOW_ROW
GRAD_ROWS = 24
CHUNK = 64
VMEM_LIMIT = 56 << 20
MESH = pl.DeviceIdType.MESH


def iota(shape, axis):
    return lax.broadcasted_iota(jnp.int32, shape, axis)


def same_filter():
    return (iota((LANES, LANES), 0) // POLES) == (iota((LANES, LANES), 1) // GROUP)


def lane_filter(shape):
    return (iota(shape, 1) % LANES) // GROUP


def column_of(row):
    return jnp.transpose(jnp.broadcast_to(row, (LANES, LANES)))


def pick(full):
    fil = lane_filter((POLES, LANES))
    out = full[0:POLES]
    for f in range(1, PER):
        out = jnp.where(fil == f, full[f * POLES : (f + 1) * POLES], out)
    return out


def spread_rows(x):
    fil = lane_filter(x.shape)
    zero = jnp.zeros_like(x)
    return jnp.concatenate([jnp.where(fil == f, x, zero) for f in range(PER)], axis=0)


def side(x):
    return jnp.concatenate([x[0:BLK], x[BLK:ROWS]], axis=1)


def unpack(sent, param):
    both = sent[0].astype(F32)
    low = both[LOW_ROW:]
    low = jnp.where(iota(low.shape, 0) == SKIP_ROW, 0.0, low)
    param[...] = both[0:LOW_ROW] + low


def group_lanes(k):
    return pl.ds(pl.multiple_of(k * LANES, LANES), LANES)


def row_mask(shape, low, high):
    row = iota(shape, 0)
    keep = jnp.logical_and(row >= low, row < high)
    return jnp.where(keep, 1.0, 0.0).astype(BF16)


def fill(scratch, rows_bf, left, right, edges, count, own):
    capacity = rows_bf.shape[0]
    if left is not None:
        scratch[0:HALO, :] = jnp.where(edges[0], left.astype(F32), 0.0)
    scratch[HALO : HALO + capacity, :] = (rows_bf * own).astype(F32)
    tail_rows = scratch.shape[0] - HALO - capacity
    scratch[HALO + capacity :, :] = jnp.zeros((tail_rows, LANES), F32)
    scratch[pl.ds(HALO + count, HALO), :] = jnp.where(edges[1], right.astype(F32), 0.0)


def front_kernel(
    groups, shards, counts, place, fq, fk, fv, cot, tq, tk, tv, hq, hk, hv, hc, sent,
    q_out, k_out, v_out, m_out, g_out, d_out, states, skips, win, masks, param,
):
    count = counts[0, 0]
    capacity = cot.shape[0]
    edges = (place[0] > 0, place[0] < shards - 1)

    @pl.when(pl.program_id(0) == 0)
    def _():
        masks[0] = row_mask((ROWS, LANES), 0, count)
        masks[1] = row_mask((ROWS, LANES), 0, count + REACH)
        masks[2] = row_mask((ROWS, LANES), REACH, count + REACH)

    unpack(sent, param)

    def group(k, carry):
        lanes = group_lanes(k)
        own = masks[0, 0:capacity]
        for m, (rows, left, right) in enumerate(((fq, tq, hq), (fk, tk, hk), (fv, tv, hv))):
            fill(win.at[m], rows[:, lanes], left[:, lanes], right[:, lanes], edges, count, own)
        fill(win.at[3], cot[:, lanes], None, hc[:, lanes], edges, count, own)
        for r in range(0, ROWS, CHUNK):
            rows = slice(r, r + CHUNK)
            keep = masks[1, rows]
            shorts = []
            for m in range(3):
                total = param[TAPS * m : TAPS * m + 1, lanes] * win[m, HALO + r : HALO + r + CHUNK, :]
                for tap in range(1, TAPS):
                    weight = param[TAPS * m + tap : TAPS * m + tap + 1, lanes]
                    at = HALO + r - tap
                    total = total + weight * win[m, at : at + CHUNK, :]
                shorts.append(total.astype(BF16) * keep)
            query, key, value = shorts
            grad = win[3, HALO + r : HALO + r + CHUNK, :].astype(BF16) * keep
            q_out[rows, lanes] = query
            k_out[rows, lanes] = key
            v_out[rows, lanes] = value
            m_out[rows, lanes] = key * value
            g_out[rows, lanes] = grad
            d_out[rows, lanes] = grad * query

        dec = column_of(param[DEC_ROW : DEC_ROW + 1, lanes])
        lane_f = iota((LANES, LANES), 1).astype(F32)
        tab_l = jnp.exp(-dec * lane_f).astype(BF16)
        tab_r = jnp.exp(-dec * (BLK - 1.0 - lane_f)).astype(BF16)
        d_long = d_out[:, lanes]
        m_own = m_out[:, lanes] * masks[0]
        fwd = jnp.dot(tab_r, side(m_own), preferred_element_type=F32)
        bwd = jnp.dot(tab_l, side(d_long * masks[2]), preferred_element_type=F32)
        rate = pick(dec)
        first = (count - BLK).astype(F32)
        states[0, :, lanes] = jnp.exp(-rate * first) * pick(fwd[:, 0:LANES]) + jnp.exp(
            -rate * (first - BLK)
        ) * pick(fwd[:, LANES:])
        states[1, :, lanes] = jnp.exp(rate * REACH) * pick(bwd[:, 0:LANES]) + jnp.exp(
            -rate * (BLK - REACH)
        ) * pick(bwd[:, LANES:])
        states[2, :, lanes] = rate
        skips[:, lanes] = jnp.dot(
            jnp.ones((HALO, ROWS), BF16), d_long * m_own, preferred_element_type=F32
        )
        return carry

    lax.fori_loop(0, groups, group, 0)


def local_group(k, m_ref, d_ref, param, masks, yf, yb, res_out, seen_out):
    lanes = group_lanes(k)
    mixed = m_ref[:, lanes]
    d_long = d_ref[:, lanes]
    res_row = param[RES_ROW : RES_ROW + 1, lanes]
    dec_row = param[DEC_ROW : DEC_ROW + 1, lanes]
    res = column_of(res_row)
    dec = column_of(dec_row)
    lane_f = iota((LANES, LANES), 1).astype(F32)
    sub_f = iota((LANES, LANES), 0).astype(F32)
    tab_l = jnp.exp(-dec * lane_f)
    tab_r = jnp.exp(-dec * (BLK - 1.0 - lane_f))
    k_lag = jnp.sum((res * tab_l).reshape(PER, POLES, LANES), axis=1)
    k_rest = jnp.sum((res * tab_r).reshape(PER, POLES, LANES), axis=1)
    k_turn = pltpu.roll(k_rest, 1, 1)
    lower = iota((BLK, BLK), 0) >= iota((BLK, BLK), 1)
    upper = iota((BLK, BLK), 0) <= iota((BLK, BLK), 1)

    def toeplitz(rows, keep):
        parts = []
        for f in range(PER):
            wide = jnp.broadcast_to(rows[f : f + 1, :], (BLK, LANES))
            wide = pltpu.roll(wide, 0, 1, stride=1, stride_axis=0)
            parts.append(jnp.where(keep, wide, 0.0).astype(BF16))
        return jnp.concatenate(parts, axis=1)

    own_side = side(d_long * masks[...])
    mirror = iota((BLK, BLK), 0) + iota((BLK, BLK), 1)
    flip = jnp.where(mirror == BLK - 1, 1.0, 0.0).astype(BF16)
    own_flip = jnp.dot(flip, own_side, preferred_element_type=F32).astype(BF16)
    m_stack = spread_rows(side(mixed))
    pair = lax.dot_general(
        own_flip, m_stack, (((1,), (1,)), ((), ())), preferred_element_type=F32
    )
    same = same_filter()
    tab_lb = tab_l.astype(BF16)
    s_first = jnp.dot(tab_r.astype(BF16), mixed[0:BLK], preferred_element_type=F32)
    s_first = jnp.where(same, s_first, 0.0)
    e_second = jnp.dot(tab_lb, d_long[BLK:ROWS], preferred_element_type=F32)
    e_second = jnp.where(same, e_second, 0.0).astype(BF16)
    seen = jnp.dot(tab_lb, own_side, preferred_element_type=F32)
    out_t = (res_row * jnp.exp(-dec_row * (sub_f + 1.0))).astype(BF16)
    in_t = (res_row * jnp.exp(-dec_row * (BLK - sub_f))).astype(BF16)
    y_next = jnp.dot(out_t, s_first.astype(BF16), preferred_element_type=F32)
    y_near = jnp.dot(in_t, e_second, preferred_element_type=F32)
    y_fwd = jnp.dot(toeplitz(k_turn, lower), m_stack, preferred_element_type=F32)
    yf[0:BLK, lanes] = y_fwd[:, 0:LANES]
    yf[BLK:ROWS, lanes] = y_fwd[:, LANES:] + y_next
    d_stack = spread_rows(side(d_long))
    y_bwd = jnp.dot(toeplitz(k_lag, upper), d_stack, preferred_element_type=F32)
    yb[0:BLK, lanes] = y_bwd[:, 0:LANES] + y_near
    yb[BLK:ROWS, lanes] = y_bwd[:, LANES:]

    lag_rows = []
    for f in range(PER):
        piece = jnp.where(mirror < BLK, pair[:, f * LANES : (f + 1) * LANES], 0.0)
        piece = pltpu.roll(piece, 0, 1, stride=1, stride_axis=0)
        lag_rows.append(jnp.broadcast_to(jnp.sum(piece, axis=0, keepdims=True), (POLES, LANES)))
    lag_sums = jnp.concatenate(lag_rows, axis=0)
    res_grad = lag_sums * tab_r + jnp.exp(-dec) * seen[:, LANES:] * s_first
    row = jnp.sum(jnp.transpose(res_grad), axis=0, keepdims=True)
    res_out[:, lanes] = jnp.broadcast_to(row, (HALO, LANES))
    rate = pick(dec)
    seen_out[:, lanes] = jnp.exp(-rate) * pick(seen[:, 0:LANES]) + jnp.exp(
        -rate * (BLK + 1.0)
    ) * pick(seen[:, LANES:])


def local_kernel(
    groups, shards, rounds, counts, every, m_ref, d_ref, sent, states,
    yf, yb, res_out, seen_out, carries, masks, param, total, outbox, inbox, send, recv,
):
    step = pl.program_id(0)
    dp, me = lax.axis_index("dp"), lax.axis_index("ctx")
    pieces = total.shape[2] // (LANES * 4)

    def peer(gap):
        return (dp, lax.rem(me + gap + shards, shards))

    def copy(j, way):
        gap = (1 << j) if way == 0 else -(1 << j)
        return pltpu.make_async_remote_copy(
            src_ref=outbox.at[j, way], dst_ref=inbox.at[j, way], send_sem=send.at[j, way],
            recv_sem=recv.at[j, way], device_id=peer(gap), device_id_type=MESH,
        )

    def sends(j, way):
        return me + (1 << j) < shards if way == 0 else me >= (1 << j)

    def start(j):
        for way in range(2):
            @pl.when(sends(j, way))
            def _(way=way):
                outbox[j, way] = total[way].astype(BF16)
                copy(j, way).start()

    def finish(j):
        for way in range(2):
            @pl.when(sends(j, 1 - way))
            def _(way=way):
                copy(j, way).wait_recv()

                gap = 1 << j
                low, high = (me - gap, me) if way == 0 else (me, me + gap)
                inner = 0.0
                for i in range(shards):
                    inside = (i > low) & (i < high)
                    inner = inner + jnp.where(inside, every[i], 0.0)
                outer = inner + counts[0, 0].astype(F32)

                def piece(p, c):
                    lanes = pl.ds(pl.multiple_of(p * LANES * 4, LANES), LANES * 4)
                    rate = states[2, :, lanes]
                    there = inbox[j, way, :, lanes].astype(F32)
                    near = jnp.exp(-rate * inner) * there
                    carries[way, :, lanes] = carries[way, :, lanes] + near
                    if j < rounds - 1:
                        far = jnp.exp(-rate * outer) * there
                        total[way, :, lanes] = total[way, :, lanes] + far
                    return c

                lax.fori_loop(0, pieces, piece, 0)

            @pl.when(sends(j, way))
            def _(way=way):
                copy(j, way).wait_send()

    @pl.when(step == 0)
    def _():
        barrier = pltpu.get_barrier_semaphore()
        greeted = 0
        for j in range(rounds):
            for way in range(2):
                there = sends(j, way)
                greeted = greeted + there.astype(jnp.int32)

                @pl.when(there)
                def _(j=j, way=way):
                    gap = (1 << j) if way == 0 else -(1 << j)
                    pl.semaphore_signal(
                        barrier, inc=1, device_id=peer(gap), device_id_type=MESH
                    )
        pl.semaphore_wait(barrier, greeted)
        masks[...] = row_mask((ROWS, LANES), 0, counts[0, 0])
        carries[...] = jnp.zeros_like(carries)
        total[...] = states[0:2]
        start(0)

    for j in range(1, rounds):
        @pl.when(step == (j * shards) // rounds)
        def _(j=j):
            finish(j - 1)
            start(j)

    unpack(sent, param)

    def group(k, carry):
        local_group(k, m_ref, d_ref, param, masks, yf, yb, res_out, seen_out)
        return carry

    lax.fori_loop(0, groups, group, 0)

    @pl.when(step == shards - 1)
    def _():
        finish(rounds - 1)


def final_kernel(
    groups, shards, counts, fq, fk, fv, q_ref, k_ref, v_ref, m_ref, g_ref, yf, yb, sent,
    carries, rates, seen, res_in, skips, out, dfeat, dparam,
    own, param, dshort, prods, dwin, sems,
):
    count = counts[0, 0]
    step = pl.program_id(0)
    capacity = fq.shape[0]
    chan = fq.shape[1]
    slot = lax.rem(step, 2)

    def writes(at, place):
        made = []
        for m in range(3):
            lanes = pl.ds(pl.multiple_of((m * shards + at) * chan, LANES), chan)
            made.append(
                pltpu.make_async_copy(dwin.at[place, m], dfeat.at[:, lanes], sems.at[place, m])
            )
        return made

    @pl.when(step == 0)
    def _():
        own[...] = row_mask((ROWS, LANES), 0, count)
        dshort[:, ROWS:, :] = jnp.zeros((3, dshort.shape[1] - ROWS, LANES), F32)
        prods[...] = jnp.zeros_like(prods)

    @pl.when(step >= 2)
    def _():
        for copy in writes(step - 2, slot):
            copy.wait()

    dparam[GRAD_ROWS - 1 : GRAD_ROWS, :] = jnp.zeros((1, chan), F32)
    unpack(sent, param)

    def group(k):
        lanes = slice(k * LANES, (k + 1) * LANES)
        res_row = param[RES_ROW : RES_ROW + 1, lanes]
        dec_row = param[DEC_ROW : DEC_ROW + 1, lanes]
        skip = param[SKIP_ROW : SKIP_ROW + 1, lanes]
        sub_f = iota((LANES, LANES), 0).astype(F32)
        out_t = (res_row * jnp.exp(-dec_row * (sub_f + 1.0))).astype(BF16)
        in_t = (res_row * jnp.exp(-dec_row * (BLK - 1.0 - sub_f))).astype(BF16)
        rate = rates[0, :, lanes]
        from_left = carries[0, :, lanes]
        from_right = carries[1, :, lanes]

        def pair(a, b):
            both = jnp.concatenate([a.astype(BF16), b.astype(BF16)], axis=1)
            return spread_rows(both)

        until = (count + (REACH + 1 - BLK)).astype(F32)
        y_left = jnp.dot(
            out_t, pair(from_left, from_left * jnp.exp(-rate * float(BLK))),
            preferred_element_type=F32,
        )
        y_right = jnp.dot(
            in_t,
            pair(from_right * jnp.exp(-rate * until), from_right * jnp.exp(-rate * (until - BLK))),
            preferred_element_type=F32,
        )
        for r in range(0, ROWS, CHUNK):
            rows = slice(r, r + CHUNK)
            at = slice(r % BLK, r % BLK + CHUNK)
            cols = slice((r // BLK) * LANES, (r // BLK + 1) * LANES)
            kept = min(r + CHUNK, capacity) - r
            query = q_ref[rows, lanes].astype(F32)
            grad = g_ref[rows, lanes].astype(F32)
            mixed = m_ref[rows, lanes].astype(F32)
            long_out = yf[rows, lanes] + y_left[at, cols] + skip * mixed
            gated = (query * long_out).astype(BF16) * own[rows]
            out[r : r + kept, lanes] = gated[0:kept]
            dshort[0, rows, :] = grad * long_out
            d_mixed = yb[rows, lanes] + y_right[at, cols] + skip * (grad * query)
            dshort[1, rows, :] = d_mixed * v_ref[rows, lanes].astype(F32)
            dshort[2, rows, :] = d_mixed * k_ref[rows, lanes].astype(F32)

        for m, feat in enumerate((fq, fk, fv)):
            for r in range(0, ROWS, CHUNK):
                kept = min(r + CHUNK, capacity) - r
                rows = slice(r, r + kept)
                keep = own[rows]
                window = feat[rows, lanes] * keep
                total = None
                for tap in range(TAPS):
                    weight = param[TAPS * m + tap : TAPS * m + tap + 1, lanes]
                    shifted = dshort[m, r + tap : r + tap + kept, :]
                    term = weight * shifted
                    total = term if total is None else total + term
                    prods[rows, tap * LANES : (tap + 1) * LANES] = shifted.astype(BF16) * window
                dwin[slot, m, rows, lanes] = total.astype(BF16) * keep
            sums = jnp.dot(jnp.ones((HALO, ROWS), BF16), prods[...], preferred_element_type=F32)
            for tap in range(TAPS):
                dparam[TAPS * m + tap : TAPS * m + tap + 1, lanes] = sums[
                    0:1, tap * LANES : (tap + 1) * LANES
                ]

        crossed = seen[:, lanes] * from_left
        high = crossed.astype(BF16)
        low = (crossed - high.astype(F32)).astype(BF16)
        gather = (iota((LANES, LANES), 0) // GROUP) == (iota((LANES, LANES), 1) // GROUP)
        gather = jnp.where(gather, 1.0, 0.0).astype(BF16)
        sums = jnp.dot(high, gather, preferred_element_type=F32)
        sums = sums + jnp.dot(low, gather, preferred_element_type=F32)
        mine = iota((POLES, LANES), 0) == iota((POLES, LANES), 1) % POLES
        row = jnp.sum(jnp.where(mine, sums, 0.0), axis=0, keepdims=True)
        dparam[RES_ROW : RES_ROW + 1, lanes] = res_in[0:1, lanes] + row
        dparam[SKIP_ROW : SKIP_ROW + 1, lanes] = skips[0:1, lanes]

    for k in range(groups):
        group(k)
    for copy in writes(step, slot):
        copy.start()

    @pl.when(step == shards - 1)
    def _():
        for copy in writes(step - 1, 1 - slot) + writes(step, slot):
            copy.wait()


def meet(peers):
    barrier = pltpu.get_barrier_semaphore()
    for peer in peers:
        pl.semaphore_signal(barrier, inc=1, device_id=peer, device_id_type=MESH)
    pl.semaphore_wait(barrier, len(peers))


def filter_lanes():
    return iota((PER, LANES), 1) // POLES == iota((PER, LANES), 0)


def pole_rows(square, table, chan):
    square[...] = jnp.zeros_like(square)
    square[0:POLES, 0 : chan // GROUP] = table
    turned = jnp.transpose(square[...])
    parts = []
    for g in range(chan // LANES):
        x = turned[g * PER : (g + 1) * PER]
        for gap in (POLES, 2 * POLES, 4 * POLES):
            x = x + pltpu.roll(x, gap, 1)
        parts.append(jnp.sum(jnp.where(filter_lanes(), x, 0.0), axis=0, keepdims=True))
    return jnp.concatenate(parts, axis=1)


def pole_table(square, row, chan):
    square[...] = jnp.zeros_like(square)
    for g in range(chan // LANES):
        x = jnp.broadcast_to(row[:, g * LANES : (g + 1) * LANES], (PER, LANES))
        x = jnp.where(filter_lanes(), x, 0.0)
        for gap in (POLES, 2 * POLES, 4 * POLES):
            x = x + pltpu.roll(x, gap, 1)
        square[g * PER : (g + 1) * PER, :] = x
    return jnp.transpose(square[...])[0:POLES, 0 : chan // GROUP]


def params_kernel(
    shards, count, taps, skip, res, dec, tail, head, head_cot,
    params, tail_in, head_in, cot_in, packed, square, rows, send, recv, own,
):
    dp, me = lax.axis_index("dp"), lax.axis_index("ctx")
    chan = skip.shape[1]
    twin = (dp + 1 - 2 * lax.rem(dp, 2), me)
    half = chan // 2
    lanes = pl.ds(pl.multiple_of(lax.rem(dp, 2) * half, LANES), half)
    peers = [(dp, lax.rem(me + d, shards)) for d in range(1, shards)]
    meet(peers + [twin])

    def post(n, src, dst, peer):
        copy = pltpu.make_async_remote_copy(
            src_ref=src, dst_ref=dst, send_sem=send.at[n], recv_sem=recv.at[n],
            device_id=peer, device_id_type=MESH,
        )
        copy.start()
        return copy

    jobs = [(tail, tail_in, peers[0]), (head, head_in, peers[-1]), (head_cot, cot_in, peers[-1])]
    copies = [post(n, *job) for n, job in enumerate(jobs)]
    for m in range(3):
        rows[TAPS * m : TAPS * (m + 1), :] = taps[m]
    tables = (skip[...], pole_rows(square, res[...], chan), pole_rows(square, dec[...], chan))
    for n, row in enumerate(tables):
        rows[SKIP_ROW + n : SKIP_ROW + n + 1, :] = row
    high = rows[...].astype(BF16)
    low = rows[...] - high.astype(F32)
    low = jnp.where(iota(low.shape, 0) == SKIP_ROW, count[0, 0].astype(F32), low)
    packed[...] = jnp.concatenate([high.astype(F32), low], axis=0).astype(BF16)
    local = pltpu.make_async_copy(packed, params.at[me], own)
    local.start()
    first = [
        post(len(jobs) + n, packed.at[:, lanes], params.at[me, :, lanes], peer)
        for n, peer in enumerate(peers)
    ]
    for n, copy in enumerate(first):
        copy.wait_recv()
        here = params.at[lax.rem(me + shards - 1 - n, shards), :, lanes]
        copies.append(post(len(jobs) + shards - 1 + n, here, here, twin))
    local.wait()
    for copy in first:
        copy.wait_send()
    for copy in copies:
        copy.wait()


def reduce_kernel(
    shards, replicas, part, out, packed, by_ctx, by_dp, send, recv, send_dp, recv_dp,
):
    dp, me = lax.axis_index("dp"), lax.axis_index("ctx")
    chan = out.shape[1]
    half = chan // 2
    peers = [(dp, lax.rem(me + d, shards)) for d in range(1, shards)]
    others = [(lax.rem(dp + d, replicas), me) for d in range(1, replicas)]

    def block(at):
        lanes = pl.ds(pl.multiple_of(at * chan, LANES), chan)
        return part[:, lanes]

    meet(peers + others)
    copies = []
    for n, peer in enumerate(peers):
        mine = block(peer[1])
        packed[n, :, 0:chan] = mine[0:POLES].astype(BF16)
        packed[n, :, chan:] = jnp.concatenate(
            [mine[POLES:, 0:half], mine[POLES:, half:]], axis=0
        ).astype(BF16)
        copies.append(
            pltpu.make_async_remote_copy(
                src_ref=packed.at[n], dst_ref=by_ctx.at[n], send_sem=send.at[n],
                recv_sem=recv.at[n], device_id=peer, device_id_type=MESH,
            )
        )
        copies[-1].start()
    total = block(me)
    top, rest = total[0:POLES], total[POLES:]
    rest = jnp.concatenate([rest[:, 0:half], rest[:, half:]], axis=0)
    for n, copy in enumerate(copies):
        copy.wait()
        top = top + by_ctx[n, :, 0:chan].astype(F32)
        rest = rest + by_ctx[n, :, chan:].astype(F32)
    by_dp[dp, :, 0:chan] = top
    by_dp[dp, :, chan:] = rest
    copies = []
    for n, peer in enumerate(others):
        copies.append(
            pltpu.make_async_remote_copy(
                src_ref=by_dp.at[dp], dst_ref=by_dp.at[dp], send_sem=send_dp.at[n],
                recv_sem=recv_dp.at[n], device_id=peer, device_id_type=MESH,
            )
        )
        copies[-1].start()
    for copy in copies:
        copy.wait()
    total = by_dp[0]
    for n in range(1, replicas):
        total = total + by_dp[n]
    rest = total[:, chan:]
    low = POLES // 2
    rest = jnp.concatenate([rest[0:low], rest[low:]], axis=1)
    out[...] = jnp.concatenate([total[:, 0:chan], rest], axis=0)


def finish_kernel(rows, taps, res, skip, square):
    chan = rows.shape[1]
    for m in range(3):
        taps[m] = rows[TAPS * m : TAPS * (m + 1), :]
    skip[...] = rows[SKIP_ROW : SKIP_ROW + 1, :]
    res[...] = pole_table(square, rows[RES_ROW : RES_ROW + 1, :], chan)


def remote(ident):
    return pltpu.CompilerParams(
        collective_id=ident, has_side_effects=True, vmem_limit_bytes=VMEM_LIMIT
    )


def per_device(features, counts, short_taps, residue, decay_rate, skip_gain, cotangent):
    shards = lax.axis_size("ctx")
    me = lax.axis_index("ctx")
    capacity = features.shape[2]
    width = cotangent.shape[3]
    chan = short_taps.shape[2]
    groups = chan // LANES
    feats = features[0, 0]
    cot = cotangent[0, 0]
    count = counts[0, 0]

    tail = lax.dynamic_slice(feats, (count - HALO, 0), (HALO, 3 * width))
    anywhere = pl.BlockSpec(memory_space=pl.ANY)
    vmem = pl.BlockSpec(memory_space=pltpu.VMEM)
    smem = pl.BlockSpec(memory_space=pltpu.SMEM)
    params, tail, head, head_cot = pl.pallas_call(
        functools.partial(params_kernel, shards),
        in_specs=[smem] + [vmem] * 4 + [anywhere] * 3,
        out_specs=[anywhere] * 4,
        out_shape=[
            jax.ShapeDtypeStruct((shards, PARAM_ROWS, chan), BF16),
            jax.ShapeDtypeStruct((HALO, 3 * width), BF16),
            jax.ShapeDtypeStruct((HALO, 3 * width), BF16),
            jax.ShapeDtypeStruct((HALO, width), BF16),
        ],
        scratch_shapes=[
            pltpu.VMEM((PARAM_ROWS, chan), BF16),
            pltpu.VMEM((LANES, LANES), F32),
            pltpu.VMEM((LOW_ROW, chan), F32),
            pltpu.SemaphoreType.DMA((2 * shards + 1,)),
            pltpu.SemaphoreType.DMA((2 * shards + 1,)),
            pltpu.SemaphoreType.DMA,
        ],
        compiler_params=remote(0),
        name="params",
    )(
        counts, jnp.transpose(short_taps, (1, 0, 2)), skip_gain.reshape(1, chan), residue,
        decay_rate, tail, feats[0:HALO], cot[0:HALO],
    )

    mine = lax.rem(lax.axis_index("dp"), 2) == 0
    every = jnp.where(mine, params[:, CNT_ROW, 0], params[:, CNT_ROW, chan // 2]).astype(F32)
    place = jnp.reshape(me, (1,))
    rounds = (shards - 1).bit_length()

    def cols(rows, offset):
        return pl.BlockSpec((rows, chan), lambda g, *_: (0, offset * shards + g))

    def planes(lead, rows, first=0):
        return pl.BlockSpec((lead, rows, chan), lambda g, *_: (first, 0, g))

    def shape(*dims, dtype=F32):
        return jax.ShapeDtypeStruct(dims, dtype)

    plain = pltpu.CompilerParams(vmem_limit_bytes=VMEM_LIMIT)
    param_spec = pl.BlockSpec((1, PARAM_ROWS, chan), lambda g, *_: (g, 0, 0))
    feat_specs = [cols(capacity, m) for m in range(3)]
    rows_spec = cols(ROWS, 0)
    rows_shape = shape(ROWS, width, dtype=BF16)
    query, key, value, mixed, grad, d_long, states, skips = pl.pallas_call(
        functools.partial(front_kernel, groups, shards),
        grid=(shards,),
        in_specs=[smem, smem] + feat_specs + [cols(capacity, 0)]
        + [cols(HALO, m) for m in range(3)] * 2 + [cols(HALO, 0), param_spec],
        out_specs=[rows_spec] * 6 + [planes(3, POLES), cols(HALO, 0)],
        out_shape=[rows_shape] * 6 + [shape(3, POLES, width), shape(HALO, width)],
        scratch_shapes=[
            pltpu.VMEM((4, HALO + ROWS + HALO, LANES), F32),
            pltpu.VMEM((3, ROWS, LANES), BF16),
            pltpu.VMEM((LOW_ROW, chan), F32),
        ],
        compiler_params=plain,
        name="front",
    )(counts, place, feats, feats, feats, cot, tail, tail, tail, head, head, head, head_cot, params)

    whole = pl.BlockSpec((3, POLES, width), lambda g: (0, 0, 0))
    y_fwd, y_bwd, res_local, seen, carries = pl.pallas_call(
        functools.partial(local_kernel, groups, shards, rounds),
        grid=(shards,),
        in_specs=[smem, smem, rows_spec, rows_spec, param_spec, whole],
        out_specs=[rows_spec, rows_spec, cols(HALO, 0), cols(POLES, 0),
                   pl.BlockSpec((2, POLES, width), lambda g: (0, 0, 0))],
        out_shape=[shape(ROWS, width), shape(ROWS, width), shape(HALO, width),
                   shape(POLES, width), shape(2, POLES, width)],
        scratch_shapes=[
            pltpu.VMEM((ROWS, LANES), BF16),
            pltpu.VMEM((LOW_ROW, chan), F32),
            pltpu.VMEM((2, POLES, width), F32),
            pltpu.VMEM((rounds, 2, POLES, width), BF16),
            pltpu.VMEM((rounds, 2, POLES, width), BF16),
            pltpu.SemaphoreType.DMA((rounds, 2)),
            pltpu.SemaphoreType.DMA((rounds, 2)),
        ],
        compiler_params=remote(1),
        name="local",
    )(counts, every, mixed, d_long, params, states)

    out, dfeat, dparam = pl.pallas_call(
        functools.partial(final_kernel, groups, shards),
        grid=(shards,),
        in_specs=[smem] + feat_specs + [rows_spec] * 7
        + [param_spec, planes(2, POLES), planes(1, POLES, 2), cols(POLES, 0),
           cols(HALO, 0), cols(HALO, 0)],
        out_specs=[cols(capacity, 0), anywhere, cols(GRAD_ROWS, 0)],
        out_shape=[
            shape(capacity, width, dtype=BF16),
            shape(capacity, 3 * width, dtype=BF16),
            shape(GRAD_ROWS, width),
        ],
        scratch_shapes=[
            pltpu.VMEM((ROWS, LANES), BF16),
            pltpu.VMEM((LOW_ROW, chan), F32),
            pltpu.VMEM((3, ROWS + HALO, LANES), F32),
            pltpu.VMEM((ROWS, TAPS * LANES), BF16),
            pltpu.VMEM((2, 3, capacity, chan), BF16),
            pltpu.SemaphoreType.DMA((2, 3)),
        ],
        compiler_params=plain,
        name="final",
    )(counts, feats, feats, feats, query, key, value, mixed, grad, y_fwd, y_bwd, params,
      carries, states, seen, res_local, skips)
    replicas = lax.axis_size("dp")
    rows = pl.pallas_call(
        functools.partial(reduce_kernel, shards, replicas),
        in_specs=[vmem],
        out_specs=vmem,
        out_shape=shape(GRAD_ROWS, chan),
        scratch_shapes=[
            pltpu.VMEM((shards - 1, POLES, chan + chan // 2), BF16),
            pltpu.VMEM((shards - 1, POLES, chan + chan // 2), BF16),
            pltpu.VMEM((replicas, POLES, chan + chan // 2), F32),
            pltpu.SemaphoreType.DMA((shards - 1,)),
            pltpu.SemaphoreType.DMA((shards - 1,)),
            pltpu.SemaphoreType.DMA((replicas - 1,)),
            pltpu.SemaphoreType.DMA((replicas - 1,)),
        ],
        compiler_params=remote(2),
        name="reduce",
    )(dparam)
    taps, res, skip = pl.pallas_call(
        finish_kernel,
        in_specs=[vmem],
        out_specs=[vmem] * 3,
        out_shape=[shape(3, TAPS, chan), shape(POLES, chan // GROUP), shape(1, chan)],
        scratch_shapes=[pltpu.VMEM((LANES, LANES), F32)],
        name="finish",
    )(rows)
    return (
        out[None, None],
        dfeat[None, None],
        jnp.transpose(taps, (1, 0, 2)),
        res,
        skip.reshape(chan),
    )


def solution(mesh):
    in_specs = (
        P("dp", "ctx", None, None),
        P("dp", "ctx"),
        P(None, None, "ctx"),
        P(None, "ctx"),
        P(None, "ctx"),
        P("ctx"),
        P("dp", "ctx", None, None),
    )
    out_specs = (
        P("dp", "ctx", None, None),
        P("dp", "ctx", None, None),
        P(None, None, "ctx"),
        P(None, "ctx"),
        P("ctx"),
    )
    return jax.shard_map(
        per_device, mesh=mesh, in_specs=in_specs, out_specs=out_specs, check_vma=False
    )
```

```python
import functools

import jax
import jax.numpy as jnp
from jax import lax
from jax.experimental import pallas as pl
from jax.experimental.pallas import tpu as pltpu
from jax.sharding import PartitionSpec as P

TAPS = 7
HALO = 8
REACH = TAPS - 1
ROWS = 256
BLK = 128
POLES = 16
GROUP = 16
LANES = 128
PER = LANES // GROUP
F32 = jnp.float32
BF16 = jnp.bfloat16
SKIP_ROW = 3 * TAPS
RES_ROW = SKIP_ROW + 1
DEC_ROW = SKIP_ROW + 2
LOW_ROW = SKIP_ROW + 3
CNT_ROW = LOW_ROW + SKIP_ROW
PARAM_ROWS = 2 * LOW_ROW
GRAD_ROWS = 24
FLAT_ROWS = 32
CHUNK = 64
VMEM_LIMIT = 56 << 20
MESH = pl.DeviceIdType.MESH


def iota(shape, axis):
    return lax.broadcasted_iota(jnp.int32, shape, axis)


def same_filter():
    return (iota((LANES, LANES), 0) // POLES) == (iota((LANES, LANES), 1) // GROUP)


def lane_filter(shape):
    return (iota(shape, 1) % LANES) // GROUP


def column_of(row):
    return jnp.transpose(jnp.broadcast_to(row, (LANES, LANES)))


def pick(full):
    fil = lane_filter((POLES, LANES))
    out = full[0:POLES]
    for f in range(1, PER):
        out = jnp.where(fil == f, full[f * POLES : (f + 1) * POLES], out)
    return out


def spread_rows(x):
    fil = lane_filter(x.shape)
    zero = jnp.zeros_like(x)
    return jnp.concatenate([jnp.where(fil == f, x, zero) for f in range(PER)], axis=0)


def side(x):
    return jnp.concatenate([x[0:BLK], x[BLK:ROWS]], axis=1)


def group_lanes(k):
    return pl.ds(pl.multiple_of(k * LANES, LANES), LANES)


def row_mask(shape, low, high):
    row = iota(shape, 0)
    keep = jnp.logical_and(row >= low, row < high)
    return jnp.where(keep, 1.0, 0.0).astype(BF16)


def fill(scratch, rows_bf, left, right, shift, count, own):
    capacity = rows_bf.shape[0]
    if left is not None:
        scratch[0:HALO, :] = left.astype(F32)
    shift[ROWS : ROWS + HALO, :] = right.astype(F32)
    after = shift[pl.ds(ROWS - count, ROWS), :]
    scratch[HALO : HALO + capacity, :] = (rows_bf * own).astype(F32) + after[0:capacity]
    scratch[HALO + capacity : HALO + ROWS, :] = after[capacity:ROWS]


def front_kernel(
    groups, shards, counts, fq, fk, fv, cot, taps, skip, res, dec_in, tail, head,
    q_out, k_out, v_out, m_out, g_out, d_out, states, skips, flat,
    win, shift, masks, param, packed, square, sent, tail_in, head_in, send, recv,
):
    count = counts[0, 0]
    step = pl.program_id(0)
    capacity = cot.shape[0]
    chan = skip.shape[1]
    dp, me = lax.axis_index("dp"), lax.axis_index("ctx")
    right = (dp, lax.rem(me + 1, shards))
    left = (dp, lax.rem(me + shards - 1, shards))
    block = lax.rem(me + step, shards)

    def copy(kind, at, src, dst, peer):
        return pltpu.make_async_remote_copy(
            src_ref=src, dst_ref=dst, send_sem=send.at[kind, at], recv_sem=recv.at[kind, at],
            device_id=peer, device_id_type=MESH,
        )

    def tail_copy(at):
        theirs = lax.rem(me + 1 + at, shards)
        return copy(0, at, tail.at[theirs], tail_in.at[theirs], right)

    def head_copy(at):
        theirs = lax.rem(me + shards - 1 + at, shards)
        return copy(1, at, head.at[theirs], head_in.at[theirs], left)

    def param_copy(at):
        return copy(2, at, packed, sent.at[me], (dp, lax.rem(me + shards - at, shards)))

    def halos(at):
        @pl.when(me < shards - 1)
        def _():
            tail_copy(at).start()

        @pl.when(me > 0)
        def _():
            head_copy(at).start()

    @pl.when(step == 0)
    def _():
        meet([(dp, lax.rem(me + d, shards)) for d in range(1, shards)])
        halos(0)
        for m in range(3):
            param[TAPS * m : TAPS * (m + 1), :] = taps[m]
        tables = (skip[...], pole_rows(square, res[...], chan), pole_rows(square, dec_in[...], chan))
        for n, row in enumerate(tables):
            param[SKIP_ROW + n : SKIP_ROW + n + 1, :] = row
        high = param[...].astype(BF16)
        low = param[...] - high.astype(F32)
        low = jnp.where(iota(low.shape, 0) == SKIP_ROW, count.astype(F32), low)
        both = jnp.concatenate([high.astype(F32), low], axis=0).astype(BF16)
        packed[...] = both
        sent[me] = both
        for at in range(1, shards):
            param_copy(at).start()
            halos(at)

        @pl.when(me == 0)
        def _():
            tail_in[...] = jnp.zeros_like(tail_in)

        @pl.when(me == shards - 1)
        def _():
            head_in[...] = jnp.zeros_like(head_in)

        masks[0] = row_mask((ROWS, LANES), 0, count)
        masks[1] = row_mask((ROWS, LANES), 0, count + REACH)
        masks[2] = row_mask((ROWS, LANES), REACH, count + REACH)
        shift[...] = jnp.zeros_like(shift)

    @pl.when(step > 0)
    def _():
        param_copy(step).wait_recv()

    @pl.when(me > 0)
    def _():
        tail_copy(step).wait_recv()

    @pl.when(me < shards - 1)
    def _():
        head_copy(step).wait_recv()

    both = sent[block].astype(F32)
    low = both[LOW_ROW:]
    known = both[0:LOW_ROW] + jnp.where(iota(low.shape, 0) == SKIP_ROW, 0.0, low)
    param[...] = known
    flat[0, 0:LOW_ROW, :] = known
    flat[0, LOW_ROW:, :] = jnp.broadcast_to(
        both[CNT_ROW : CNT_ROW + 1], (FLAT_ROWS - LOW_ROW, chan)
    )

    def group(k):
        lanes = slice(k * LANES, (k + 1) * LANES)
        own = masks[0, 0:capacity]

        def near(ref, m):
            at = m * chan + k * LANES
            return ref[block, :, at : at + LANES]

        for m, rows in enumerate((fq, fk, fv)):
            fill(
                win.at[m], rows[:, lanes], near(tail_in, m), near(head_in, m), shift.at[m],
                count, own,
            )
        fill(win.at[3], cot[:, lanes], None, near(head_in, 3), shift.at[3], count, own)
        for r in range(0, ROWS, CHUNK):
            rows = slice(r, r + CHUNK)
            keep = masks[1, rows]
            shorts = []
            for m in range(3):
                total = param[TAPS * m : TAPS * m + 1, lanes] * win[m, HALO + r : HALO + r + CHUNK, :]
                for tap in range(1, TAPS):
                    weight = param[TAPS * m + tap : TAPS * m + tap + 1, lanes]
                    at = HALO + r - tap
                    total = total + weight * win[m, at : at + CHUNK, :]
                shorts.append(total.astype(BF16) * keep)
            query, key, value = shorts
            grad = win[3, HALO + r : HALO + r + CHUNK, :].astype(BF16) * keep
            q_out[rows, lanes] = query
            k_out[rows, lanes] = key
            v_out[rows, lanes] = value
            m_out[rows, lanes] = key * value
            g_out[rows, lanes] = grad
            d_out[rows, lanes] = grad * query

        dec = column_of(param[DEC_ROW : DEC_ROW + 1, lanes])
        lane_f = iota((LANES, LANES), 1).astype(F32)
        tab_l = jnp.exp(-dec * lane_f).astype(BF16)
        tab_r = jnp.exp(-dec * (BLK - 1.0 - lane_f)).astype(BF16)
        d_long = d_out[:, lanes]
        m_own = m_out[:, lanes] * masks[0]
        fwd = jnp.dot(tab_r, side(m_own), preferred_element_type=F32)
        bwd = jnp.dot(tab_l, side(d_long * masks[2]), preferred_element_type=F32)
        rate = pick(dec)
        first = (count - BLK).astype(F32)
        states[0, :, lanes] = jnp.exp(-rate * first) * pick(fwd[:, 0:LANES]) + jnp.exp(
            -rate * (first - BLK)
        ) * pick(fwd[:, LANES:])
        states[1, :, lanes] = jnp.exp(rate * REACH) * pick(bwd[:, 0:LANES]) + jnp.exp(
            -rate * (BLK - REACH)
        ) * pick(bwd[:, LANES:])
        states[2, :, lanes] = rate
        skips[:, lanes] = jnp.dot(
            jnp.ones((HALO, ROWS), BF16), d_long * m_own, preferred_element_type=F32
        )

    for k in range(groups):
        group(k)

    @pl.when(step == shards - 1)
    def _():
        for at in range(shards):
            @pl.when(me < shards - 1)
            def _(at=at):
                tail_copy(at).wait_send()

            @pl.when(me > 0)
            def _(at=at):
                head_copy(at).wait_send()

            if at > 0:
                param_copy(at).wait_send()


def local_group(k, m_ref, d_ref, param, masks, yf, yb, res_out, seen_out):
    lanes = slice(k * LANES, (k + 1) * LANES)
    mixed = m_ref[:, lanes]
    d_long = d_ref[:, lanes]
    res_row = param[0, RES_ROW : RES_ROW + 1, lanes]
    dec_row = param[0, DEC_ROW : DEC_ROW + 1, lanes]
    res = column_of(res_row)
    dec = column_of(dec_row)
    lane_f = iota((LANES, LANES), 1).astype(F32)
    sub_f = iota((LANES, LANES), 0).astype(F32)
    tab_l = jnp.exp(-dec * lane_f)
    tab_r = jnp.exp(-dec * (BLK - 1.0 - lane_f))
    k_lag = jnp.sum((res * tab_l).reshape(PER, POLES, LANES), axis=1)
    k_rest = jnp.sum((res * tab_r).reshape(PER, POLES, LANES), axis=1)
    k_turn = pltpu.roll(k_rest, 1, 1)
    lower = iota((BLK, BLK), 0) >= iota((BLK, BLK), 1)
    upper = iota((BLK, BLK), 0) <= iota((BLK, BLK), 1)

    def toeplitz(rows, keep):
        parts = []
        for f in range(PER):
            wide = jnp.broadcast_to(rows[f : f + 1, :], (BLK, LANES))
            wide = pltpu.roll(wide, 0, 1, stride=1, stride_axis=0)
            parts.append(jnp.where(keep, wide, 0.0).astype(BF16))
        return jnp.concatenate(parts, axis=1)

    own_side = side(d_long * masks[...])
    mirror = iota((BLK, BLK), 0) + iota((BLK, BLK), 1)
    flip = jnp.where(mirror == BLK - 1, 1.0, 0.0).astype(BF16)
    own_flip = jnp.dot(flip, own_side, preferred_element_type=F32).astype(BF16)
    m_stack = spread_rows(side(mixed))
    pair = lax.dot_general(
        own_flip, m_stack, (((1,), (1,)), ((), ())), preferred_element_type=F32
    )
    same = same_filter()
    tab_lb = tab_l.astype(BF16)
    s_first = jnp.dot(tab_r.astype(BF16), mixed[0:BLK], preferred_element_type=F32)
    s_first = jnp.where(same, s_first, 0.0)
    e_second = jnp.dot(tab_lb, d_long[BLK:ROWS], preferred_element_type=F32)
    e_second = jnp.where(same, e_second, 0.0).astype(BF16)
    seen = jnp.dot(tab_lb, own_side, preferred_element_type=F32)
    out_t = (res_row * jnp.exp(-dec_row * (sub_f + 1.0))).astype(BF16)
    in_t = (res_row * jnp.exp(-dec_row * (BLK - sub_f))).astype(BF16)
    y_next = jnp.dot(out_t, s_first.astype(BF16), preferred_element_type=F32)
    y_near = jnp.dot(in_t, e_second, preferred_element_type=F32)
    y_fwd = jnp.dot(toeplitz(k_turn, lower), m_stack, preferred_element_type=F32)
    yf[0:BLK, lanes] = y_fwd[:, 0:LANES]
    yf[BLK:ROWS, lanes] = y_fwd[:, LANES:] + y_next
    d_stack = spread_rows(side(d_long))
    y_bwd = jnp.dot(toeplitz(k_lag, upper), d_stack, preferred_element_type=F32)
    yb[0:BLK, lanes] = y_bwd[:, 0:LANES] + y_near
    yb[BLK:ROWS, lanes] = y_bwd[:, LANES:]

    lag_rows = []
    for f in range(PER):
        piece = jnp.where(mirror < BLK, pair[:, f * LANES : (f + 1) * LANES], 0.0)
        piece = pltpu.roll(piece, 0, 1, stride=1, stride_axis=0)
        lag_rows.append(jnp.broadcast_to(jnp.sum(piece, axis=0, keepdims=True), (POLES, LANES)))
    lag_sums = jnp.concatenate(lag_rows, axis=0)
    res_grad = lag_sums * tab_r + jnp.exp(-dec) * seen[:, LANES:] * s_first
    row = jnp.sum(jnp.transpose(res_grad), axis=0, keepdims=True)
    res_out[:, lanes] = jnp.broadcast_to(row, (HALO, LANES))
    rate = pick(dec)
    seen_out[:, lanes] = jnp.exp(-rate) * pick(seen[:, 0:LANES]) + jnp.exp(
        -rate * (BLK + 1.0)
    ) * pick(seen[:, LANES:])


def local_kernel(
    groups, shards, rounds, counts, every, m_ref, d_ref, param, states,
    yf, yb, res_out, seen_out, carries, masks, total, outbox, inbox, send, recv,
):
    step = pl.program_id(0)
    dp, me = lax.axis_index("dp"), lax.axis_index("ctx")
    chan = m_ref.shape[1]

    def peer(gap):
        return (dp, lax.rem(me + gap + shards, shards))

    def copy(j, way):
        gap = (1 << j) if way == 0 else -(1 << j)
        return pltpu.make_async_remote_copy(
            src_ref=outbox.at[j, way], dst_ref=inbox.at[j, way], send_sem=send.at[j, way],
            recv_sem=recv.at[j, way], device_id=peer(gap), device_id_type=MESH,
        )

    def sends(j, way):
        return me + (1 << j) < shards if way == 0 else me >= (1 << j)

    def start(j):
        for way in range(2):
            @pl.when(sends(j, way))
            def _(way=way):
                outbox[j, way] = total[way].astype(BF16)
                copy(j, way).start()

    def finish(j):
        for way in range(2):
            @pl.when(sends(j, 1 - way))
            def _(way=way):
                copy(j, way).wait_recv()

                gap = 1 << j
                low, high = (me - gap, me) if way == 0 else (me, me + gap)
                inner = jnp.zeros((1, chan), F32)
                for i in range(shards):
                    inside = (i > low) & (i < high)
                    inner = inner + jnp.where(inside, every[i, LOW_ROW : LOW_ROW + 1, :], 0.0)
                outer = inner + counts[0, 0].astype(F32)

                def piece(p, c):
                    lanes = pl.ds(pl.multiple_of(p * chan, LANES), chan)
                    rate = states[2, :, lanes]
                    there = inbox[j, way, :, lanes].astype(F32)
                    near = jnp.exp(-rate * inner) * there
                    carries[way, :, lanes] = carries[way, :, lanes] + near
                    if j < rounds - 1:
                        far = jnp.exp(-rate * outer) * there
                        total[way, :, lanes] = total[way, :, lanes] + far
                    return c

                lax.fori_loop(0, shards, piece, 0)

            @pl.when(sends(j, way))
            def _(way=way):
                copy(j, way).wait_send()

    @pl.when(step == 0)
    def _():
        barrier = pltpu.get_barrier_semaphore()
        greeted = 0
        for j in range(rounds):
            for way in range(2):
                there = sends(j, way)
                greeted = greeted + there.astype(jnp.int32)

                @pl.when(there)
                def _(j=j, way=way):
                    gap = (1 << j) if way == 0 else -(1 << j)
                    pl.semaphore_signal(
                        barrier, inc=1, device_id=peer(gap), device_id_type=MESH
                    )
        pl.semaphore_wait(barrier, greeted)
        masks[...] = row_mask((ROWS, LANES), 0, counts[0, 0])
        carries[...] = jnp.zeros_like(carries)
        total[...] = states[0:2]
        start(0)

    for j in range(1, rounds):
        @pl.when(step == (j * shards) // rounds)
        def _(j=j):
            finish(j - 1)
            start(j)

    for k in range(groups):
        local_group(k, m_ref, d_ref, param, masks, yf, yb, res_out, seen_out)

    @pl.when(step == shards - 1)
    def _():
        finish(rounds - 1)


def final_kernel(
    groups, shards, counts, fq, fk, fv, q_ref, k_ref, v_ref, m_ref, g_ref, yf, yb, param,
    carries, rates, seen, res_in, skips, out, dfeat, dparam,
    own, dshort, prods, dwin, sems,
):
    count = counts[0, 0]
    step = pl.program_id(0)
    capacity = fq.shape[0]
    chan = fq.shape[1]
    slot = lax.rem(step, 2)

    def writes(at, place):
        made = []
        for m in range(3):
            lanes = pl.ds(pl.multiple_of((m * shards + at) * chan, LANES), chan)
            made.append(
                pltpu.make_async_copy(dwin.at[place, m], dfeat.at[:, lanes], sems.at[place, m])
            )
        return made

    @pl.when(step == 0)
    def _():
        own[...] = row_mask((ROWS, LANES), 0, count)
        dshort[:, ROWS:, :] = jnp.zeros((3, dshort.shape[1] - ROWS, LANES), F32)
        prods[...] = jnp.zeros_like(prods)

    @pl.when(step >= 2)
    def _():
        for copy in writes(step - 2, slot):
            copy.wait()

    dparam[GRAD_ROWS - 1 : GRAD_ROWS, :] = jnp.zeros((1, chan), F32)
    def group(k):
        lanes = slice(k * LANES, (k + 1) * LANES)
        res_row = param[0, RES_ROW : RES_ROW + 1, lanes]
        dec_row = param[0, DEC_ROW : DEC_ROW + 1, lanes]
        skip = param[0, SKIP_ROW : SKIP_ROW + 1, lanes]
        sub_f = iota((LANES, LANES), 0).astype(F32)
        out_t = (res_row * jnp.exp(-dec_row * (sub_f + 1.0))).astype(BF16)
        in_t = (res_row * jnp.exp(-dec_row * (BLK - 1.0 - sub_f))).astype(BF16)
        rate = rates[0, :, lanes]
        from_left = carries[0, :, lanes]
        from_right = carries[1, :, lanes]

        def pair(a, b):
            both = jnp.concatenate([a.astype(BF16), b.astype(BF16)], axis=1)
            return spread_rows(both)

        until = (count + (REACH + 1 - BLK)).astype(F32)
        y_left = jnp.dot(
            out_t, pair(from_left, from_left * jnp.exp(-rate * float(BLK))),
            preferred_element_type=F32,
        )
        y_right = jnp.dot(
            in_t,
            pair(from_right * jnp.exp(-rate * until), from_right * jnp.exp(-rate * (until - BLK))),
            preferred_element_type=F32,
        )
        for r in range(0, ROWS, CHUNK):
            rows = slice(r, r + CHUNK)
            at = slice(r % BLK, r % BLK + CHUNK)
            cols = slice((r // BLK) * LANES, (r // BLK + 1) * LANES)
            kept = min(r + CHUNK, capacity) - r
            query = q_ref[rows, lanes].astype(F32)
            grad = g_ref[rows, lanes].astype(F32)
            mixed = m_ref[rows, lanes].astype(F32)
            long_out = yf[rows, lanes] + y_left[at, cols] + skip * mixed
            gated = (query * long_out).astype(BF16) * own[rows]
            out[r : r + kept, lanes] = gated[0:kept]
            dshort[0, rows, :] = grad * long_out
            d_mixed = yb[rows, lanes] + y_right[at, cols] + skip * (grad * query)
            dshort[1, rows, :] = d_mixed * v_ref[rows, lanes].astype(F32)
            dshort[2, rows, :] = d_mixed * k_ref[rows, lanes].astype(F32)

        for m, feat in enumerate((fq, fk, fv)):
            for r in range(0, ROWS, CHUNK):
                kept = min(r + CHUNK, capacity) - r
                rows = slice(r, r + kept)
                keep = own[rows]
                window = feat[rows, lanes] * keep
                total = None
                for tap in range(TAPS):
                    weight = param[0, TAPS * m + tap : TAPS * m + tap + 1, lanes]
                    shifted = dshort[m, r + tap : r + tap + kept, :]
                    term = weight * shifted
                    total = term if total is None else total + term
                    prods[rows, tap * LANES : (tap + 1) * LANES] = shifted.astype(BF16) * window
                dwin[slot, m, rows, lanes] = total.astype(BF16) * keep
            sums = jnp.dot(jnp.ones((HALO, ROWS), BF16), prods[...], preferred_element_type=F32)
            for tap in range(TAPS):
                dparam[TAPS * m + tap : TAPS * m + tap + 1, lanes] = sums[
                    0:1, tap * LANES : (tap + 1) * LANES
                ]

        crossed = seen[:, lanes] * from_left
        high = crossed.astype(BF16)
        low = (crossed - high.astype(F32)).astype(BF16)
        gather = (iota((LANES, LANES), 0) // GROUP) == (iota((LANES, LANES), 1) // GROUP)
        gather = jnp.where(gather, 1.0, 0.0).astype(BF16)
        sums = jnp.dot(high, gather, preferred_element_type=F32)
        sums = sums + jnp.dot(low, gather, preferred_element_type=F32)
        mine = iota((POLES, LANES), 0) == iota((POLES, LANES), 1) % POLES
        row = jnp.sum(jnp.where(mine, sums, 0.0), axis=0, keepdims=True)
        dparam[RES_ROW : RES_ROW + 1, lanes] = res_in[0:1, lanes] + row
        dparam[SKIP_ROW : SKIP_ROW + 1, lanes] = skips[0:1, lanes]

    for k in range(groups):
        group(k)
    for copy in writes(step, slot):
        copy.start()

    @pl.when(step == shards - 1)
    def _():
        for copy in writes(step - 1, 1 - slot) + writes(step, slot):
            copy.wait()


def meet(peers):
    barrier = pltpu.get_barrier_semaphore()
    for peer in peers:
        pl.semaphore_signal(barrier, inc=1, device_id=peer, device_id_type=MESH)
    pl.semaphore_wait(barrier, len(peers))


def filter_lanes():
    return iota((PER, LANES), 1) // POLES == iota((PER, LANES), 0)


def pole_rows(square, table, chan):
    square[...] = jnp.zeros_like(square)
    square[0:POLES, 0 : chan // GROUP] = table
    turned = jnp.transpose(square[...])
    parts = []
    for g in range(chan // LANES):
        x = turned[g * PER : (g + 1) * PER]
        for gap in (POLES, 2 * POLES, 4 * POLES):
            x = x + pltpu.roll(x, gap, 1)
        parts.append(jnp.sum(jnp.where(filter_lanes(), x, 0.0), axis=0, keepdims=True))
    return jnp.concatenate(parts, axis=1)


def pole_table(square, row, chan):
    square[...] = jnp.zeros_like(square)
    for g in range(chan // LANES):
        x = jnp.broadcast_to(row[:, g * LANES : (g + 1) * LANES], (PER, LANES))
        x = jnp.where(filter_lanes(), x, 0.0)
        for gap in (POLES, 2 * POLES, 4 * POLES):
            x = x + pltpu.roll(x, gap, 1)
        square[g * PER : (g + 1) * PER, :] = x
    return jnp.transpose(square[...])[0:POLES, 0 : chan // GROUP]


def reduce_kernel(
    shards, replicas, part, out, packed, by_ctx, by_dp, send, recv, send_dp, recv_dp,
):
    dp, me = lax.axis_index("dp"), lax.axis_index("ctx")
    chan = out.shape[1]
    half = chan // 2
    peers = [(dp, lax.rem(me + d, shards)) for d in range(1, shards)]
    others = [(lax.rem(dp + d, replicas), me) for d in range(1, replicas)]

    def block(at):
        lanes = pl.ds(pl.multiple_of(at * chan, LANES), chan)
        return part[:, lanes]

    meet(peers + others)
    copies = []
    for n, peer in enumerate(peers):
        mine = block(peer[1])
        packed[n, :, 0:chan] = mine[0:POLES].astype(BF16)
        packed[n, :, chan:] = jnp.concatenate(
            [mine[POLES:, 0:half], mine[POLES:, half:]], axis=0
        ).astype(BF16)
        copies.append(
            pltpu.make_async_remote_copy(
                src_ref=packed.at[n], dst_ref=by_ctx.at[n], send_sem=send.at[n],
                recv_sem=recv.at[n], device_id=peer, device_id_type=MESH,
            )
        )
        copies[-1].start()
    total = block(me)
    top, rest = total[0:POLES], total[POLES:]
    rest = jnp.concatenate([rest[:, 0:half], rest[:, half:]], axis=0)
    for n, copy in enumerate(copies):
        copy.wait()
        top = top + by_ctx[n, :, 0:chan].astype(F32)
        rest = rest + by_ctx[n, :, chan:].astype(F32)
    by_dp[dp, :, 0:chan] = top
    by_dp[dp, :, chan:] = rest
    copies = []
    for n, peer in enumerate(others):
        copies.append(
            pltpu.make_async_remote_copy(
                src_ref=by_dp.at[dp], dst_ref=by_dp.at[dp], send_sem=send_dp.at[n],
                recv_sem=recv_dp.at[n], device_id=peer, device_id_type=MESH,
            )
        )
        copies[-1].start()
    for copy in copies:
        copy.wait()
    total = by_dp[0]
    for n in range(1, replicas):
        total = total + by_dp[n]
    rest = total[:, chan:]
    low = POLES // 2
    rest = jnp.concatenate([rest[0:low], rest[low:]], axis=1)
    out[...] = jnp.concatenate([total[:, 0:chan], rest], axis=0)


def finish_kernel(rows, taps, res, skip, square):
    chan = rows.shape[1]
    for m in range(3):
        taps[m] = rows[TAPS * m : TAPS * (m + 1), :]
    skip[...] = rows[SKIP_ROW : SKIP_ROW + 1, :]
    res[...] = pole_table(square, rows[RES_ROW : RES_ROW + 1, :], chan)


def remote(ident):
    return pltpu.CompilerParams(
        collective_id=ident, has_side_effects=True, vmem_limit_bytes=VMEM_LIMIT
    )


def per_device(features, counts, short_taps, residue, decay_rate, skip_gain, cotangent):
    shards = lax.axis_size("ctx")
    capacity = features.shape[2]
    width = cotangent.shape[3]
    chan = short_taps.shape[2]
    groups = chan // LANES
    feats = features[0, 0]
    cot = cotangent[0, 0]
    count = counts[0, 0]

    def by_block(rows):
        rows = rows.reshape(HALO, -1, shards, chan)
        return jnp.transpose(rows, (2, 0, 1, 3)).reshape(shards, HALO, -1)

    tail = by_block(lax.dynamic_slice(feats, (count - HALO, 0), (HALO, 3 * width)))
    head = by_block(jnp.concatenate([feats[0:HALO], cot[0:HALO]], axis=1))
    anywhere = pl.BlockSpec(memory_space=pl.ANY)
    vmem = pl.BlockSpec(memory_space=pltpu.VMEM)
    smem = pl.BlockSpec(memory_space=pltpu.SMEM)
    rounds = (shards - 1).bit_length()

    def cols(rows, offset):
        return pl.BlockSpec((rows, chan), lambda g, *_: (0, offset * shards + g))

    def turn(g):
        return lax.rem(lax.axis_index("ctx") + g, shards)

    def turned(rows, offset):
        return pl.BlockSpec((rows, chan), lambda g: (0, offset * shards + turn(g)))

    def planes(lead, rows, first=0):
        return pl.BlockSpec((lead, rows, chan), lambda g, *_: (first, 0, g))

    def shape(*dims, dtype=F32):
        return jax.ShapeDtypeStruct(dims, dtype)

    plain = pltpu.CompilerParams(vmem_limit_bytes=VMEM_LIMIT)
    param_spec = pl.BlockSpec((1, FLAT_ROWS, chan), lambda g: (g, 0, 0))
    feat_specs = [cols(capacity, m) for m in range(3)]
    rows_spec = cols(ROWS, 0)
    rows_shape = shape(ROWS, width, dtype=BF16)
    query, key, value, mixed, grad, d_long, states, skips, flat = pl.pallas_call(
        functools.partial(front_kernel, groups, shards),
        grid=(shards,),
        in_specs=[smem] + [turned(capacity, m) for m in range(3)] + [turned(capacity, 0)]
        + [vmem] * 4 + [anywhere] * 2,
        out_specs=[turned(ROWS, 0)] * 6
        + [pl.BlockSpec((3, POLES, chan), lambda g: (0, 0, turn(g))), turned(HALO, 0)]
        + [pl.BlockSpec((1, FLAT_ROWS, chan), lambda g: (turn(g), 0, 0))],
        out_shape=[rows_shape] * 6
        + [shape(3, POLES, width), shape(HALO, width), shape(shards, FLAT_ROWS, chan)],
        scratch_shapes=[
            pltpu.VMEM((4, HALO + ROWS, LANES), F32),
            pltpu.VMEM((4, 2 * ROWS + HALO, LANES), F32),
            pltpu.VMEM((3, ROWS, LANES), BF16),
            pltpu.VMEM((LOW_ROW, chan), F32),
            pltpu.VMEM((PARAM_ROWS, chan), BF16),
            pltpu.VMEM((LANES, LANES), F32),
            pltpu.VMEM((shards, PARAM_ROWS, chan), BF16),
            pltpu.VMEM((shards, HALO, 3 * chan), BF16),
            pltpu.VMEM((shards, HALO, 4 * chan), BF16),
            pltpu.SemaphoreType.DMA((3, shards)),
            pltpu.SemaphoreType.DMA((3, shards)),
        ],
        compiler_params=remote(0),
        name="front",
    )(
        counts, feats, feats, feats, cot, jnp.transpose(short_taps, (1, 0, 2)),
        skip_gain.reshape(1, chan), residue, decay_rate, tail, head,
    )

    whole = pl.BlockSpec((3, POLES, width), lambda g: (0, 0, 0))
    y_fwd, y_bwd, res_local, seen, carries = pl.pallas_call(
        functools.partial(local_kernel, groups, shards, rounds),
        grid=(shards,),
        in_specs=[smem, pl.BlockSpec((shards, FLAT_ROWS, chan), lambda g: (0, 0, 0)), rows_spec, rows_spec, param_spec, whole],
        out_specs=[rows_spec, rows_spec, cols(HALO, 0), cols(POLES, 0),
                   pl.BlockSpec((2, POLES, width), lambda g: (0, 0, 0))],
        out_shape=[shape(ROWS, width), shape(ROWS, width), shape(HALO, width),
                   shape(POLES, width), shape(2, POLES, width)],
        scratch_shapes=[
            pltpu.VMEM((ROWS, LANES), BF16),
            pltpu.VMEM((2, POLES, width), F32),
            pltpu.VMEM((rounds, 2, POLES, width), BF16),
            pltpu.VMEM((rounds, 2, POLES, width), BF16),
            pltpu.SemaphoreType.DMA((rounds, 2)),
            pltpu.SemaphoreType.DMA((rounds, 2)),
        ],
        compiler_params=remote(1),
        name="local",
    )(counts, flat, mixed, d_long, flat, states)

    out, dfeat, dparam = pl.pallas_call(
        functools.partial(final_kernel, groups, shards),
        grid=(shards,),
        in_specs=[smem] + feat_specs + [rows_spec] * 7
        + [param_spec, planes(2, POLES), planes(1, POLES, 2), cols(POLES, 0),
           cols(HALO, 0), cols(HALO, 0)],
        out_specs=[cols(capacity, 0), anywhere, cols(GRAD_ROWS, 0)],
        out_shape=[
            shape(capacity, width, dtype=BF16),
            shape(capacity, 3 * width, dtype=BF16),
            shape(GRAD_ROWS, width),
        ],
        scratch_shapes=[
            pltpu.VMEM((ROWS, LANES), BF16),
            pltpu.VMEM((3, ROWS + HALO, LANES), F32),
            pltpu.VMEM((ROWS, TAPS * LANES), BF16),
            pltpu.VMEM((2, 3, capacity, chan), BF16),
            pltpu.SemaphoreType.DMA((2, 3)),
        ],
        compiler_params=plain,
        name="final",
    )(counts, feats, feats, feats, query, key, value, mixed, grad, y_fwd, y_bwd, flat,
      carries, states, seen, res_local, skips)
    replicas = lax.axis_size("dp")
    rows = pl.pallas_call(
        functools.partial(reduce_kernel, shards, replicas),
        in_specs=[vmem],
        out_specs=vmem,
        out_shape=shape(GRAD_ROWS, chan),
        scratch_shapes=[
            pltpu.VMEM((shards - 1, POLES, chan + chan // 2), BF16),
            pltpu.VMEM((shards - 1, POLES, chan + chan // 2), BF16),
            pltpu.VMEM((replicas, POLES, chan + chan // 2), F32),
            pltpu.SemaphoreType.DMA((shards - 1,)),
            pltpu.SemaphoreType.DMA((shards - 1,)),
            pltpu.SemaphoreType.DMA((replicas - 1,)),
            pltpu.SemaphoreType.DMA((replicas - 1,)),
        ],
        compiler_params=remote(2),
        name="reduce",
    )(dparam)
    taps, res, skip = pl.pallas_call(
        finish_kernel,
        in_specs=[vmem],
        out_specs=[vmem] * 3,
        out_shape=[shape(3, TAPS, chan), shape(POLES, chan // GROUP), shape(1, chan)],
        scratch_shapes=[pltpu.VMEM((LANES, LANES), F32)],
        name="finish",
    )(rows)
    return (
        out[None, None],
        dfeat[None, None],
        jnp.transpose(taps, (1, 0, 2)),
        res,
        skip.reshape(chan),
    )


def solution(mesh):
    in_specs = (
        P("dp", "ctx", None, None),
        P("dp", "ctx"),
        P(None, None, "ctx"),
        P(None, "ctx"),
        P(None, "ctx"),
        P("ctx"),
        P("dp", "ctx", None, None),
    )
    out_specs = (
        P("dp", "ctx", None, None),
        P("dp", "ctx", None, None),
        P(None, None, "ctx"),
        P(None, "ctx"),
        P("ctx"),
    )
    return jax.shard_map(
        per_device, mesh=mesh, in_specs=in_specs, out_specs=out_specs, check_vma=False
    )
```

```python
import functools

import jax
import jax.numpy as jnp
from jax import lax
from jax.experimental import pallas as pl
from jax.experimental.pallas import tpu as pltpu
from jax.sharding import PartitionSpec as P

TAPS = 7
HALO = 8
REACH = TAPS - 1
ROWS = 256
BLK = 128
POLES = 16
GROUP = 16
LANES = 128
PER = LANES // GROUP
F32 = jnp.float32
BF16 = jnp.bfloat16
SKIP_ROW = 3 * TAPS
RES_ROW = SKIP_ROW + 1
DEC_ROW = SKIP_ROW + 2
LOW_ROW = SKIP_ROW + 3
CNT_ROW = LOW_ROW + SKIP_ROW
PARAM_ROWS = 2 * LOW_ROW
GRAD_ROWS = 24
FLAT_ROWS = 32
CHUNK = 64
AHEAD = 2
VMEM_LIMIT = 56 << 20
MESH = pl.DeviceIdType.MESH


def iota(shape, axis):
    return lax.broadcasted_iota(jnp.int32, shape, axis)


def same_filter():
    return (iota((LANES, LANES), 0) // POLES) == (iota((LANES, LANES), 1) // GROUP)


def lane_filter(shape):
    return (iota(shape, 1) % LANES) // GROUP


def column_of(row):
    return jnp.transpose(jnp.broadcast_to(row, (LANES, LANES)))


def pick(full):
    fil = lane_filter((POLES, LANES))
    out = full[0:POLES]
    for f in range(1, PER):
        out = jnp.where(fil == f, full[f * POLES : (f + 1) * POLES], out)
    return out


def spread_rows(x):
    fil = lane_filter(x.shape)
    zero = jnp.zeros_like(x)
    return jnp.concatenate([jnp.where(fil == f, x, zero) for f in range(PER)], axis=0)


def side(x):
    return jnp.concatenate([x[0:BLK], x[BLK:ROWS]], axis=1)


def group_lanes(k):
    return pl.ds(pl.multiple_of(k * LANES, LANES), LANES)


def row_mask(shape, low, high):
    row = iota(shape, 0)
    keep = jnp.logical_and(row >= low, row < high)
    return jnp.where(keep, 1.0, 0.0).astype(BF16)


def fill(scratch, rows_bf, left, right, shift, count, own):
    capacity = rows_bf.shape[0]
    if left is not None:
        scratch[0:HALO, :] = left.astype(F32)
    shift[ROWS : ROWS + HALO, :] = right.astype(F32)
    after = shift[pl.ds(ROWS - count, ROWS), :]
    scratch[HALO : HALO + capacity, :] = (rows_bf * own).astype(F32) + after[0:capacity]
    scratch[HALO + capacity : HALO + ROWS, :] = after[capacity:ROWS]


def front_kernel(
    groups, shards, counts, fq, fk, fv, cot, taps, skip, res, dec_in, last, first, first_cot,
    q_out, k_out, v_out, m_out, g_out, d_out, states, skips, flat,
    win, shift, masks, param, packed, square, sent, tail, head, tail_in, head_in, send, recv,
):
    count = counts[0, 0]
    step = pl.program_id(0)
    capacity = cot.shape[0]
    chan = skip.shape[1]
    dp, me = lax.axis_index("dp"), lax.axis_index("ctx")
    right = (dp, lax.rem(me + 1, shards))
    left = (dp, lax.rem(me + shards - 1, shards))
    block = lax.rem(me + step, shards)

    def copy(kind, at, src, dst, peer):
        return pltpu.make_async_remote_copy(
            src_ref=src, dst_ref=dst, send_sem=send.at[kind, at], recv_sem=recv.at[kind, at],
            device_id=peer, device_id_type=MESH,
        )

    def tail_copy(at):
        theirs = lax.rem(me + 1 + at, shards)
        return copy(0, at, tail.at[theirs], tail_in.at[theirs], right)

    def head_copy(at):
        theirs = lax.rem(me + shards - 1 + at, shards)
        return copy(1, at, head.at[theirs], head_in.at[theirs], left)

    def param_copy(at):
        return copy(2, at, packed, sent.at[me], (dp, lax.rem(me + shards - at, shards)))

    def halos(at):
        @pl.when(me < shards - 1)
        def _():
            tail_copy(at).start()

        @pl.when(me > 0)
        def _():
            head_copy(at).start()

    @pl.when(step == 0)
    def _():
        for at in range(shards):
            for m in range(4):
                into = slice(m * chan, (m + 1) * chan)
                lanes = slice((m * shards + at) * chan, (m * shards + at + 1) * chan)
                if m < 3:
                    tail[at, :, into] = last[:, lanes]
                    head[at, :, into] = first[:, lanes]
                else:
                    head[at, :, into] = first_cot[:, at * chan : (at + 1) * chan]
        meet([(dp, lax.rem(me + d, shards)) for d in range(1, shards)])
        halos(0)
        for m in range(3):
            param[TAPS * m : TAPS * (m + 1), :] = taps[m]
        tables = (skip[...], pole_rows(square, res[...], chan), pole_rows(square, dec_in[...], chan))
        for n, row in enumerate(tables):
            param[SKIP_ROW + n : SKIP_ROW + n + 1, :] = row
        high = param[...].astype(BF16)
        low = param[...] - high.astype(F32)
        low = jnp.where(iota(low.shape, 0) == SKIP_ROW, count.astype(F32), low)
        both = jnp.concatenate([high.astype(F32), low], axis=0).astype(BF16)
        packed[...] = both
        sent[me] = both
        for at in range(1, min(AHEAD + 1, shards)):
            param_copy(at).start()
            halos(at)

        @pl.when(me == 0)
        def _():
            tail_in[...] = jnp.zeros_like(tail_in)

        @pl.when(me == shards - 1)
        def _():
            head_in[...] = jnp.zeros_like(head_in)

        masks[0] = row_mask((ROWS, LANES), 0, count)
        masks[1] = row_mask((ROWS, LANES), 0, count + REACH)
        masks[2] = row_mask((ROWS, LANES), REACH, count + REACH)
        shift[...] = jnp.zeros_like(shift)

    @pl.when(jnp.logical_and(step > 0, step + AHEAD < shards))
    def _():
        param_copy(step + AHEAD).start()
        halos(step + AHEAD)

    @pl.when(step > 0)
    def _():
        param_copy(step).wait_recv()

    @pl.when(me > 0)
    def _():
        tail_copy(step).wait_recv()

    @pl.when(me < shards - 1)
    def _():
        head_copy(step).wait_recv()

    both = sent[block].astype(F32)
    low = both[LOW_ROW:]
    known = both[0:LOW_ROW] + jnp.where(iota(low.shape, 0) == SKIP_ROW, 0.0, low)
    param[...] = known
    flat[0, 0:LOW_ROW, :] = known
    flat[0, LOW_ROW:, :] = jnp.broadcast_to(
        both[CNT_ROW : CNT_ROW + 1], (FLAT_ROWS - LOW_ROW, chan)
    )

    def group(k):
        lanes = slice(k * LANES, (k + 1) * LANES)
        own = masks[0, 0:capacity]

        def near(ref, m):
            at = m * chan + k * LANES
            return ref[block, :, at : at + LANES]

        for m, rows in enumerate((fq, fk, fv)):
            fill(
                win.at[m], rows[:, lanes], near(tail_in, m), near(head_in, m), shift.at[m],
                count, own,
            )
        fill(win.at[3], cot[:, lanes], None, near(head_in, 3), shift.at[3], count, own)
        for r in range(0, ROWS, CHUNK):
            rows = slice(r, r + CHUNK)
            keep = masks[1, rows]
            shorts = []
            for m in range(3):
                total = param[TAPS * m : TAPS * m + 1, lanes] * win[m, HALO + r : HALO + r + CHUNK, :]
                for tap in range(1, TAPS):
                    weight = param[TAPS * m + tap : TAPS * m + tap + 1, lanes]
                    at = HALO + r - tap
                    total = total + weight * win[m, at : at + CHUNK, :]
                shorts.append(total.astype(BF16) * keep)
            query, key, value = shorts
            grad = win[3, HALO + r : HALO + r + CHUNK, :].astype(BF16) * keep
            q_out[rows, lanes] = query
            k_out[rows, lanes] = key
            v_out[rows, lanes] = value
            m_out[rows, lanes] = key * value
            g_out[rows, lanes] = grad
            d_out[rows, lanes] = grad * query

        dec = column_of(param[DEC_ROW : DEC_ROW + 1, lanes])
        lane_f = iota((LANES, LANES), 1).astype(F32)
        tab_l = jnp.exp(-dec * lane_f).astype(BF16)
        tab_r = jnp.exp(-dec * (BLK - 1.0 - lane_f)).astype(BF16)
        d_long = d_out[:, lanes]
        m_own = m_out[:, lanes] * masks[0]
        fwd = jnp.dot(tab_r, side(m_own), preferred_element_type=F32)
        bwd = jnp.dot(tab_l, side(d_long * masks[2]), preferred_element_type=F32)
        rate = pick(dec)
        first = (count - BLK).astype(F32)
        states[0, :, lanes] = jnp.exp(-rate * first) * pick(fwd[:, 0:LANES]) + jnp.exp(
            -rate * (first - BLK)
        ) * pick(fwd[:, LANES:])
        states[1, :, lanes] = jnp.exp(rate * REACH) * pick(bwd[:, 0:LANES]) + jnp.exp(
            -rate * (BLK - REACH)
        ) * pick(bwd[:, LANES:])
        states[2, :, lanes] = rate
        skips[:, lanes] = jnp.dot(
            jnp.ones((HALO, ROWS), BF16), d_long * m_own, preferred_element_type=F32
        )

    for k in range(groups):
        group(k)

    @pl.when(step == shards - 1)
    def _():
        for at in range(shards):
            @pl.when(me < shards - 1)
            def _(at=at):
                tail_copy(at).wait_send()

            @pl.when(me > 0)
            def _(at=at):
                head_copy(at).wait_send()

            if at > 0:
                param_copy(at).wait_send()


def local_group(k, m_ref, d_ref, param, masks, yf, yb, res_out, seen_out):
    lanes = slice(k * LANES, (k + 1) * LANES)
    mixed = m_ref[:, lanes]
    d_long = d_ref[:, lanes]
    res_row = param[0, RES_ROW : RES_ROW + 1, lanes]
    dec_row = param[0, DEC_ROW : DEC_ROW + 1, lanes]
    res = column_of(res_row)
    dec = column_of(dec_row)
    lane_f = iota((LANES, LANES), 1).astype(F32)
    sub_f = iota((LANES, LANES), 0).astype(F32)
    tab_l = jnp.exp(-dec * lane_f)
    tab_r = jnp.exp(-dec * (BLK - 1.0 - lane_f))
    k_lag = jnp.sum((res * tab_l).reshape(PER, POLES, LANES), axis=1)
    k_rest = jnp.sum((res * tab_r).reshape(PER, POLES, LANES), axis=1)
    k_turn = pltpu.roll(k_rest, 1, 1)
    lower = iota((BLK, BLK), 0) >= iota((BLK, BLK), 1)
    upper = iota((BLK, BLK), 0) <= iota((BLK, BLK), 1)

    def toeplitz(rows, keep):
        parts = []
        for f in range(PER):
            wide = jnp.broadcast_to(rows[f : f + 1, :], (BLK, LANES))
            wide = pltpu.roll(wide, 0, 1, stride=1, stride_axis=0)
            parts.append(jnp.where(keep, wide, 0.0).astype(BF16))
        return jnp.concatenate(parts, axis=1)

    t_fwd = toeplitz(k_turn, lower)
    yield
    own_side = side(d_long * masks[...])
    mirror = iota((BLK, BLK), 0) + iota((BLK, BLK), 1)
    flip = jnp.where(mirror == BLK - 1, 1.0, 0.0).astype(BF16)
    own_flip = jnp.dot(flip, own_side, preferred_element_type=F32).astype(BF16)
    m_stack = spread_rows(side(mixed))
    pair = lax.dot_general(
        own_flip, m_stack, (((1,), (1,)), ((), ())), preferred_element_type=F32
    )
    yield
    same = same_filter()
    tab_lb = tab_l.astype(BF16)
    s_first = jnp.dot(tab_r.astype(BF16), mixed[0:BLK], preferred_element_type=F32)
    s_first = jnp.where(same, s_first, 0.0)
    e_second = jnp.dot(tab_lb, d_long[BLK:ROWS], preferred_element_type=F32)
    e_second = jnp.where(same, e_second, 0.0).astype(BF16)
    seen = jnp.dot(tab_lb, own_side, preferred_element_type=F32)
    out_t = (res_row * jnp.exp(-dec_row * (sub_f + 1.0))).astype(BF16)
    in_t = (res_row * jnp.exp(-dec_row * (BLK - sub_f))).astype(BF16)
    y_next = jnp.dot(out_t, s_first.astype(BF16), preferred_element_type=F32)
    y_near = jnp.dot(in_t, e_second, preferred_element_type=F32)
    yield
    y_fwd = jnp.dot(t_fwd, m_stack, preferred_element_type=F32)
    yf[0:BLK, lanes] = y_fwd[:, 0:LANES]
    yf[BLK:ROWS, lanes] = y_fwd[:, LANES:] + y_next
    t_bwd = toeplitz(k_lag, upper)
    yield
    d_stack = spread_rows(side(d_long))
    y_bwd = jnp.dot(t_bwd, d_stack, preferred_element_type=F32)
    yb[0:BLK, lanes] = y_bwd[:, 0:LANES] + y_near
    yb[BLK:ROWS, lanes] = y_bwd[:, LANES:]

    yield
    lag_rows = []
    for f in range(PER):
        piece = jnp.where(mirror < BLK, pair[:, f * LANES : (f + 1) * LANES], 0.0)
        piece = pltpu.roll(piece, 0, 1, stride=1, stride_axis=0)
        lag_rows.append(jnp.broadcast_to(jnp.sum(piece, axis=0, keepdims=True), (POLES, LANES)))
    lag_sums = jnp.concatenate(lag_rows, axis=0)
    res_grad = lag_sums * tab_r + jnp.exp(-dec) * seen[:, LANES:] * s_first
    row = jnp.sum(jnp.transpose(res_grad), axis=0, keepdims=True)
    res_out[:, lanes] = jnp.broadcast_to(row, (HALO, LANES))
    rate = pick(dec)
    seen_out[:, lanes] = jnp.exp(-rate) * pick(seen[:, 0:LANES]) + jnp.exp(
        -rate * (BLK + 1.0)
    ) * pick(seen[:, LANES:])
    yield


def staggered(makers, stages, lag):
    for turn in range(stages + lag * (len(makers) - 1)):
        for k, maker in enumerate(makers):
            if 0 <= turn - lag * k < stages:
                next(maker)


def local_kernel(
    groups, shards, rounds, counts, every, m_ref, d_ref, param, states,
    yf, yb, res_out, seen_out, carries, masks, total, outbox, inbox, send, recv,
):
    step = pl.program_id(0)
    dp, me = lax.axis_index("dp"), lax.axis_index("ctx")
    chan = m_ref.shape[1]

    def peer(gap):
        return (dp, lax.rem(me + gap + shards, shards))

    def copy(j, way):
        gap = (1 << j) if way == 0 else -(1 << j)
        return pltpu.make_async_remote_copy(
            src_ref=outbox.at[j, way], dst_ref=inbox.at[j, way], send_sem=send.at[j, way],
            recv_sem=recv.at[j, way], device_id=peer(gap), device_id_type=MESH,
        )

    def sends(j, way):
        return me + (1 << j) < shards if way == 0 else me >= (1 << j)

    def start(j):
        for way in range(2):
            @pl.when(sends(j, way))
            def _(way=way):
                outbox[j, way] = total[way].astype(BF16)
                copy(j, way).start()

    def finish(j):
        for way in range(2):
            @pl.when(sends(j, 1 - way))
            def _(way=way):
                copy(j, way).wait_recv()

                gap = 1 << j
                low, high = (me - gap, me) if way == 0 else (me, me + gap)
                inner = jnp.zeros((1, chan), F32)
                for i in range(shards):
                    inside = (i > low) & (i < high)
                    inner = inner + jnp.where(inside, every[i, LOW_ROW : LOW_ROW + 1, :], 0.0)
                outer = inner + counts[0, 0].astype(F32)

                def piece(p, c):
                    lanes = pl.ds(pl.multiple_of(p * chan, LANES), chan)
                    rate = states[2, :, lanes]
                    there = inbox[j, way, :, lanes].astype(F32)
                    near = jnp.exp(-rate * inner) * there
                    carries[way, :, lanes] = carries[way, :, lanes] + near
                    if j < rounds - 1:
                        far = jnp.exp(-rate * outer) * there
                        total[way, :, lanes] = total[way, :, lanes] + far
                    return c

                lax.fori_loop(0, shards, piece, 0)

            @pl.when(sends(j, way))
            def _(way=way):
                copy(j, way).wait_send()

    @pl.when(step == 0)
    def _():
        barrier = pltpu.get_barrier_semaphore()
        greeted = 0
        for j in range(rounds):
            for way in range(2):
                there = sends(j, way)
                greeted = greeted + there.astype(jnp.int32)

                @pl.when(there)
                def _(j=j, way=way):
                    gap = (1 << j) if way == 0 else -(1 << j)
                    pl.semaphore_signal(
                        barrier, inc=1, device_id=peer(gap), device_id_type=MESH
                    )
        pl.semaphore_wait(barrier, greeted)
        masks[...] = row_mask((ROWS, LANES), 0, counts[0, 0])
        carries[...] = jnp.zeros_like(carries)
        total[...] = states[0:2]
        start(0)

    for j in range(1, rounds):
        @pl.when(step == (j * shards) // rounds)
        def _(j=j):
            finish(j - 1)
            start(j)

    makers = [
        local_group(k, m_ref, d_ref, param, masks, yf, yb, res_out, seen_out)
        for k in range(groups)
    ]
    staggered(makers, 6, 1)

    @pl.when(step == shards - 1)
    def _():
        finish(rounds - 1)


def final_kernel(
    groups, shards, counts, fq, fk, fv, q_ref, k_ref, v_ref, m_ref, g_ref, yf, yb, param,
    carries, rates, seen, res_in, skips, out, dfeat, dparam,
    own, dshort, prods, dwin, sems,
):
    count = counts[0, 0]
    step = pl.program_id(0)
    capacity = fq.shape[0]
    chan = fq.shape[1]
    slot = lax.rem(step, 2)

    def writes(at, place):
        made = []
        for m in range(3):
            lanes = pl.ds(pl.multiple_of((m * shards + at) * chan, LANES), chan)
            made.append(
                pltpu.make_async_copy(dwin.at[place, m], dfeat.at[:, lanes], sems.at[place, m])
            )
        return made

    @pl.when(step == 0)
    def _():
        own[...] = row_mask((ROWS, LANES), 0, count)
        dshort[:, ROWS:, :] = jnp.zeros((3, dshort.shape[1] - ROWS, LANES), F32)
        prods[...] = jnp.zeros_like(prods)

    @pl.when(step >= 2)
    def _():
        for copy in writes(step - 2, slot):
            copy.wait()

    dparam[GRAD_ROWS - 1 : GRAD_ROWS, :] = jnp.zeros((1, chan), F32)
    def group(k):
        lanes = slice(k * LANES, (k + 1) * LANES)
        res_row = param[0, RES_ROW : RES_ROW + 1, lanes]
        dec_row = param[0, DEC_ROW : DEC_ROW + 1, lanes]
        skip = param[0, SKIP_ROW : SKIP_ROW + 1, lanes]
        sub_f = iota((LANES, LANES), 0).astype(F32)
        out_t = (res_row * jnp.exp(-dec_row * (sub_f + 1.0))).astype(BF16)
        in_t = (res_row * jnp.exp(-dec_row * (BLK - 1.0 - sub_f))).astype(BF16)
        rate = rates[0, :, lanes]
        from_left = carries[0, :, lanes]
        from_right = carries[1, :, lanes]

        def pair(a, b):
            both = jnp.concatenate([a.astype(BF16), b.astype(BF16)], axis=1)
            return spread_rows(both)

        until = (count + (REACH + 1 - BLK)).astype(F32)
        y_left = jnp.dot(
            out_t, pair(from_left, from_left * jnp.exp(-rate * float(BLK))),
            preferred_element_type=F32,
        )
        y_right = jnp.dot(
            in_t,
            pair(from_right * jnp.exp(-rate * until), from_right * jnp.exp(-rate * (until - BLK))),
            preferred_element_type=F32,
        )
        for r in range(0, ROWS, CHUNK):
            rows = slice(r, r + CHUNK)
            at = slice(r % BLK, r % BLK + CHUNK)
            cols = slice((r // BLK) * LANES, (r // BLK + 1) * LANES)
            kept = min(r + CHUNK, capacity) - r
            query = q_ref[rows, lanes].astype(F32)
            grad = g_ref[rows, lanes].astype(F32)
            mixed = m_ref[rows, lanes].astype(F32)
            long_out = yf[rows, lanes] + y_left[at, cols] + skip * mixed
            gated = (query * long_out).astype(BF16) * own[rows]
            out[r : r + kept, lanes] = gated[0:kept]
            dshort[0, rows, :] = grad * long_out
            d_mixed = yb[rows, lanes] + y_right[at, cols] + skip * (grad * query)
            dshort[1, rows, :] = d_mixed * v_ref[rows, lanes].astype(F32)
            dshort[2, rows, :] = d_mixed * k_ref[rows, lanes].astype(F32)

        for m, feat in enumerate((fq, fk, fv)):
            for r in range(0, ROWS, CHUNK):
                kept = min(r + CHUNK, capacity) - r
                rows = slice(r, r + kept)
                keep = own[rows]
                window = feat[rows, lanes] * keep
                total = None
                for tap in range(TAPS):
                    weight = param[0, TAPS * m + tap : TAPS * m + tap + 1, lanes]
                    shifted = dshort[m, r + tap : r + tap + kept, :]
                    term = weight * shifted
                    total = term if total is None else total + term
                    prods[rows, tap * LANES : (tap + 1) * LANES] = shifted.astype(BF16) * window
                dwin[slot, m, rows, lanes] = total.astype(BF16) * keep
            sums = jnp.dot(jnp.ones((HALO, ROWS), BF16), prods[...], preferred_element_type=F32)
            for tap in range(TAPS):
                dparam[TAPS * m + tap : TAPS * m + tap + 1, lanes] = sums[
                    0:1, tap * LANES : (tap + 1) * LANES
                ]

        crossed = seen[:, lanes] * from_left
        high = crossed.astype(BF16)
        low = (crossed - high.astype(F32)).astype(BF16)
        gather = (iota((LANES, LANES), 0) // GROUP) == (iota((LANES, LANES), 1) // GROUP)
        gather = jnp.where(gather, 1.0, 0.0).astype(BF16)
        sums = jnp.dot(high, gather, preferred_element_type=F32)
        sums = sums + jnp.dot(low, gather, preferred_element_type=F32)
        mine = iota((POLES, LANES), 0) == iota((POLES, LANES), 1) % POLES
        row = jnp.sum(jnp.where(mine, sums, 0.0), axis=0, keepdims=True)
        dparam[RES_ROW : RES_ROW + 1, lanes] = res_in[0:1, lanes] + row
        dparam[SKIP_ROW : SKIP_ROW + 1, lanes] = skips[0:1, lanes]

    for k in range(groups):
        group(k)
    for copy in writes(step, slot):
        copy.start()

    @pl.when(step == shards - 1)
    def _():
        for copy in writes(step - 1, 1 - slot) + writes(step, slot):
            copy.wait()


def meet(peers):
    barrier = pltpu.get_barrier_semaphore()
    for peer in peers:
        pl.semaphore_signal(barrier, inc=1, device_id=peer, device_id_type=MESH)
    pl.semaphore_wait(barrier, len(peers))


def filter_lanes():
    return iota((PER, LANES), 1) // POLES == iota((PER, LANES), 0)


def pole_rows(square, table, chan):
    square[...] = jnp.zeros_like(square)
    square[0:POLES, 0 : chan // GROUP] = table
    turned = jnp.transpose(square[...])
    parts = []
    for g in range(chan // LANES):
        x = turned[g * PER : (g + 1) * PER]
        for gap in (POLES, 2 * POLES, 4 * POLES):
            x = x + pltpu.roll(x, gap, 1)
        parts.append(jnp.sum(jnp.where(filter_lanes(), x, 0.0), axis=0, keepdims=True))
    return jnp.concatenate(parts, axis=1)


def pole_table(square, row, chan):
    square[...] = jnp.zeros_like(square)
    for g in range(chan // LANES):
        x = jnp.broadcast_to(row[:, g * LANES : (g + 1) * LANES], (PER, LANES))
        x = jnp.where(filter_lanes(), x, 0.0)
        for gap in (POLES, 2 * POLES, 4 * POLES):
            x = x + pltpu.roll(x, gap, 1)
        square[g * PER : (g + 1) * PER, :] = x
    return jnp.transpose(square[...])[0:POLES, 0 : chan // GROUP]


def reduce_kernel(
    shards, replicas, part, out, packed, by_ctx, by_dp, send, recv, send_dp, recv_dp,
):
    dp, me = lax.axis_index("dp"), lax.axis_index("ctx")
    chan = out.shape[1]
    half = chan // 2
    peers = [(dp, lax.rem(me + d, shards)) for d in range(1, shards)]
    others = [(lax.rem(dp + d, replicas), me) for d in range(1, replicas)]

    def block(at):
        lanes = pl.ds(pl.multiple_of(at * chan, LANES), chan)
        return part[:, lanes]

    meet(peers + others)
    copies = []
    for n, peer in enumerate(peers):
        mine = block(peer[1])
        packed[n, :, 0:chan] = mine[0:POLES].astype(BF16)
        packed[n, :, chan:] = jnp.concatenate(
            [mine[POLES:, 0:half], mine[POLES:, half:]], axis=0
        ).astype(BF16)
        copies.append(
            pltpu.make_async_remote_copy(
                src_ref=packed.at[n], dst_ref=by_ctx.at[n], send_sem=send.at[n],
                recv_sem=recv.at[n], device_id=peer, device_id_type=MESH,
            )
        )
        copies[-1].start()
    total = block(me)
    top, rest = total[0:POLES], total[POLES:]
    rest = jnp.concatenate([rest[:, 0:half], rest[:, half:]], axis=0)
    for n, copy in enumerate(copies):
        copy.wait()
        top = top + by_ctx[n, :, 0:chan].astype(F32)
        rest = rest + by_ctx[n, :, chan:].astype(F32)
    by_dp[dp, :, 0:chan] = top
    by_dp[dp, :, chan:] = rest
    copies = []
    for n, peer in enumerate(others):
        copies.append(
            pltpu.make_async_remote_copy(
                src_ref=by_dp.at[dp], dst_ref=by_dp.at[dp], send_sem=send_dp.at[n],
                recv_sem=recv_dp.at[n], device_id=peer, device_id_type=MESH,
            )
        )
        copies[-1].start()
    for copy in copies:
        copy.wait()
    total = by_dp[0]
    for n in range(1, replicas):
        total = total + by_dp[n]
    rest = total[:, chan:]
    low = POLES // 2
    rest = jnp.concatenate([rest[0:low], rest[low:]], axis=1)
    out[...] = jnp.concatenate([total[:, 0:chan], rest], axis=0)


def finish_kernel(rows, taps, res, skip, square):
    chan = rows.shape[1]
    for m in range(3):
        taps[m] = rows[TAPS * m : TAPS * (m + 1), :]
    skip[...] = rows[SKIP_ROW : SKIP_ROW + 1, :]
    res[...] = pole_table(square, rows[RES_ROW : RES_ROW + 1, :], chan)


def remote(ident):
    return pltpu.CompilerParams(
        collective_id=ident, has_side_effects=True, vmem_limit_bytes=VMEM_LIMIT
    )


def per_device(features, counts, short_taps, residue, decay_rate, skip_gain, cotangent):
    shards = lax.axis_size("ctx")
    capacity = features.shape[2]
    width = cotangent.shape[3]
    chan = short_taps.shape[2]
    groups = chan // LANES
    feats = features[0, 0]
    cot = cotangent[0, 0]
    count = counts[0, 0]

    tail = lax.dynamic_slice(feats, (count - HALO, 0), (HALO, 3 * width))
    anywhere = pl.BlockSpec(memory_space=pl.ANY)
    vmem = pl.BlockSpec(memory_space=pltpu.VMEM)
    smem = pl.BlockSpec(memory_space=pltpu.SMEM)
    rounds = (shards - 1).bit_length()

    def cols(rows, offset):
        return pl.BlockSpec((rows, chan), lambda g, *_: (0, offset * shards + g))

    def turn(g):
        return lax.rem(lax.axis_index("ctx") + g, shards)

    def turned(rows, offset):
        return pl.BlockSpec((rows, chan), lambda g: (0, offset * shards + turn(g)))

    def planes(lead, rows, first=0):
        return pl.BlockSpec((lead, rows, chan), lambda g, *_: (first, 0, g))

    def shape(*dims, dtype=F32):
        return jax.ShapeDtypeStruct(dims, dtype)

    plain = pltpu.CompilerParams(vmem_limit_bytes=VMEM_LIMIT)
    param_spec = pl.BlockSpec((1, FLAT_ROWS, chan), lambda g: (g, 0, 0))
    feat_specs = [cols(capacity, m) for m in range(3)]
    rows_spec = cols(ROWS, 0)
    rows_shape = shape(ROWS, width, dtype=BF16)
    query, key, value, mixed, grad, d_long, states, skips, flat = pl.pallas_call(
        functools.partial(front_kernel, groups, shards),
        grid=(shards,),
        in_specs=[smem] + [turned(capacity, m) for m in range(3)] + [turned(capacity, 0)]
        + [vmem] * 7,
        out_specs=[turned(ROWS, 0)] * 6
        + [pl.BlockSpec((3, POLES, chan), lambda g: (0, 0, turn(g))), turned(HALO, 0)]
        + [pl.BlockSpec((1, FLAT_ROWS, chan), lambda g: (turn(g), 0, 0))],
        out_shape=[rows_shape] * 6
        + [shape(3, POLES, width), shape(HALO, width), shape(shards, FLAT_ROWS, chan)],
        scratch_shapes=[
            pltpu.VMEM((4, HALO + ROWS, LANES), F32),
            pltpu.VMEM((4, 2 * ROWS + HALO, LANES), F32),
            pltpu.VMEM((3, ROWS, LANES), BF16),
            pltpu.VMEM((LOW_ROW, chan), F32),
            pltpu.VMEM((PARAM_ROWS, chan), BF16),
            pltpu.VMEM((LANES, LANES), F32),
            pltpu.VMEM((shards, PARAM_ROWS, chan), BF16),
            pltpu.VMEM((shards, HALO, 3 * chan), BF16),
            pltpu.VMEM((shards, HALO, 4 * chan), BF16),
            pltpu.VMEM((shards, HALO, 3 * chan), BF16),
            pltpu.VMEM((shards, HALO, 4 * chan), BF16),
            pltpu.SemaphoreType.DMA((3, shards)),
            pltpu.SemaphoreType.DMA((3, shards)),
        ],
        compiler_params=remote(0),
        name="front",
    )(
        counts, feats, feats, feats, cot, jnp.transpose(short_taps, (1, 0, 2)),
        skip_gain.reshape(1, chan), residue, decay_rate, tail, feats[0:HALO], cot[0:HALO],
    )

    whole = pl.BlockSpec((3, POLES, width), lambda g: (0, 0, 0))
    y_fwd, y_bwd, res_local, seen, carries = pl.pallas_call(
        functools.partial(local_kernel, groups, shards, rounds),
        grid=(shards,),
        in_specs=[smem, pl.BlockSpec((shards, FLAT_ROWS, chan), lambda g: (0, 0, 0)), rows_spec, rows_spec, param_spec, whole],
        out_specs=[rows_spec, rows_spec, cols(HALO, 0), cols(POLES, 0),
                   pl.BlockSpec((2, POLES, width), lambda g: (0, 0, 0))],
        out_shape=[shape(ROWS, width), shape(ROWS, width), shape(HALO, width),
                   shape(POLES, width), shape(2, POLES, width)],
        scratch_shapes=[
            pltpu.VMEM((ROWS, LANES), BF16),
            pltpu.VMEM((2, POLES, width), F32),
            pltpu.VMEM((rounds, 2, POLES, width), BF16),
            pltpu.VMEM((rounds, 2, POLES, width), BF16),
            pltpu.SemaphoreType.DMA((rounds, 2)),
            pltpu.SemaphoreType.DMA((rounds, 2)),
        ],
        compiler_params=remote(1),
        name="local",
    )(counts, flat, mixed, d_long, flat, states)

    out, dfeat, dparam = pl.pallas_call(
        functools.partial(final_kernel, groups, shards),
        grid=(shards,),
        in_specs=[smem] + feat_specs + [rows_spec] * 7
        + [param_spec, planes(2, POLES), planes(1, POLES, 2), cols(POLES, 0),
           cols(HALO, 0), cols(HALO, 0)],
        out_specs=[cols(capacity, 0), anywhere, cols(GRAD_ROWS, 0)],
        out_shape=[
            shape(capacity, width, dtype=BF16),
            shape(capacity, 3 * width, dtype=BF16),
            shape(GRAD_ROWS, width),
        ],
        scratch_shapes=[
            pltpu.VMEM((ROWS, LANES), BF16),
            pltpu.VMEM((3, ROWS + HALO, LANES), F32),
            pltpu.VMEM((ROWS, TAPS * LANES), BF16),
            pltpu.VMEM((2, 3, capacity, chan), BF16),
            pltpu.SemaphoreType.DMA((2, 3)),
        ],
        compiler_params=plain,
        name="final",
    )(counts, feats, feats, feats, query, key, value, mixed, grad, y_fwd, y_bwd, flat,
      carries, states, seen, res_local, skips)
    replicas = lax.axis_size("dp")
    rows = pl.pallas_call(
        functools.partial(reduce_kernel, shards, replicas),
        in_specs=[vmem],
        out_specs=vmem,
        out_shape=shape(GRAD_ROWS, chan),
        scratch_shapes=[
            pltpu.VMEM((shards - 1, POLES, chan + chan // 2), BF16),
            pltpu.VMEM((shards - 1, POLES, chan + chan // 2), BF16),
            pltpu.VMEM((replicas, POLES, chan + chan // 2), F32),
            pltpu.SemaphoreType.DMA((shards - 1,)),
            pltpu.SemaphoreType.DMA((shards - 1,)),
            pltpu.SemaphoreType.DMA((replicas - 1,)),
            pltpu.SemaphoreType.DMA((replicas - 1,)),
        ],
        compiler_params=remote(2),
        name="reduce",
    )(dparam)
    taps, res, skip = pl.pallas_call(
        finish_kernel,
        in_specs=[vmem],
        out_specs=[vmem] * 3,
        out_shape=[shape(3, TAPS, chan), shape(POLES, chan // GROUP), shape(1, chan)],
        scratch_shapes=[pltpu.VMEM((LANES, LANES), F32)],
        name="finish",
    )(rows)
    return (
        out[None, None],
        dfeat[None, None],
        jnp.transpose(taps, (1, 0, 2)),
        res,
        skip.reshape(chan),
    )


def solution(mesh):
    in_specs = (
        P("dp", "ctx", None, None),
        P("dp", "ctx"),
        P(None, None, "ctx"),
        P(None, "ctx"),
        P(None, "ctx"),
        P("ctx"),
        P("dp", "ctx", None, None),
    )
    out_specs = (
        P("dp", "ctx", None, None),
        P("dp", "ctx", None, None),
        P(None, None, "ctx"),
        P(None, "ctx"),
        P("ctx"),
    )
    return jax.shard_map(
        per_device, mesh=mesh, in_specs=in_specs, out_specs=out_specs, check_vma=False
    )
```

```python
import functools

import jax
import jax.numpy as jnp
from jax import lax
from jax.experimental import pallas as pl
from jax.experimental.pallas import tpu as pltpu
from jax.sharding import PartitionSpec as P

TAPS = 7
HALO = 8
REACH = TAPS - 1
ROWS = 256
BLK = 128
POLES = 16
GROUP = 16
LANES = 128
PER = LANES // GROUP
F32 = jnp.float32
BF16 = jnp.bfloat16
SKIP_ROW = 3 * TAPS
RES_ROW = SKIP_ROW + 1
DEC_ROW = SKIP_ROW + 2
LOW_ROW = SKIP_ROW + 3
CNT_ROW = LOW_ROW + SKIP_ROW
PARAM_ROWS = 2 * LOW_ROW
GRAD_ROWS = 24
FLAT_ROWS = 32
CHUNK = 64
AHEAD = 2
VMEM_LIMIT = 56 << 20
MESH = pl.DeviceIdType.MESH


def iota(shape, axis):
    return lax.broadcasted_iota(jnp.int32, shape, axis)


def same_filter():
    return (iota((LANES, LANES), 0) // POLES) == (iota((LANES, LANES), 1) // GROUP)


def lane_filter(shape):
    return (iota(shape, 1) % LANES) // GROUP


def column_of(row):
    return jnp.transpose(jnp.broadcast_to(row, (LANES, LANES)))


def pick(full):
    fil = lane_filter((POLES, LANES))
    out = full[0:POLES]
    for f in range(1, PER):
        out = jnp.where(fil == f, full[f * POLES : (f + 1) * POLES], out)
    return out


def spread_rows(x):
    fil = lane_filter(x.shape)
    zero = jnp.zeros_like(x)
    return jnp.concatenate([jnp.where(fil == f, x, zero) for f in range(PER)], axis=0)


def side(x):
    return jnp.concatenate([x[0:BLK], x[BLK:ROWS]], axis=1)


def group_lanes(k):
    return pl.ds(pl.multiple_of(k * LANES, LANES), LANES)


def row_mask(shape, low, high):
    row = iota(shape, 0)
    keep = jnp.logical_and(row >= low, row < high)
    return jnp.where(keep, 1.0, 0.0).astype(BF16)


def fill(scratch, rows_bf, left, right, shift, count, own):
    capacity = rows_bf.shape[0]
    if left is not None:
        scratch[0:HALO, :] = left.astype(F32)
    shift[ROWS : ROWS + HALO, :] = right.astype(F32)
    after = shift[pl.ds(ROWS - count, ROWS), :]
    scratch[HALO : HALO + capacity, :] = (rows_bf * own).astype(F32) + after[0:capacity]
    scratch[HALO + capacity : HALO + ROWS, :] = after[capacity:ROWS]


def front_kernel(
    groups, shards, counts, fq, fk, fv, cot, taps, skip, res, dec_in, last, first, first_cot,
    q_out, k_out, v_out, m_out, g_out, d_out, states, skips, flat,
    win, shift, masks, param, packed, square, sent, tail, head, tail_in, head_in, send, recv,
):
    count = counts[0, 0]
    step = pl.program_id(0)
    capacity = cot.shape[0]
    chan = skip.shape[1]
    dp, me = lax.axis_index("dp"), lax.axis_index("ctx")
    right = (dp, lax.rem(me + 1, shards))
    left = (dp, lax.rem(me + shards - 1, shards))
    block = lax.rem(me + step, shards)

    def copy(kind, at, src, dst, peer):
        return pltpu.make_async_remote_copy(
            src_ref=src, dst_ref=dst, send_sem=send.at[kind, at], recv_sem=recv.at[kind, at],
            device_id=peer, device_id_type=MESH,
        )

    def tail_copy(at):
        theirs = lax.rem(me + 1 + at, shards)
        return copy(0, at, tail.at[theirs], tail_in.at[theirs], right)

    def head_copy(at):
        theirs = lax.rem(me + shards - 1 + at, shards)
        return copy(1, at, head.at[theirs], head_in.at[theirs], left)

    def param_copy(at):
        return copy(2, at, packed, sent.at[me], (dp, lax.rem(me + shards - at, shards)))

    def top(rows, lanes):
        return rows[:, lanes].astype(F32)[0:HALO].astype(BF16)

    def halos(at):
        @pl.when(me < shards - 1)
        def _():
            tail_copy(at).start()

        @pl.when(me > 0)
        def _():
            head_copy(at).start()

    @pl.when(step == 0)
    def _():
        for at in range(shards):
            for m in range(4):
                into = slice(m * chan, (m + 1) * chan)
                lanes = slice((m * shards + at) * chan, (m * shards + at + 1) * chan)
                if m < 3:
                    tail[at, :, into] = last[:, lanes]
                    head[at, :, into] = top(first, lanes)
                else:
                    head[at, :, into] = top(first_cot, slice(at * chan, (at + 1) * chan))
        meet([(dp, lax.rem(me + d, shards)) for d in range(1, shards)])
        halos(0)
        for m in range(3):
            param[TAPS * m : TAPS * (m + 1), :] = taps[m]
        tables = (skip[...], pole_rows(square, res[...], chan), pole_rows(square, dec_in[...], chan))
        for n, row in enumerate(tables):
            param[SKIP_ROW + n : SKIP_ROW + n + 1, :] = row
        high = param[...].astype(BF16)
        low = param[...] - high.astype(F32)
        low = jnp.where(iota(low.shape, 0) == SKIP_ROW, count.astype(F32), low)
        both = jnp.concatenate([high.astype(F32), low], axis=0).astype(BF16)
        packed[...] = both
        sent[me] = both
        for at in range(1, min(AHEAD + 1, shards)):
            param_copy(at).start()
            halos(at)

        @pl.when(me == 0)
        def _():
            tail_in[...] = jnp.zeros_like(tail_in)

        @pl.when(me == shards - 1)
        def _():
            head_in[...] = jnp.zeros_like(head_in)

        masks[0] = row_mask((ROWS, LANES), 0, count)
        masks[1] = row_mask((ROWS, LANES), 0, count + REACH)
        masks[2] = row_mask((ROWS, LANES), REACH, count + REACH)
        shift[...] = jnp.zeros_like(shift)

    @pl.when(jnp.logical_and(step > 0, step + AHEAD < shards))
    def _():
        param_copy(step + AHEAD).start()
        halos(step + AHEAD)

    @pl.when(step > 0)
    def _():
        param_copy(step).wait_recv()

    @pl.when(me > 0)
    def _():
        tail_copy(step).wait_recv()

    @pl.when(me < shards - 1)
    def _():
        head_copy(step).wait_recv()

    both = sent[block].astype(F32)
    low = both[LOW_ROW:]
    known = both[0:LOW_ROW] + jnp.where(iota(low.shape, 0) == SKIP_ROW, 0.0, low)
    param[...] = known
    flat[0, 0:LOW_ROW, :] = known
    flat[0, LOW_ROW:, :] = jnp.broadcast_to(
        both[CNT_ROW : CNT_ROW + 1], (FLAT_ROWS - LOW_ROW, chan)
    )

    def group(k):
        lanes = slice(k * LANES, (k + 1) * LANES)
        own = masks[0, 0:capacity]

        def near(ref, m):
            at = m * chan + k * LANES
            return ref[block, :, at : at + LANES]

        for m, rows in enumerate((fq, fk, fv)):
            fill(
                win.at[m], rows[:, lanes], near(tail_in, m), near(head_in, m), shift.at[m],
                count, own,
            )
        fill(win.at[3], cot[:, lanes], None, near(head_in, 3), shift.at[3], count, own)
        for r in range(0, ROWS, CHUNK):
            rows = slice(r, r + CHUNK)
            keep = masks[1, rows]
            shorts = []
            for m in range(3):
                total = param[TAPS * m : TAPS * m + 1, lanes] * win[m, HALO + r : HALO + r + CHUNK, :]
                for tap in range(1, TAPS):
                    weight = param[TAPS * m + tap : TAPS * m + tap + 1, lanes]
                    at = HALO + r - tap
                    total = total + weight * win[m, at : at + CHUNK, :]
                shorts.append(total.astype(BF16) * keep)
            query, key, value = shorts
            grad = win[3, HALO + r : HALO + r + CHUNK, :].astype(BF16) * keep
            q_out[rows, lanes] = query
            k_out[rows, lanes] = key
            v_out[rows, lanes] = value
            m_out[rows, lanes] = key * value
            g_out[rows, lanes] = grad
            d_out[rows, lanes] = grad * query

        dec = column_of(param[DEC_ROW : DEC_ROW + 1, lanes])
        lane_f = iota((LANES, LANES), 1).astype(F32)
        tab_l = jnp.exp(-dec * lane_f).astype(BF16)
        tab_r = jnp.exp(-dec * (BLK - 1.0 - lane_f)).astype(BF16)
        d_long = d_out[:, lanes]
        m_own = m_out[:, lanes] * masks[0]
        fwd = jnp.dot(tab_r, side(m_own), preferred_element_type=F32)
        bwd = jnp.dot(tab_l, side(d_long * masks[2]), preferred_element_type=F32)
        rate = pick(dec)
        first = (count - BLK).astype(F32)
        states[0, :, lanes] = jnp.exp(-rate * first) * pick(fwd[:, 0:LANES]) + jnp.exp(
            -rate * (first - BLK)
        ) * pick(fwd[:, LANES:])
        states[1, :, lanes] = jnp.exp(rate * REACH) * pick(bwd[:, 0:LANES]) + jnp.exp(
            -rate * (BLK - REACH)
        ) * pick(bwd[:, LANES:])
        states[2, :, lanes] = rate
        skips[:, lanes] = jnp.dot(
            jnp.ones((HALO, ROWS), BF16), d_long * m_own, preferred_element_type=F32
        )

    for k in range(groups):
        group(k)

    @pl.when(step == shards - 1)
    def _():
        for at in range(shards):
            @pl.when(me < shards - 1)
            def _(at=at):
                tail_copy(at).wait_send()

            @pl.when(me > 0)
            def _(at=at):
                head_copy(at).wait_send()

            if at > 0:
                param_copy(at).wait_send()


def local_group(k, m_ref, d_ref, param, masks, yf, yb, res_out, seen_out):
    lanes = slice(k * LANES, (k + 1) * LANES)
    mixed = m_ref[:, lanes]
    d_long = d_ref[:, lanes]
    res_row = param[0, RES_ROW : RES_ROW + 1, lanes]
    dec_row = param[0, DEC_ROW : DEC_ROW + 1, lanes]
    res = column_of(res_row)
    dec = column_of(dec_row)
    lane_f = iota((LANES, LANES), 1).astype(F32)
    sub_f = iota((LANES, LANES), 0).astype(F32)
    tab_l = jnp.exp(-dec * lane_f)
    tab_r = jnp.exp(-dec * (BLK - 1.0 - lane_f))
    k_lag = jnp.sum((res * tab_l).reshape(PER, POLES, LANES), axis=1)
    k_rest = jnp.sum((res * tab_r).reshape(PER, POLES, LANES), axis=1)
    k_turn = pltpu.roll(k_rest, 1, 1)
    lower = iota((BLK, BLK), 0) >= iota((BLK, BLK), 1)
    upper = iota((BLK, BLK), 0) <= iota((BLK, BLK), 1)

    def toeplitz(rows, keep):
        parts = []
        for f in range(PER):
            wide = jnp.broadcast_to(rows[f : f + 1, :], (BLK, LANES))
            wide = pltpu.roll(wide, 0, 1, stride=1, stride_axis=0)
            parts.append(jnp.where(keep, wide, 0.0).astype(BF16))
        return jnp.concatenate(parts, axis=1)

    t_fwd = toeplitz(k_turn, lower)
    yield
    own_side = side(d_long * masks[...])
    mirror = iota((BLK, BLK), 0) + iota((BLK, BLK), 1)
    flip = jnp.where(mirror == BLK - 1, 1.0, 0.0).astype(BF16)
    own_flip = jnp.dot(flip, own_side, preferred_element_type=F32).astype(BF16)
    m_stack = spread_rows(side(mixed))
    pair = lax.dot_general(
        own_flip, m_stack, (((1,), (1,)), ((), ())), preferred_element_type=F32
    )
    yield
    same = same_filter()
    tab_lb = tab_l.astype(BF16)
    s_first = jnp.dot(tab_r.astype(BF16), mixed[0:BLK], preferred_element_type=F32)
    s_first = jnp.where(same, s_first, 0.0)
    e_second = jnp.dot(tab_lb, d_long[BLK:ROWS], preferred_element_type=F32)
    e_second = jnp.where(same, e_second, 0.0).astype(BF16)
    seen = jnp.dot(tab_lb, own_side, preferred_element_type=F32)
    out_t = (res_row * jnp.exp(-dec_row * (sub_f + 1.0))).astype(BF16)
    in_t = (res_row * jnp.exp(-dec_row * (BLK - sub_f))).astype(BF16)
    y_next = jnp.dot(out_t, s_first.astype(BF16), preferred_element_type=F32)
    y_near = jnp.dot(in_t, e_second, preferred_element_type=F32)
    yield
    y_fwd = jnp.dot(t_fwd, m_stack, preferred_element_type=F32)
    yf[0:BLK, lanes] = y_fwd[:, 0:LANES]
    yf[BLK:ROWS, lanes] = y_fwd[:, LANES:] + y_next
    t_bwd = toeplitz(k_lag, upper)
    yield
    d_stack = spread_rows(side(d_long))
    y_bwd = jnp.dot(t_bwd, d_stack, preferred_element_type=F32)
    yb[0:BLK, lanes] = y_bwd[:, 0:LANES] + y_near
    yb[BLK:ROWS, lanes] = y_bwd[:, LANES:]

    yield
    lag_rows = []
    for f in range(PER):
        piece = jnp.where(mirror < BLK, pair[:, f * LANES : (f + 1) * LANES], 0.0)
        piece = pltpu.roll(piece, 0, 1, stride=1, stride_axis=0)
        lag_rows.append(jnp.broadcast_to(jnp.sum(piece, axis=0, keepdims=True), (POLES, LANES)))
    lag_sums = jnp.concatenate(lag_rows, axis=0)
    res_grad = lag_sums * tab_r + jnp.exp(-dec) * seen[:, LANES:] * s_first
    row = jnp.sum(jnp.transpose(res_grad), axis=0, keepdims=True)
    res_out[:, lanes] = jnp.broadcast_to(row, (HALO, LANES))
    rate = pick(dec)
    seen_out[:, lanes] = jnp.exp(-rate) * pick(seen[:, 0:LANES]) + jnp.exp(
        -rate * (BLK + 1.0)
    ) * pick(seen[:, LANES:])
    yield


def staggered(makers, stages, lag):
    for turn in range(stages + lag * (len(makers) - 1)):
        for k, maker in enumerate(makers):
            if 0 <= turn - lag * k < stages:
                next(maker)


def local_kernel(
    groups, shards, rounds, counts, every, m_ref, d_ref, param, states,
    yf, yb, res_out, seen_out, carries, masks, total, outbox, inbox, send, recv,
):
    step = pl.program_id(0)
    dp, me = lax.axis_index("dp"), lax.axis_index("ctx")
    chan = m_ref.shape[1]

    def peer(gap):
        return (dp, lax.rem(me + gap + shards, shards))

    def copy(j, way):
        gap = (1 << j) if way == 0 else -(1 << j)
        return pltpu.make_async_remote_copy(
            src_ref=outbox.at[j, way], dst_ref=inbox.at[j, way], send_sem=send.at[j, way],
            recv_sem=recv.at[j, way], device_id=peer(gap), device_id_type=MESH,
        )

    def sends(j, way):
        return me + (1 << j) < shards if way == 0 else me >= (1 << j)

    def start(j):
        for way in range(2):
            @pl.when(sends(j, way))
            def _(way=way):
                outbox[j, way] = total[way].astype(BF16)
                copy(j, way).start()

    def finish(j):
        for way in range(2):
            @pl.when(sends(j, 1 - way))
            def _(way=way):
                copy(j, way).wait_recv()

                gap = 1 << j
                low, high = (me - gap, me) if way == 0 else (me, me + gap)
                inner = jnp.zeros((1, chan), F32)
                for i in range(shards):
                    inside = (i > low) & (i < high)
                    inner = inner + jnp.where(inside, every[i, LOW_ROW : LOW_ROW + 1, :], 0.0)
                outer = inner + counts[0, 0].astype(F32)

                def piece(p, c):
                    lanes = pl.ds(pl.multiple_of(p * chan, LANES), chan)
                    rate = states[2, :, lanes]
                    there = inbox[j, way, :, lanes].astype(F32)
                    near = jnp.exp(-rate * inner) * there
                    carries[way, :, lanes] = carries[way, :, lanes] + near
                    if j < rounds - 1:
                        far = jnp.exp(-rate * outer) * there
                        total[way, :, lanes] = total[way, :, lanes] + far
                    return c

                lax.fori_loop(0, shards, piece, 0)

            @pl.when(sends(j, way))
            def _(way=way):
                copy(j, way).wait_send()

    @pl.when(step == 0)
    def _():
        barrier = pltpu.get_barrier_semaphore()
        greeted = 0
        for j in range(rounds):
            for way in range(2):
                there = sends(j, way)
                greeted = greeted + there.astype(jnp.int32)

                @pl.when(there)
                def _(j=j, way=way):
                    gap = (1 << j) if way == 0 else -(1 << j)
                    pl.semaphore_signal(
                        barrier, inc=1, device_id=peer(gap), device_id_type=MESH
                    )
        pl.semaphore_wait(barrier, greeted)
        masks[...] = row_mask((ROWS, LANES), 0, counts[0, 0])
        carries[...] = jnp.zeros_like(carries)
        total[...] = states[0:2]
        start(0)

    for j in range(1, rounds):
        @pl.when(step == (j * shards) // rounds)
        def _(j=j):
            finish(j - 1)
            start(j)

    makers = [
        local_group(k, m_ref, d_ref, param, masks, yf, yb, res_out, seen_out)
        for k in range(groups)
    ]
    staggered(makers, 6, 1)

    @pl.when(step == shards - 1)
    def _():
        finish(rounds - 1)


def final_kernel(
    groups, shards, counts, fq, fk, fv, q_ref, k_ref, v_ref, m_ref, g_ref, yf, yb, param,
    carries, rates, seen, res_in, skips, out, dfeat, dparam,
    own, dshort, prods, dwin, sems,
):
    count = counts[0, 0]
    step = pl.program_id(0)
    capacity = fq.shape[0]
    chan = fq.shape[1]
    slot = lax.rem(step, 2)

    def writes(at, place):
        made = []
        for m in range(3):
            lanes = pl.ds(pl.multiple_of((m * shards + at) * chan, LANES), chan)
            made.append(
                pltpu.make_async_copy(dwin.at[place, m], dfeat.at[:, lanes], sems.at[place, m])
            )
        return made

    @pl.when(step == 0)
    def _():
        own[...] = row_mask((ROWS, LANES), 0, count)
        dshort[:, ROWS:, :] = jnp.zeros((3, dshort.shape[1] - ROWS, LANES), F32)
        prods[...] = jnp.zeros_like(prods)

    @pl.when(step >= 2)
    def _():
        for copy in writes(step - 2, slot):
            copy.wait()

    dparam[GRAD_ROWS - 1 : GRAD_ROWS, :] = jnp.zeros((1, chan), F32)
    def group(k):
        lanes = slice(k * LANES, (k + 1) * LANES)
        res_row = param[0, RES_ROW : RES_ROW + 1, lanes]
        dec_row = param[0, DEC_ROW : DEC_ROW + 1, lanes]
        skip = param[0, SKIP_ROW : SKIP_ROW + 1, lanes]
        sub_f = iota((LANES, LANES), 0).astype(F32)
        out_t = (res_row * jnp.exp(-dec_row * (sub_f + 1.0))).astype(BF16)
        in_t = (res_row * jnp.exp(-dec_row * (BLK - 1.0 - sub_f))).astype(BF16)
        rate = rates[0, :, lanes]
        from_left = carries[0, :, lanes]
        from_right = carries[1, :, lanes]

        def pair(a, b):
            both = jnp.concatenate([a.astype(BF16), b.astype(BF16)], axis=1)
            return spread_rows(both)

        until = (count + (REACH + 1 - BLK)).astype(F32)
        y_left = jnp.dot(
            out_t, pair(from_left, from_left * jnp.exp(-rate * float(BLK))),
            preferred_element_type=F32,
        )
        y_right = jnp.dot(
            in_t,
            pair(from_right * jnp.exp(-rate * until), from_right * jnp.exp(-rate * (until - BLK))),
            preferred_element_type=F32,
        )
        crossed = seen[:, lanes] * from_left
        high = crossed.astype(BF16)
        low = (crossed - high.astype(F32)).astype(BF16)
        gather = (iota((LANES, LANES), 0) // GROUP) == (iota((LANES, LANES), 1) // GROUP)
        gather = jnp.where(gather, 1.0, 0.0).astype(BF16)
        sums = jnp.dot(high, gather, preferred_element_type=F32)
        sums = sums + jnp.dot(low, gather, preferred_element_type=F32)
        mine = iota((POLES, LANES), 0) == iota((POLES, LANES), 1) % POLES
        row = jnp.sum(jnp.where(mine, sums, 0.0), axis=0, keepdims=True)
        dparam[RES_ROW : RES_ROW + 1, lanes] = res_in[0:1, lanes] + row
        yield
        for r in range(0, ROWS, CHUNK):
            rows = slice(r, r + CHUNK)
            at = slice(r % BLK, r % BLK + CHUNK)
            cols = slice((r // BLK) * LANES, (r // BLK + 1) * LANES)
            kept = min(r + CHUNK, capacity) - r
            query = q_ref[rows, lanes].astype(F32)
            grad = g_ref[rows, lanes].astype(F32)
            mixed = m_ref[rows, lanes].astype(F32)
            long_out = yf[rows, lanes] + y_left[at, cols] + skip * mixed
            gated = (query * long_out).astype(BF16) * own[rows]
            out[r : r + kept, lanes] = gated[0:kept]
            dshort[0, rows, :] = grad * long_out
            d_mixed = yb[rows, lanes] + y_right[at, cols] + skip * (grad * query)
            dshort[1, rows, :] = d_mixed * v_ref[rows, lanes].astype(F32)
            dshort[2, rows, :] = d_mixed * k_ref[rows, lanes].astype(F32)

        yield
        for m, feat in enumerate((fq, fk, fv)):
            for r in range(0, ROWS, CHUNK):
                kept = min(r + CHUNK, capacity) - r
                rows = slice(r, r + kept)
                keep = own[rows]
                window = feat[rows, lanes] * keep
                total = None
                for tap in range(TAPS):
                    weight = param[0, TAPS * m + tap : TAPS * m + tap + 1, lanes]
                    shifted = dshort[m, r + tap : r + tap + kept, :]
                    term = weight * shifted
                    total = term if total is None else total + term
                    prods[rows, tap * LANES : (tap + 1) * LANES] = shifted.astype(BF16) * window
                dwin[slot, m, rows, lanes] = total.astype(BF16) * keep
            sums = jnp.dot(jnp.ones((HALO, ROWS), BF16), prods[...], preferred_element_type=F32)
            for tap in range(TAPS):
                dparam[TAPS * m + tap : TAPS * m + tap + 1, lanes] = sums[
                    0:1, tap * LANES : (tap + 1) * LANES
                ]

        dparam[SKIP_ROW : SKIP_ROW + 1, lanes] = skips[0:1, lanes]
        yield

    makers = [group(k) for k in range(groups)]
    next(makers[0])
    for k in range(groups):
        next(makers[k])
        if k + 1 < groups:
            next(makers[k + 1])
        next(makers[k])
    for copy in writes(step, slot):
        copy.start()

    @pl.when(step == shards - 1)
    def _():
        for copy in writes(step - 1, 1 - slot) + writes(step, slot):
            copy.wait()


def meet(peers):
    barrier = pltpu.get_barrier_semaphore()
    for peer in peers:
        pl.semaphore_signal(barrier, inc=1, device_id=peer, device_id_type=MESH)
    pl.semaphore_wait(barrier, len(peers))


def filter_lanes():
    return iota((PER, LANES), 1) // POLES == iota((PER, LANES), 0)


def pole_rows(square, table, chan):
    square[...] = jnp.zeros_like(square)
    square[0:POLES, 0 : chan // GROUP] = table
    turned = jnp.transpose(square[...])
    parts = []
    for g in range(chan // LANES):
        x = turned[g * PER : (g + 1) * PER]
        for gap in (POLES, 2 * POLES, 4 * POLES):
            x = x + pltpu.roll(x, gap, 1)
        parts.append(jnp.sum(jnp.where(filter_lanes(), x, 0.0), axis=0, keepdims=True))
    return jnp.concatenate(parts, axis=1)


def pole_table(square, row, chan):
    square[...] = jnp.zeros_like(square)
    for g in range(chan // LANES):
        x = jnp.broadcast_to(row[:, g * LANES : (g + 1) * LANES], (PER, LANES))
        x = jnp.where(filter_lanes(), x, 0.0)
        for gap in (POLES, 2 * POLES, 4 * POLES):
            x = x + pltpu.roll(x, gap, 1)
        square[g * PER : (g + 1) * PER, :] = x
    return jnp.transpose(square[...])[0:POLES, 0 : chan // GROUP]


def reduce_kernel(
    shards, replicas, part, out, packed, by_ctx, by_dp, send, recv, send_dp, recv_dp,
):
    dp, me = lax.axis_index("dp"), lax.axis_index("ctx")
    chan = out.shape[1]
    half = chan // 2
    peers = [(dp, lax.rem(me + d, shards)) for d in range(1, shards)]
    others = [(lax.rem(dp + d, replicas), me) for d in range(1, replicas)]

    def block(at):
        lanes = pl.ds(pl.multiple_of(at * chan, LANES), chan)
        return part[:, lanes]

    meet(peers + others)
    copies = []
    for n, peer in enumerate(peers):
        mine = block(peer[1])
        packed[n, :, 0:chan] = mine[0:POLES].astype(BF16)
        packed[n, :, chan:] = jnp.concatenate(
            [mine[POLES:, 0:half], mine[POLES:, half:]], axis=0
        ).astype(BF16)
        copies.append(
            pltpu.make_async_remote_copy(
                src_ref=packed.at[n], dst_ref=by_ctx.at[n], send_sem=send.at[n],
                recv_sem=recv.at[n], device_id=peer, device_id_type=MESH,
            )
        )
        copies[-1].start()
    total = block(me)
    top, rest = total[0:POLES], total[POLES:]
    rest = jnp.concatenate([rest[:, 0:half], rest[:, half:]], axis=0)
    for n, copy in enumerate(copies):
        copy.wait()
        top = top + by_ctx[n, :, 0:chan].astype(F32)
        rest = rest + by_ctx[n, :, chan:].astype(F32)
    by_dp[dp, :, 0:chan] = top
    by_dp[dp, :, chan:] = rest
    copies = []
    for n, peer in enumerate(others):
        copies.append(
            pltpu.make_async_remote_copy(
                src_ref=by_dp.at[dp], dst_ref=by_dp.at[dp], send_sem=send_dp.at[n],
                recv_sem=recv_dp.at[n], device_id=peer, device_id_type=MESH,
            )
        )
        copies[-1].start()
    for copy in copies:
        copy.wait()
    total = by_dp[0]
    for n in range(1, replicas):
        total = total + by_dp[n]
    rest = total[:, chan:]
    low = POLES // 2
    rest = jnp.concatenate([rest[0:low], rest[low:]], axis=1)
    out[...] = jnp.concatenate([total[:, 0:chan], rest], axis=0)


def finish_kernel(rows, taps, res, skip, square):
    chan = rows.shape[1]
    for m in range(3):
        taps[m] = rows[TAPS * m : TAPS * (m + 1), :]
    skip[...] = rows[SKIP_ROW : SKIP_ROW + 1, :]
    res[...] = pole_table(square, rows[RES_ROW : RES_ROW + 1, :], chan)


def remote(ident):
    return pltpu.CompilerParams(
        collective_id=ident, has_side_effects=True, vmem_limit_bytes=VMEM_LIMIT
    )


def per_device(features, counts, short_taps, residue, decay_rate, skip_gain, cotangent):
    shards = lax.axis_size("ctx")
    capacity = features.shape[2]
    width = cotangent.shape[3]
    chan = short_taps.shape[2]
    groups = chan // LANES
    feats = features[0, 0]
    cot = cotangent[0, 0]
    count = counts[0, 0]

    tail = lax.dynamic_slice(feats, (count - HALO, 0), (HALO, 3 * width))
    anywhere = pl.BlockSpec(memory_space=pl.ANY)
    vmem = pl.BlockSpec(memory_space=pltpu.VMEM)
    smem = pl.BlockSpec(memory_space=pltpu.SMEM)
    rounds = (shards - 1).bit_length()

    def cols(rows, offset):
        return pl.BlockSpec((rows, chan), lambda g, *_: (0, offset * shards + g))

    def turn(g):
        return lax.rem(lax.axis_index("ctx") + g, shards)

    def turned(rows, offset):
        return pl.BlockSpec((rows, chan), lambda g: (0, offset * shards + turn(g)))

    def planes(lead, rows, first=0):
        return pl.BlockSpec((lead, rows, chan), lambda g, *_: (first, 0, g))

    def shape(*dims, dtype=F32):
        return jax.ShapeDtypeStruct(dims, dtype)

    plain = pltpu.CompilerParams(vmem_limit_bytes=VMEM_LIMIT)
    param_spec = pl.BlockSpec((1, FLAT_ROWS, chan), lambda g: (g, 0, 0))
    feat_specs = [cols(capacity, m) for m in range(3)]
    rows_spec = cols(ROWS, 0)
    rows_shape = shape(ROWS, width, dtype=BF16)
    query, key, value, mixed, grad, d_long, states, skips, flat = pl.pallas_call(
        functools.partial(front_kernel, groups, shards),
        grid=(shards,),
        in_specs=[smem] + [turned(capacity, m) for m in range(3)] + [turned(capacity, 0)]
        + [vmem] * 5
        + [pl.BlockSpec((2 * HALO, n * width), lambda g: (0, 0)) for n in (3, 1)],
        out_specs=[turned(ROWS, 0)] * 6
        + [pl.BlockSpec((3, POLES, chan), lambda g: (0, 0, turn(g))), turned(HALO, 0)]
        + [pl.BlockSpec((1, FLAT_ROWS, chan), lambda g: (turn(g), 0, 0))],
        out_shape=[rows_shape] * 6
        + [shape(3, POLES, width), shape(HALO, width), shape(shards, FLAT_ROWS, chan)],
        scratch_shapes=[
            pltpu.VMEM((4, HALO + ROWS, LANES), F32),
            pltpu.VMEM((4, 2 * ROWS + HALO, LANES), F32),
            pltpu.VMEM((3, ROWS, LANES), BF16),
            pltpu.VMEM((LOW_ROW, chan), F32),
            pltpu.VMEM((PARAM_ROWS, chan), BF16),
            pltpu.VMEM((LANES, LANES), F32),
            pltpu.VMEM((shards, PARAM_ROWS, chan), BF16),
            pltpu.VMEM((shards, HALO, 3 * chan), BF16),
            pltpu.VMEM((shards, HALO, 4 * chan), BF16),
            pltpu.VMEM((shards, HALO, 3 * chan), BF16),
            pltpu.VMEM((shards, HALO, 4 * chan), BF16),
            pltpu.SemaphoreType.DMA((3, shards)),
            pltpu.SemaphoreType.DMA((3, shards)),
        ],
        compiler_params=remote(0),
        name="front",
    )(
        counts, feats, feats, feats, cot, jnp.transpose(short_taps, (1, 0, 2)),
        skip_gain.reshape(1, chan), residue, decay_rate, tail, feats, cot,
    )

    whole = pl.BlockSpec((3, POLES, width), lambda g: (0, 0, 0))
    y_fwd, y_bwd, res_local, seen, carries = pl.pallas_call(
        functools.partial(local_kernel, groups, shards, rounds),
        grid=(shards,),
        in_specs=[smem, pl.BlockSpec((shards, FLAT_ROWS, chan), lambda g: (0, 0, 0)), rows_spec, rows_spec, param_spec, whole],
        out_specs=[rows_spec, rows_spec, cols(HALO, 0), cols(POLES, 0),
                   pl.BlockSpec((2, POLES, width), lambda g: (0, 0, 0))],
        out_shape=[shape(ROWS, width), shape(ROWS, width), shape(HALO, width),
                   shape(POLES, width), shape(2, POLES, width)],
        scratch_shapes=[
            pltpu.VMEM((ROWS, LANES), BF16),
            pltpu.VMEM((2, POLES, width), F32),
            pltpu.VMEM((rounds, 2, POLES, width), BF16),
            pltpu.VMEM((rounds, 2, POLES, width), BF16),
            pltpu.SemaphoreType.DMA((rounds, 2)),
            pltpu.SemaphoreType.DMA((rounds, 2)),
        ],
        compiler_params=remote(1),
        name="local",
    )(counts, flat, mixed, d_long, flat, states)

    out, dfeat, dparam = pl.pallas_call(
        functools.partial(final_kernel, groups, shards),
        grid=(shards,),
        in_specs=[smem] + feat_specs + [rows_spec] * 7
        + [param_spec, planes(2, POLES), planes(1, POLES, 2), cols(POLES, 0),
           cols(HALO, 0), cols(HALO, 0)],
        out_specs=[cols(capacity, 0), anywhere, cols(GRAD_ROWS, 0)],
        out_shape=[
            shape(capacity, width, dtype=BF16),
            shape(capacity, 3 * width, dtype=BF16),
            shape(GRAD_ROWS, width),
        ],
        scratch_shapes=[
            pltpu.VMEM((ROWS, LANES), BF16),
            pltpu.VMEM((3, ROWS + HALO, LANES), F32),
            pltpu.VMEM((ROWS, TAPS * LANES), BF16),
            pltpu.VMEM((2, 3, capacity, chan), BF16),
            pltpu.SemaphoreType.DMA((2, 3)),
        ],
        compiler_params=plain,
        name="final",
    )(counts, feats, feats, feats, query, key, value, mixed, grad, y_fwd, y_bwd, flat,
      carries, states, seen, res_local, skips)
    replicas = lax.axis_size("dp")
    rows = pl.pallas_call(
        functools.partial(reduce_kernel, shards, replicas),
        in_specs=[vmem],
        out_specs=vmem,
        out_shape=shape(GRAD_ROWS, chan),
        scratch_shapes=[
            pltpu.VMEM((shards - 1, POLES, chan + chan // 2), BF16),
            pltpu.VMEM((shards - 1, POLES, chan + chan // 2), BF16),
            pltpu.VMEM((replicas, POLES, chan + chan // 2), F32),
            pltpu.SemaphoreType.DMA((shards - 1,)),
            pltpu.SemaphoreType.DMA((shards - 1,)),
            pltpu.SemaphoreType.DMA((replicas - 1,)),
            pltpu.SemaphoreType.DMA((replicas - 1,)),
        ],
        compiler_params=remote(2),
        name="reduce",
    )(dparam)
    taps, res, skip = pl.pallas_call(
        finish_kernel,
        in_specs=[vmem],
        out_specs=[vmem] * 3,
        out_shape=[shape(3, TAPS, chan), shape(POLES, chan // GROUP), shape(1, chan)],
        scratch_shapes=[pltpu.VMEM((LANES, LANES), F32)],
        name="finish",
    )(rows)
    return (
        out[None, None],
        dfeat[None, None],
        jnp.transpose(taps, (1, 0, 2)),
        res,
        skip.reshape(chan),
    )


def solution(mesh):
    in_specs = (
        P("dp", "ctx", None, None),
        P("dp", "ctx"),
        P(None, None, "ctx"),
        P(None, "ctx"),
        P(None, "ctx"),
        P("ctx"),
        P("dp", "ctx", None, None),
    )
    out_specs = (
        P("dp", "ctx", None, None),
        P("dp", "ctx", None, None),
        P(None, None, "ctx"),
        P(None, "ctx"),
        P("ctx"),
    )
    return jax.shard_map(
        per_device, mesh=mesh, in_specs=in_specs, out_specs=out_specs, check_vma=False
    )
```

```python
import functools

import jax
import jax.numpy as jnp
from jax import lax
from jax.experimental import pallas as pl
from jax.experimental.pallas import tpu as pltpu
from jax.sharding import PartitionSpec as P

TAPS = 7
HALO = 8
REACH = TAPS - 1
ROWS = 256
BLK = 128
POLES = 16
GROUP = 16
LANES = 128
PER = LANES // GROUP
F32 = jnp.float32
BF16 = jnp.bfloat16
SKIP_ROW = 3 * TAPS
RES_ROW = SKIP_ROW + 1
DEC_ROW = SKIP_ROW + 2
LOW_ROW = SKIP_ROW + 3
CNT_ROW = LOW_ROW + SKIP_ROW
PARAM_ROWS = 2 * LOW_ROW
GRAD_ROWS = 24
FLAT_ROWS = 32
CHUNK = 64
AHEAD = 2
VMEM_LIMIT = 56 << 20
MESH = pl.DeviceIdType.MESH


def iota(shape, axis):
    return lax.broadcasted_iota(jnp.int32, shape, axis)


def same_filter():
    return (iota((LANES, LANES), 0) // POLES) == (iota((LANES, LANES), 1) // GROUP)


def lane_filter(shape):
    return (iota(shape, 1) % LANES) // GROUP


def column_of(row):
    return jnp.transpose(jnp.broadcast_to(row, (LANES, LANES)))


def pick(full):
    fil = lane_filter((POLES, LANES))
    out = full[0:POLES]
    for f in range(1, PER):
        out = jnp.where(fil == f, full[f * POLES : (f + 1) * POLES], out)
    return out


def spread_rows(x):
    fil = lane_filter(x.shape)
    zero = jnp.zeros_like(x)
    return jnp.concatenate([jnp.where(fil == f, x, zero) for f in range(PER)], axis=0)


def side(x):
    return jnp.concatenate([x[0:BLK], x[BLK:ROWS]], axis=1)


def group_lanes(k):
    return pl.ds(pl.multiple_of(k * LANES, LANES), LANES)


def row_mask(shape, low, high):
    row = iota(shape, 0)
    keep = jnp.logical_and(row >= low, row < high)
    return jnp.where(keep, 1.0, 0.0).astype(BF16)


def fill(scratch, rows_bf, left, right, shift, count, own):
    capacity = rows_bf.shape[0]
    if left is not None:
        scratch[0:HALO, :] = left.astype(F32)
    shift[ROWS : ROWS + HALO, :] = right.astype(F32)
    after = shift[pl.ds(ROWS - count, ROWS), :]
    scratch[HALO : HALO + capacity, :] = (rows_bf * own).astype(F32) + after[0:capacity]
    scratch[HALO + capacity : HALO + ROWS, :] = after[capacity:ROWS]


def front_kernel(
    groups, shards, counts, fq, fk, fv, cot, taps, skip, res, dec_in, last, first, first_cot,
    q_out, k_out, v_out, m_out, g_out, d_out, states, skips, flat,
    win, shift, masks, param, packed, square, sent, tail, head, tail_in, head_in, send, recv,
):
    count = counts[0, 0]
    step = pl.program_id(0)
    capacity = cot.shape[0]
    chan = skip.shape[1]
    dp, me = lax.axis_index("dp"), lax.axis_index("ctx")
    right = (dp, lax.rem(me + 1, shards))
    left = (dp, lax.rem(me + shards - 1, shards))
    block = lax.rem(me + step, shards)

    def copy(kind, at, src, dst, peer):
        return pltpu.make_async_remote_copy(
            src_ref=src, dst_ref=dst, send_sem=send.at[kind, at], recv_sem=recv.at[kind, at],
            device_id=peer, device_id_type=MESH,
        )

    def tail_copy(at):
        theirs = lax.rem(me + 1 + at, shards)
        return copy(0, at, tail.at[theirs], tail_in.at[theirs], right)

    def head_copy(at):
        theirs = lax.rem(me + shards - 1 + at, shards)
        return copy(1, at, head.at[theirs], head_in.at[theirs], left)

    def param_copy(at):
        return copy(2, at, packed, sent.at[me], (dp, lax.rem(me + shards - at, shards)))

    def top(rows, lanes):
        return rows[:, lanes].astype(F32)[0:HALO].astype(BF16)

    def halos(at):
        @pl.when(me < shards - 1)
        def _():
            tail_copy(at).start()

        @pl.when(me > 0)
        def _():
            head_copy(at).start()

    @pl.when(step == 0)
    def _():
        greet([(dp, lax.rem(me + d, shards)) for d in range(1, shards)])
        for at in range(shards):
            for m in range(4):
                into = slice(m * chan, (m + 1) * chan)
                lanes = slice((m * shards + at) * chan, (m * shards + at + 1) * chan)
                if m < 3:
                    tail[at, :, into] = last[:, lanes]
                    head[at, :, into] = top(first, lanes)
                else:
                    head[at, :, into] = top(first_cot, slice(at * chan, (at + 1) * chan))
        for m in range(3):
            param[TAPS * m : TAPS * (m + 1), :] = taps[m]
        tables = (skip[...], pole_rows(square, res[...], chan), pole_rows(square, dec_in[...], chan))
        for n, row in enumerate(tables):
            param[SKIP_ROW + n : SKIP_ROW + n + 1, :] = row
        high = param[...].astype(BF16)
        low = param[...] - high.astype(F32)
        low = jnp.where(iota(low.shape, 0) == SKIP_ROW, count.astype(F32), low)
        both = jnp.concatenate([high.astype(F32), low], axis=0).astype(BF16)
        packed[...] = both
        sent[me] = both
        masks[0] = row_mask((ROWS, LANES), 0, count)
        masks[1] = row_mask((ROWS, LANES), 0, count + REACH)
        masks[2] = row_mask((ROWS, LANES), REACH, count + REACH)
        shift[...] = jnp.zeros_like(shift)
        gather(shards - 1)
        halos(0)
        for at in range(1, min(AHEAD + 1, shards)):
            param_copy(at).start()
            halos(at)

        @pl.when(me == 0)
        def _():
            tail_in[...] = jnp.zeros_like(tail_in)

        @pl.when(me == shards - 1)
        def _():
            head_in[...] = jnp.zeros_like(head_in)

    @pl.when(jnp.logical_and(step > 0, step + AHEAD < shards))
    def _():
        param_copy(step + AHEAD).start()
        halos(step + AHEAD)

    @pl.when(step > 0)
    def _():
        param_copy(step).wait_recv()

    @pl.when(me > 0)
    def _():
        tail_copy(step).wait_recv()

    @pl.when(me < shards - 1)
    def _():
        head_copy(step).wait_recv()

    both = sent[block].astype(F32)
    low = both[LOW_ROW:]
    known = both[0:LOW_ROW] + jnp.where(iota(low.shape, 0) == SKIP_ROW, 0.0, low)
    param[...] = known
    flat[0, 0:LOW_ROW, :] = known
    flat[0, LOW_ROW:, :] = jnp.broadcast_to(
        both[CNT_ROW : CNT_ROW + 1], (FLAT_ROWS - LOW_ROW, chan)
    )

    def group(k):
        lanes = slice(k * LANES, (k + 1) * LANES)
        own = masks[0, 0:capacity]

        def near(ref, m):
            at = m * chan + k * LANES
            return ref[block, :, at : at + LANES]

        for m, rows in enumerate((fq, fk, fv)):
            fill(
                win.at[m], rows[:, lanes], near(tail_in, m), near(head_in, m), shift.at[m],
                count, own,
            )
        fill(win.at[3], cot[:, lanes], None, near(head_in, 3), shift.at[3], count, own)
        for r in range(0, ROWS, CHUNK):
            rows = slice(r, r + CHUNK)
            keep = masks[1, rows]
            shorts = []
            for m in range(3):
                total = param[TAPS * m : TAPS * m + 1, lanes] * win[m, HALO + r : HALO + r + CHUNK, :]
                for tap in range(1, TAPS):
                    weight = param[TAPS * m + tap : TAPS * m + tap + 1, lanes]
                    at = HALO + r - tap
                    total = total + weight * win[m, at : at + CHUNK, :]
                shorts.append(total.astype(BF16) * keep)
            query, key, value = shorts
            grad = win[3, HALO + r : HALO + r + CHUNK, :].astype(BF16) * keep
            q_out[rows, lanes] = query
            k_out[rows, lanes] = key
            v_out[rows, lanes] = value
            m_out[rows, lanes] = key * value
            g_out[rows, lanes] = grad
            d_out[rows, lanes] = grad * query

        dec = column_of(param[DEC_ROW : DEC_ROW + 1, lanes])
        lane_f = iota((LANES, LANES), 1).astype(F32)
        tab_l = jnp.exp(-dec * lane_f).astype(BF16)
        tab_r = jnp.exp(-dec * (BLK - 1.0 - lane_f)).astype(BF16)
        d_long = d_out[:, lanes]
        m_own = m_out[:, lanes] * masks[0]
        fwd = jnp.dot(tab_r, side(m_own), preferred_element_type=F32)
        bwd = jnp.dot(tab_l, side(d_long * masks[2]), preferred_element_type=F32)
        rate = pick(dec)
        first = (count - BLK).astype(F32)
        states[0, :, lanes] = jnp.exp(-rate * first) * pick(fwd[:, 0:LANES]) + jnp.exp(
            -rate * (first - BLK)
        ) * pick(fwd[:, LANES:])
        states[1, :, lanes] = jnp.exp(rate * REACH) * pick(bwd[:, 0:LANES]) + jnp.exp(
            -rate * (BLK - REACH)
        ) * pick(bwd[:, LANES:])
        states[2, :, lanes] = rate
        skips[:, lanes] = jnp.dot(
            jnp.ones((HALO, ROWS), BF16), d_long * m_own, preferred_element_type=F32
        )

    for k in range(groups):
        group(k)

    @pl.when(step == shards - 1)
    def _():
        for at in range(shards):
            @pl.when(me < shards - 1)
            def _(at=at):
                tail_copy(at).wait_send()

            @pl.when(me > 0)
            def _(at=at):
                head_copy(at).wait_send()

            if at > 0:
                param_copy(at).wait_send()


def local_group(k, m_ref, d_ref, param, masks, yf, yb, res_out, seen_out):
    lanes = slice(k * LANES, (k + 1) * LANES)
    mixed = m_ref[:, lanes]
    d_long = d_ref[:, lanes]
    res_row = param[0, RES_ROW : RES_ROW + 1, lanes]
    dec_row = param[0, DEC_ROW : DEC_ROW + 1, lanes]
    res = column_of(res_row)
    dec = column_of(dec_row)
    lane_f = iota((LANES, LANES), 1).astype(F32)
    sub_f = iota((LANES, LANES), 0).astype(F32)
    tab_l = jnp.exp(-dec * lane_f)
    tab_r = jnp.exp(-dec * (BLK - 1.0 - lane_f))
    k_lag = jnp.sum((res * tab_l).reshape(PER, POLES, LANES), axis=1)
    k_rest = jnp.sum((res * tab_r).reshape(PER, POLES, LANES), axis=1)
    k_turn = pltpu.roll(k_rest, 1, 1)
    lower = iota((BLK, BLK), 0) >= iota((BLK, BLK), 1)
    upper = iota((BLK, BLK), 0) <= iota((BLK, BLK), 1)

    def toeplitz(rows, keep):
        parts = []
        for f in range(PER):
            wide = jnp.broadcast_to(rows[f : f + 1, :], (BLK, LANES))
            wide = pltpu.roll(wide, 0, 1, stride=1, stride_axis=0)
            parts.append(jnp.where(keep, wide, 0.0).astype(BF16))
        return jnp.concatenate(parts, axis=1)

    t_fwd = toeplitz(k_turn, lower)
    yield
    own_side = side(d_long * masks[...])
    mirror = iota((BLK, BLK), 0) + iota((BLK, BLK), 1)
    flip = jnp.where(mirror == BLK - 1, 1.0, 0.0).astype(BF16)
    own_flip = jnp.dot(flip, own_side, preferred_element_type=F32).astype(BF16)
    m_stack = spread_rows(side(mixed))
    pair = lax.dot_general(
        own_flip, m_stack, (((1,), (1,)), ((), ())), preferred_element_type=F32
    )
    yield
    same = same_filter()
    tab_lb = tab_l.astype(BF16)
    s_first = jnp.dot(tab_r.astype(BF16), mixed[0:BLK], preferred_element_type=F32)
    s_first = jnp.where(same, s_first, 0.0)
    e_second = jnp.dot(tab_lb, d_long[BLK:ROWS], preferred_element_type=F32)
    e_second = jnp.where(same, e_second, 0.0).astype(BF16)
    seen = jnp.dot(tab_lb, own_side, preferred_element_type=F32)
    out_t = (res_row * jnp.exp(-dec_row * (sub_f + 1.0))).astype(BF16)
    in_t = (res_row * jnp.exp(-dec_row * (BLK - sub_f))).astype(BF16)
    y_next = jnp.dot(out_t, s_first.astype(BF16), preferred_element_type=F32)
    y_near = jnp.dot(in_t, e_second, preferred_element_type=F32)
    yield
    y_fwd = jnp.dot(t_fwd, m_stack, preferred_element_type=F32)
    yf[0:BLK, lanes] = y_fwd[:, 0:LANES]
    yf[BLK:ROWS, lanes] = y_fwd[:, LANES:] + y_next
    t_bwd = toeplitz(k_lag, upper)
    yield
    d_stack = spread_rows(side(d_long))
    y_bwd = jnp.dot(t_bwd, d_stack, preferred_element_type=F32)
    yb[0:BLK, lanes] = y_bwd[:, 0:LANES] + y_near
    yb[BLK:ROWS, lanes] = y_bwd[:, LANES:]

    yield
    lag_rows = []
    for f in range(PER):
        piece = jnp.where(mirror < BLK, pair[:, f * LANES : (f + 1) * LANES], 0.0)
        piece = pltpu.roll(piece, 0, 1, stride=1, stride_axis=0)
        lag_rows.append(jnp.broadcast_to(jnp.sum(piece, axis=0, keepdims=True), (POLES, LANES)))
    lag_sums = jnp.concatenate(lag_rows, axis=0)
    res_grad = lag_sums * tab_r + jnp.exp(-dec) * seen[:, LANES:] * s_first
    row = jnp.sum(jnp.transpose(res_grad), axis=0, keepdims=True)
    res_out[:, lanes] = jnp.broadcast_to(row, (HALO, LANES))
    rate = pick(dec)
    seen_out[:, lanes] = jnp.exp(-rate) * pick(seen[:, 0:LANES]) + jnp.exp(
        -rate * (BLK + 1.0)
    ) * pick(seen[:, LANES:])
    yield


def staggered(makers, stages, lag):
    for turn in range(stages + lag * (len(makers) - 1)):
        for k, maker in enumerate(makers):
            if 0 <= turn - lag * k < stages:
                next(maker)


def local_kernel(
    groups, shards, rounds, counts, every, m_ref, d_ref, param, states,
    yf, yb, res_out, seen_out, carries, masks, total, outbox, inbox, send, recv,
):
    step = pl.program_id(0)
    dp, me = lax.axis_index("dp"), lax.axis_index("ctx")
    chan = m_ref.shape[1]

    def peer(gap):
        return (dp, lax.rem(me + gap + shards, shards))

    def copy(j, way):
        gap = (1 << j) if way == 0 else -(1 << j)
        return pltpu.make_async_remote_copy(
            src_ref=outbox.at[j, way], dst_ref=inbox.at[j, way], send_sem=send.at[j, way],
            recv_sem=recv.at[j, way], device_id=peer(gap), device_id_type=MESH,
        )

    def sends(j, way):
        return me + (1 << j) < shards if way == 0 else me >= (1 << j)

    def start(j):
        for way in range(2):
            @pl.when(sends(j, way))
            def _(way=way):
                outbox[j, way] = total[way].astype(BF16)
                copy(j, way).start()

    def finish(j):
        for way in range(2):
            @pl.when(sends(j, 1 - way))
            def _(way=way):
                copy(j, way).wait_recv()

                gap = 1 << j
                low, high = (me - gap, me) if way == 0 else (me, me + gap)
                inner = jnp.zeros((1, chan), F32)
                for i in range(shards):
                    inside = (i > low) & (i < high)
                    inner = inner + jnp.where(inside, every[i, LOW_ROW : LOW_ROW + 1, :], 0.0)
                outer = inner + counts[0, 0].astype(F32)

                def piece(p, c):
                    lanes = pl.ds(pl.multiple_of(p * chan, LANES), chan)
                    rate = states[2, :, lanes]
                    there = inbox[j, way, :, lanes].astype(F32)
                    near = jnp.exp(-rate * inner) * there
                    carries[way, :, lanes] = carries[way, :, lanes] + near
                    if j < rounds - 1:
                        far = jnp.exp(-rate * outer) * there
                        total[way, :, lanes] = total[way, :, lanes] + far
                    return c

                lax.fori_loop(0, shards, piece, 0)

            @pl.when(sends(j, way))
            def _(way=way):
                copy(j, way).wait_send()

    @pl.when(step == 0)
    def _():
        barrier = pltpu.get_barrier_semaphore()
        greeted = 0
        for j in range(rounds):
            for way in range(2):
                there = sends(j, way)
                greeted = greeted + there.astype(jnp.int32)

                @pl.when(there)
                def _(j=j, way=way):
                    gap = (1 << j) if way == 0 else -(1 << j)
                    pl.semaphore_signal(
                        barrier, inc=1, device_id=peer(gap), device_id_type=MESH
                    )
        masks[...] = row_mask((ROWS, LANES), 0, counts[0, 0])
        carries[...] = jnp.zeros_like(carries)
        total[...] = states[0:2]
        pl.semaphore_wait(barrier, greeted)
        start(0)

    for j in range(1, rounds):
        @pl.when(step == (j * shards) // rounds)
        def _(j=j):
            finish(j - 1)
            start(j)

    makers = [
        local_group(k, m_ref, d_ref, param, masks, yf, yb, res_out, seen_out)
        for k in range(groups)
    ]
    staggered(makers, 6, 1)

    @pl.when(step == shards - 1)
    def _():
        finish(rounds - 1)


def final_kernel(
    groups, shards, counts, fq, fk, fv, q_ref, k_ref, v_ref, m_ref, g_ref, yf, yb, param,
    carries, rates, seen, res_in, skips, out, dfeat, dparam,
    own, dshort, prods, dwin, sems,
):
    count = counts[0, 0]
    step = pl.program_id(0)
    capacity = fq.shape[0]
    chan = fq.shape[1]
    slot = lax.rem(step, 2)

    def writes(at, place):
        made = []
        for m in range(3):
            lanes = pl.ds(pl.multiple_of((m * shards + at) * chan, LANES), chan)
            made.append(
                pltpu.make_async_copy(dwin.at[place, m], dfeat.at[:, lanes], sems.at[place, m])
            )
        return made

    @pl.when(step == 0)
    def _():
        own[...] = row_mask((ROWS, LANES), 0, count)
        dshort[:, ROWS:, :] = jnp.zeros((3, dshort.shape[1] - ROWS, LANES), F32)
        prods[...] = jnp.zeros_like(prods)

    @pl.when(step >= 2)
    def _():
        for copy in writes(step - 2, slot):
            copy.wait()

    dparam[GRAD_ROWS - 1 : GRAD_ROWS, :] = jnp.zeros((1, chan), F32)
    def group(k):
        lanes = slice(k * LANES, (k + 1) * LANES)
        res_row = param[0, RES_ROW : RES_ROW + 1, lanes]
        dec_row = param[0, DEC_ROW : DEC_ROW + 1, lanes]
        skip = param[0, SKIP_ROW : SKIP_ROW + 1, lanes]
        sub_f = iota((LANES, LANES), 0).astype(F32)
        out_t = (res_row * jnp.exp(-dec_row * (sub_f + 1.0))).astype(BF16)
        in_t = (res_row * jnp.exp(-dec_row * (BLK - 1.0 - sub_f))).astype(BF16)
        rate = rates[0, :, lanes]
        from_left = carries[0, :, lanes]
        from_right = carries[1, :, lanes]

        def pair(a, b):
            both = jnp.concatenate([a.astype(BF16), b.astype(BF16)], axis=1)
            return spread_rows(both)

        until = (count + (REACH + 1 - BLK)).astype(F32)
        y_left = jnp.dot(
            out_t, pair(from_left, from_left * jnp.exp(-rate * float(BLK))),
            preferred_element_type=F32,
        )
        y_right = jnp.dot(
            in_t,
            pair(from_right * jnp.exp(-rate * until), from_right * jnp.exp(-rate * (until - BLK))),
            preferred_element_type=F32,
        )
        crossed = seen[:, lanes] * from_left
        high = crossed.astype(BF16)
        low = (crossed - high.astype(F32)).astype(BF16)
        gather = (iota((LANES, LANES), 0) // GROUP) == (iota((LANES, LANES), 1) // GROUP)
        gather = jnp.where(gather, 1.0, 0.0).astype(BF16)
        sums = jnp.dot(high, gather, preferred_element_type=F32)
        sums = sums + jnp.dot(low, gather, preferred_element_type=F32)
        mine = iota((POLES, LANES), 0) == iota((POLES, LANES), 1) % POLES
        row = jnp.sum(jnp.where(mine, sums, 0.0), axis=0, keepdims=True)
        dparam[RES_ROW : RES_ROW + 1, lanes] = res_in[0:1, lanes] + row
        yield
        for r in range(0, ROWS, CHUNK):
            rows = slice(r, r + CHUNK)
            at = slice(r % BLK, r % BLK + CHUNK)
            cols = slice((r // BLK) * LANES, (r // BLK + 1) * LANES)
            kept = min(r + CHUNK, capacity) - r
            query = q_ref[rows, lanes].astype(F32)
            grad = g_ref[rows, lanes].astype(F32)
            mixed = m_ref[rows, lanes].astype(F32)
            long_out = yf[rows, lanes] + y_left[at, cols] + skip * mixed
            gated = (query * long_out).astype(BF16) * own[rows]
            out[r : r + kept, lanes] = gated[0:kept]
            dshort[0, rows, :] = grad * long_out
            d_mixed = yb[rows, lanes] + y_right[at, cols] + skip * (grad * query)
            dshort[1, rows, :] = d_mixed * v_ref[rows, lanes].astype(F32)
            dshort[2, rows, :] = d_mixed * k_ref[rows, lanes].astype(F32)

        yield
        for m, feat in enumerate((fq, fk, fv)):
            for r in range(0, ROWS, CHUNK):
                kept = min(r + CHUNK, capacity) - r
                rows = slice(r, r + kept)
                keep = own[rows]
                window = feat[rows, lanes] * keep
                total = None
                for tap in range(TAPS):
                    weight = param[0, TAPS * m + tap : TAPS * m + tap + 1, lanes]
                    shifted = dshort[m, r + tap : r + tap + kept, :]
                    term = weight * shifted
                    total = term if total is None else total + term
                    prods[rows, tap * LANES : (tap + 1) * LANES] = shifted.astype(BF16) * window
                dwin[slot, m, rows, lanes] = total.astype(BF16) * keep
            sums = jnp.dot(jnp.ones((HALO, ROWS), BF16), prods[...], preferred_element_type=F32)
            for tap in range(TAPS):
                dparam[TAPS * m + tap : TAPS * m + tap + 1, lanes] = sums[
                    0:1, tap * LANES : (tap + 1) * LANES
                ]

        dparam[SKIP_ROW : SKIP_ROW + 1, lanes] = skips[0:1, lanes]
        yield

    makers = [group(k) for k in range(groups)]
    next(makers[0])
    for k in range(groups):
        next(makers[k])
        if k + 1 < groups:
            next(makers[k + 1])
        next(makers[k])
    for copy in writes(step, slot):
        copy.start()

    @pl.when(step == shards - 1)
    def _():
        for copy in writes(step - 1, 1 - slot) + writes(step, slot):
            copy.wait()


def greet(peers):
    barrier = pltpu.get_barrier_semaphore()
    for peer in peers:
        pl.semaphore_signal(barrier, inc=1, device_id=peer, device_id_type=MESH)


def gather(count):
    pl.semaphore_wait(pltpu.get_barrier_semaphore(), count)


def filter_lanes():
    return iota((PER, LANES), 1) // POLES == iota((PER, LANES), 0)


def pole_rows(square, table, chan):
    square[...] = jnp.zeros_like(square)
    square[0:POLES, 0 : chan // GROUP] = table
    turned = jnp.transpose(square[...])
    parts = []
    for g in range(chan // LANES):
        x = turned[g * PER : (g + 1) * PER]
        for gap in (POLES, 2 * POLES, 4 * POLES):
            x = x + pltpu.roll(x, gap, 1)
        parts.append(jnp.sum(jnp.where(filter_lanes(), x, 0.0), axis=0, keepdims=True))
    return jnp.concatenate(parts, axis=1)


def pole_table(square, row, chan):
    square[...] = jnp.zeros_like(square)
    for g in range(chan // LANES):
        x = jnp.broadcast_to(row[:, g * LANES : (g + 1) * LANES], (PER, LANES))
        x = jnp.where(filter_lanes(), x, 0.0)
        for gap in (POLES, 2 * POLES, 4 * POLES):
            x = x + pltpu.roll(x, gap, 1)
        square[g * PER : (g + 1) * PER, :] = x
    return jnp.transpose(square[...])[0:POLES, 0 : chan // GROUP]


def reduce_kernel(
    shards, replicas, part, out, packed, by_ctx, by_dp, send, recv, send_dp, recv_dp,
):
    dp, me = lax.axis_index("dp"), lax.axis_index("ctx")
    chan = out.shape[1]
    half = chan // 2
    peers = [(dp, lax.rem(me + d, shards)) for d in range(1, shards)]
    others = [(lax.rem(dp + d, replicas), me) for d in range(1, replicas)]

    def block(at):
        lanes = pl.ds(pl.multiple_of(at * chan, LANES), chan)
        return part[:, lanes]

    greet(peers + others)
    for n, peer in enumerate(peers):
        mine = block(peer[1])
        packed[n, :, 0:chan] = mine[0:POLES].astype(BF16)
        packed[n, :, chan:] = jnp.concatenate(
            [mine[POLES:, 0:half], mine[POLES:, half:]], axis=0
        ).astype(BF16)
    gather(len(peers + others))
    copies = []
    for n, peer in enumerate(peers):
        copies.append(
            pltpu.make_async_remote_copy(
                src_ref=packed.at[n], dst_ref=by_ctx.at[n], send_sem=send.at[n],
                recv_sem=recv.at[n], device_id=peer, device_id_type=MESH,
            )
        )
        copies[-1].start()
    total = block(me)
    top, rest = total[0:POLES], total[POLES:]
    rest = jnp.concatenate([rest[:, 0:half], rest[:, half:]], axis=0)
    for n, copy in enumerate(copies):
        copy.wait()
        top = top + by_ctx[n, :, 0:chan].astype(F32)
        rest = rest + by_ctx[n, :, chan:].astype(F32)
    by_dp[dp, :, 0:chan] = top
    by_dp[dp, :, chan:] = rest
    copies = []
    for n, peer in enumerate(others):
        copies.append(
            pltpu.make_async_remote_copy(
                src_ref=by_dp.at[dp], dst_ref=by_dp.at[dp], send_sem=send_dp.at[n],
                recv_sem=recv_dp.at[n], device_id=peer, device_id_type=MESH,
            )
        )
        copies[-1].start()
    for copy in copies:
        copy.wait()
    total = by_dp[0]
    for n in range(1, replicas):
        total = total + by_dp[n]
    rest = total[:, chan:]
    low = POLES // 2
    rest = jnp.concatenate([rest[0:low], rest[low:]], axis=1)
    out[...] = jnp.concatenate([total[:, 0:chan], rest], axis=0)


def finish_kernel(rows, taps, res, skip, square):
    chan = rows.shape[1]
    for m in range(3):
        taps[m] = rows[TAPS * m : TAPS * (m + 1), :]
    skip[...] = rows[SKIP_ROW : SKIP_ROW + 1, :]
    res[...] = pole_table(square, rows[RES_ROW : RES_ROW + 1, :], chan)


def remote(ident):
    return pltpu.CompilerParams(
        collective_id=ident, has_side_effects=True, vmem_limit_bytes=VMEM_LIMIT
    )


def per_device(features, counts, short_taps, residue, decay_rate, skip_gain, cotangent):
    shards = lax.axis_size("ctx")
    capacity = features.shape[2]
    width = cotangent.shape[3]
    chan = short_taps.shape[2]
    groups = chan // LANES
    feats = features[0, 0]
    cot = cotangent[0, 0]
    count = counts[0, 0]

    tail = lax.dynamic_slice(feats, (count - HALO, 0), (HALO, 3 * width))
    anywhere = pl.BlockSpec(memory_space=pl.ANY)
    vmem = pl.BlockSpec(memory_space=pltpu.VMEM)
    smem = pl.BlockSpec(memory_space=pltpu.SMEM)
    rounds = (shards - 1).bit_length()

    def cols(rows, offset):
        return pl.BlockSpec((rows, chan), lambda g, *_: (0, offset * shards + g))

    def turn(g):
        return lax.rem(lax.axis_index("ctx") + g, shards)

    def turned(rows, offset):
        return pl.BlockSpec((rows, chan), lambda g: (0, offset * shards + turn(g)))

    def planes(lead, rows, first=0):
        return pl.BlockSpec((lead, rows, chan), lambda g, *_: (first, 0, g))

    def shape(*dims, dtype=F32):
        return jax.ShapeDtypeStruct(dims, dtype)

    plain = pltpu.CompilerParams(vmem_limit_bytes=VMEM_LIMIT)
    param_spec = pl.BlockSpec((1, FLAT_ROWS, chan), lambda g: (g, 0, 0))
    feat_specs = [cols(capacity, m) for m in range(3)]
    rows_spec = cols(ROWS, 0)
    rows_shape = shape(ROWS, width, dtype=BF16)
    query, key, value, mixed, grad, d_long, states, skips, flat = pl.pallas_call(
        functools.partial(front_kernel, groups, shards),
        grid=(shards,),
        in_specs=[smem] + [turned(capacity, m) for m in range(3)] + [turned(capacity, 0)]
        + [vmem] * 5
        + [pl.BlockSpec((2 * HALO, n * width), lambda g: (0, 0)) for n in (3, 1)],
        out_specs=[turned(ROWS, 0)] * 6
        + [pl.BlockSpec((3, POLES, chan), lambda g: (0, 0, turn(g))), turned(HALO, 0)]
        + [pl.BlockSpec((1, FLAT_ROWS, chan), lambda g: (turn(g), 0, 0))],
        out_shape=[rows_shape] * 6
        + [shape(3, POLES, width), shape(HALO, width), shape(shards, FLAT_ROWS, chan)],
        scratch_shapes=[
            pltpu.VMEM((4, HALO + ROWS, LANES), F32),
            pltpu.VMEM((4, 2 * ROWS + HALO, LANES), F32),
            pltpu.VMEM((3, ROWS, LANES), BF16),
            pltpu.VMEM((LOW_ROW, chan), F32),
            pltpu.VMEM((PARAM_ROWS, chan), BF16),
            pltpu.VMEM((LANES, LANES), F32),
            pltpu.VMEM((shards, PARAM_ROWS, chan), BF16),
            pltpu.VMEM((shards, HALO, 3 * chan), BF16),
            pltpu.VMEM((shards, HALO, 4 * chan), BF16),
            pltpu.VMEM((shards, HALO, 3 * chan), BF16),
            pltpu.VMEM((shards, HALO, 4 * chan), BF16),
            pltpu.SemaphoreType.DMA((3, shards)),
            pltpu.SemaphoreType.DMA((3, shards)),
        ],
        compiler_params=remote(0),
        name="front",
    )(
        counts, feats, feats, feats, cot, jnp.transpose(short_taps, (1, 0, 2)),
        skip_gain.reshape(1, chan), residue, decay_rate, tail, feats, cot,
    )

    whole = pl.BlockSpec((3, POLES, width), lambda g: (0, 0, 0))
    y_fwd, y_bwd, res_local, seen, carries = pl.pallas_call(
        functools.partial(local_kernel, groups, shards, rounds),
        grid=(shards,),
        in_specs=[smem, pl.BlockSpec((shards, FLAT_ROWS, chan), lambda g: (0, 0, 0)), rows_spec, rows_spec, param_spec, whole],
        out_specs=[rows_spec, rows_spec, cols(HALO, 0), cols(POLES, 0),
                   pl.BlockSpec((2, POLES, width), lambda g: (0, 0, 0))],
        out_shape=[shape(ROWS, width), shape(ROWS, width), shape(HALO, width),
                   shape(POLES, width), shape(2, POLES, width)],
        scratch_shapes=[
            pltpu.VMEM((ROWS, LANES), BF16),
            pltpu.VMEM((2, POLES, width), F32),
            pltpu.VMEM((rounds, 2, POLES, width), BF16),
            pltpu.VMEM((rounds, 2, POLES, width), BF16),
            pltpu.SemaphoreType.DMA((rounds, 2)),
            pltpu.SemaphoreType.DMA((rounds, 2)),
        ],
        compiler_params=remote(1),
        name="local",
    )(counts, flat, mixed, d_long, flat, states)

    out, dfeat, dparam = pl.pallas_call(
        functools.partial(final_kernel, groups, shards),
        grid=(shards,),
        in_specs=[smem] + feat_specs + [rows_spec] * 7
        + [param_spec, planes(2, POLES), planes(1, POLES, 2), cols(POLES, 0),
           cols(HALO, 0), cols(HALO, 0)],
        out_specs=[cols(capacity, 0), anywhere, cols(GRAD_ROWS, 0)],
        out_shape=[
            shape(capacity, width, dtype=BF16),
            shape(capacity, 3 * width, dtype=BF16),
            shape(GRAD_ROWS, width),
        ],
        scratch_shapes=[
            pltpu.VMEM((ROWS, LANES), BF16),
            pltpu.VMEM((3, ROWS + HALO, LANES), F32),
            pltpu.VMEM((ROWS, TAPS * LANES), BF16),
            pltpu.VMEM((2, 3, capacity, chan), BF16),
            pltpu.SemaphoreType.DMA((2, 3)),
        ],
        compiler_params=plain,
        name="final",
    )(counts, feats, feats, feats, query, key, value, mixed, grad, y_fwd, y_bwd, flat,
      carries, states, seen, res_local, skips)
    replicas = lax.axis_size("dp")
    rows = pl.pallas_call(
        functools.partial(reduce_kernel, shards, replicas),
        in_specs=[vmem],
        out_specs=vmem,
        out_shape=shape(GRAD_ROWS, chan),
        scratch_shapes=[
            pltpu.VMEM((shards - 1, POLES, chan + chan // 2), BF16),
            pltpu.VMEM((shards - 1, POLES, chan + chan // 2), BF16),
            pltpu.VMEM((replicas, POLES, chan + chan // 2), F32),
            pltpu.SemaphoreType.DMA((shards - 1,)),
            pltpu.SemaphoreType.DMA((shards - 1,)),
            pltpu.SemaphoreType.DMA((replicas - 1,)),
            pltpu.SemaphoreType.DMA((replicas - 1,)),
        ],
        compiler_params=remote(2),
        name="reduce",
    )(dparam)
    taps, res, skip = pl.pallas_call(
        finish_kernel,
        in_specs=[vmem],
        out_specs=[vmem] * 3,
        out_shape=[shape(3, TAPS, chan), shape(POLES, chan // GROUP), shape(1, chan)],
        scratch_shapes=[pltpu.VMEM((LANES, LANES), F32)],
        name="finish",
    )(rows)
    return (
        out[None, None],
        dfeat[None, None],
        jnp.transpose(taps, (1, 0, 2)),
        res,
        skip.reshape(chan),
    )


def solution(mesh):
    in_specs = (
        P("dp", "ctx", None, None),
        P("dp", "ctx"),
        P(None, None, "ctx"),
        P(None, "ctx"),
        P(None, "ctx"),
        P("ctx"),
        P("dp", "ctx", None, None),
    )
    out_specs = (
        P("dp", "ctx", None, None),
        P("dp", "ctx", None, None),
        P(None, None, "ctx"),
        P(None, "ctx"),
        P("ctx"),
    )
    return jax.shard_map(
        per_device, mesh=mesh, in_specs=in_specs, out_specs=out_specs, check_vma=False
    )
```

```python
import functools

import jax
import jax.numpy as jnp
from jax import lax
from jax.experimental import pallas as pl
from jax.experimental.pallas import tpu as pltpu
from jax.sharding import PartitionSpec as P

TAPS = 7
HALO = 8
REACH = TAPS - 1
ROWS = 256
BLK = 128
POLES = 16
GROUP = 16
LANES = 128
PER = LANES // GROUP
F32 = jnp.float32
BF16 = jnp.bfloat16
SKIP_ROW = 3 * TAPS
RES_ROW = SKIP_ROW + 1
DEC_ROW = SKIP_ROW + 2
LOW_ROW = SKIP_ROW + 3
CNT_ROW = LOW_ROW + SKIP_ROW
PARAM_ROWS = 2 * LOW_ROW
GRAD_ROWS = 24
FLAT_ROWS = 32
CHUNK = 64
AHEAD = 2
VMEM_LIMIT = 56 << 20
MESH = pl.DeviceIdType.MESH


def iota(shape, axis):
    return lax.broadcasted_iota(jnp.int32, shape, axis)


def same_filter():
    return (iota((LANES, LANES), 0) // POLES) == (iota((LANES, LANES), 1) // GROUP)


def lane_filter(shape):
    return (iota(shape, 1) % LANES) // GROUP


def column_of(row):
    return jnp.transpose(jnp.broadcast_to(row, (LANES, LANES)))


def pick(full):
    fil = lane_filter((POLES, LANES))
    out = full[0:POLES]
    for f in range(1, PER):
        out = jnp.where(fil == f, full[f * POLES : (f + 1) * POLES], out)
    return out


def spread_rows(x):
    fil = lane_filter(x.shape)
    zero = jnp.zeros_like(x)
    return jnp.concatenate([jnp.where(fil == f, x, zero) for f in range(PER)], axis=0)


def side(x):
    return jnp.concatenate([x[0:BLK], x[BLK:ROWS]], axis=1)


def group_lanes(k):
    return pl.ds(pl.multiple_of(k * LANES, LANES), LANES)


def row_mask(shape, low, high):
    row = iota(shape, 0)
    keep = jnp.logical_and(row >= low, row < high)
    return jnp.where(keep, 1.0, 0.0).astype(BF16)


def fill(scratch, rows_bf, left, right, shift, count, own):
    capacity = rows_bf.shape[0]
    if left is not None:
        scratch[0:HALO, :] = left.astype(F32)
    shift[ROWS : ROWS + HALO, :] = right.astype(F32)
    after = shift[pl.ds(ROWS - count, ROWS), :]
    scratch[HALO : HALO + capacity, :] = (rows_bf * own).astype(F32) + after[0:capacity]
    scratch[HALO + capacity : HALO + ROWS, :] = after[capacity:ROWS]


def front_kernel(
    groups, shards, counts, fq, fk, fv, cot, taps, skip, res, dec_in, last, first, first_cot,
    q_out, k_out, v_out, m_out, g_out, d_out, states, skips, flat,
    win, shift, masks, param, packed, square, sent, tail, head, tail_in, head_in, send, recv,
):
    count = counts[0, 0]
    step = pl.program_id(0)
    capacity = cot.shape[0]
    chan = skip.shape[1]
    dp, me = lax.axis_index("dp"), lax.axis_index("ctx")
    right = (dp, lax.rem(me + 1, shards))
    left = (dp, lax.rem(me + shards - 1, shards))
    block = lax.rem(me + step, shards)

    def copy(kind, at, src, dst, peer):
        return pltpu.make_async_remote_copy(
            src_ref=src, dst_ref=dst, send_sem=send.at[kind, at], recv_sem=recv.at[kind, at],
            device_id=peer, device_id_type=MESH,
        )

    def tail_copy(at):
        theirs = lax.rem(me + 1 + at, shards)
        return copy(0, at, tail.at[theirs], tail_in.at[theirs], right)

    def head_copy(at):
        theirs = lax.rem(me + shards - 1 + at, shards)
        return copy(1, at, head.at[theirs], head_in.at[theirs], left)

    def param_copy(at):
        return copy(2, at, packed, sent.at[me], (dp, lax.rem(me + shards - at, shards)))

    def top(rows, lanes):
        return rows[:, lanes].astype(F32)[0:HALO].astype(BF16)

    def halos(at):
        @pl.when(me < shards - 1)
        def _():
            tail_copy(at).start()

        @pl.when(me > 0)
        def _():
            head_copy(at).start()

    @pl.when(step == 0)
    def _():
        for at in range(shards):
            for m in range(4):
                into = slice(m * chan, (m + 1) * chan)
                lanes = slice((m * shards + at) * chan, (m * shards + at + 1) * chan)
                if m < 3:
                    tail[at, :, into] = last[:, lanes]
                    head[at, :, into] = top(first, lanes)
                else:
                    head[at, :, into] = top(first_cot, slice(at * chan, (at + 1) * chan))
        meet([(dp, lax.rem(me + d, shards)) for d in range(1, shards)])
        halos(0)
        for m in range(3):
            param[TAPS * m : TAPS * (m + 1), :] = taps[m]
        tables = (skip[...], pole_rows(square, res[...], chan), pole_rows(square, dec_in[...], chan))
        for n, row in enumerate(tables):
            param[SKIP_ROW + n : SKIP_ROW + n + 1, :] = row
        high = param[...].astype(BF16)
        low = param[...] - high.astype(F32)
        low = jnp.where(iota(low.shape, 0) == SKIP_ROW, count.astype(F32), low)
        both = jnp.concatenate([high.astype(F32), low], axis=0).astype(BF16)
        packed[...] = both
        sent[me] = both
        for at in range(1, min(AHEAD + 1, shards)):
            param_copy(at).start()
            halos(at)

        @pl.when(me == 0)
        def _():
            tail_in[...] = jnp.zeros_like(tail_in)

        @pl.when(me == shards - 1)
        def _():
            head_in[...] = jnp.zeros_like(head_in)

        masks[0] = row_mask((ROWS, LANES), 0, count)
        masks[1] = row_mask((ROWS, LANES), 0, count + REACH)
        masks[2] = row_mask((ROWS, LANES), REACH, count + REACH)
        shift[...] = jnp.zeros_like(shift)

    @pl.when(jnp.logical_and(step > 0, step + AHEAD < shards))
    def _():
        param_copy(step + AHEAD).start()
        halos(step + AHEAD)

    @pl.when(step > 0)
    def _():
        param_copy(step).wait_recv()

    @pl.when(me > 0)
    def _():
        tail_copy(step).wait_recv()

    @pl.when(me < shards - 1)
    def _():
        head_copy(step).wait_recv()

    both = sent[block].astype(F32)
    low = both[LOW_ROW:]
    known = both[0:LOW_ROW] + jnp.where(iota(low.shape, 0) == SKIP_ROW, 0.0, low)
    param[...] = known
    flat[0, 0:LOW_ROW, :] = known
    flat[0, LOW_ROW:, :] = jnp.broadcast_to(
        both[CNT_ROW : CNT_ROW + 1], (FLAT_ROWS - LOW_ROW, chan)
    )

    def group(k):
        lanes = slice(k * LANES, (k + 1) * LANES)
        own = masks[0, 0:capacity]

        def near(ref, m):
            at = m * chan + k * LANES
            return ref[block, :, at : at + LANES]

        for m, rows in enumerate((fq, fk, fv)):
            fill(
                win.at[m], rows[:, lanes], near(tail_in, m), near(head_in, m), shift.at[m],
                count, own,
            )
        fill(win.at[3], cot[:, lanes], None, near(head_in, 3), shift.at[3], count, own)
        for r in range(0, ROWS, CHUNK):
            rows = slice(r, r + CHUNK)
            keep = masks[1, rows]
            shorts = []
            for m in range(3):
                total = param[TAPS * m : TAPS * m + 1, lanes] * win[m, HALO + r : HALO + r + CHUNK, :]
                for tap in range(1, TAPS):
                    weight = param[TAPS * m + tap : TAPS * m + tap + 1, lanes]
                    at = HALO + r - tap
                    total = total + weight * win[m, at : at + CHUNK, :]
                shorts.append(total.astype(BF16) * keep)
            query, key, value = shorts
            grad = win[3, HALO + r : HALO + r + CHUNK, :].astype(BF16) * keep
            q_out[rows, lanes] = query
            k_out[rows, lanes] = key
            v_out[rows, lanes] = value
            m_out[rows, lanes] = key * value
            g_out[rows, lanes] = grad
            d_out[rows, lanes] = grad * query

        dec = column_of(param[DEC_ROW : DEC_ROW + 1, lanes])
        lane_f = iota((LANES, LANES), 1).astype(F32)
        tab_l = jnp.exp(-dec * lane_f).astype(BF16)
        tab_r = jnp.exp(-dec * (BLK - 1.0 - lane_f)).astype(BF16)
        d_long = d_out[:, lanes]
        m_own = m_out[:, lanes] * masks[0]
        fwd = jnp.dot(tab_r, side(m_own), preferred_element_type=F32)
        bwd = jnp.dot(tab_l, side(d_long * masks[2]), preferred_element_type=F32)
        rate = pick(dec)
        first = (count - BLK).astype(F32)
        states[0, :, lanes] = jnp.exp(-rate * first) * pick(fwd[:, 0:LANES]) + jnp.exp(
            -rate * (first - BLK)
        ) * pick(fwd[:, LANES:])
        states[1, :, lanes] = jnp.exp(rate * REACH) * pick(bwd[:, 0:LANES]) + jnp.exp(
            -rate * (BLK - REACH)
        ) * pick(bwd[:, LANES:])
        states[2, :, lanes] = rate
        skips[:, lanes] = jnp.dot(
            jnp.ones((HALO, ROWS), BF16), d_long * m_own, preferred_element_type=F32
        )

    for k in range(groups):
        group(k)

    @pl.when(step == shards - 1)
    def _():
        for at in range(shards):
            @pl.when(me < shards - 1)
            def _(at=at):
                tail_copy(at).wait_send()

            @pl.when(me > 0)
            def _(at=at):
                head_copy(at).wait_send()

            if at > 0:
                param_copy(at).wait_send()


def local_group(k, m_ref, d_ref, param, masks, yf, yb, res_out, seen_out):
    lanes = slice(k * LANES, (k + 1) * LANES)
    mixed = m_ref[:, lanes]
    d_long = d_ref[:, lanes]
    res_row = param[0, RES_ROW : RES_ROW + 1, lanes]
    dec_row = param[0, DEC_ROW : DEC_ROW + 1, lanes]
    res = column_of(res_row)
    dec = column_of(dec_row)
    lane_f = iota((LANES, LANES), 1).astype(F32)
    sub_f = iota((LANES, LANES), 0).astype(F32)
    tab_l = jnp.exp(-dec * lane_f)
    tab_r = jnp.exp(-dec * (BLK - 1.0 - lane_f))
    k_lag = jnp.sum((res * tab_l).reshape(PER, POLES, LANES), axis=1)
    k_rest = jnp.sum((res * tab_r).reshape(PER, POLES, LANES), axis=1)
    k_turn = pltpu.roll(k_rest, 1, 1)
    lower = iota((BLK, BLK), 0) >= iota((BLK, BLK), 1)
    upper = iota((BLK, BLK), 0) <= iota((BLK, BLK), 1)

    def toeplitz(rows, keep):
        parts = []
        for f in range(PER):
            wide = jnp.broadcast_to(rows[f : f + 1, :], (BLK, LANES))
            wide = pltpu.roll(wide, 0, 1, stride=1, stride_axis=0)
            parts.append(jnp.where(keep, wide, 0.0).astype(BF16))
        return jnp.concatenate(parts, axis=1)

    t_fwd = toeplitz(k_turn, lower)
    yield
    own_side = side(d_long * masks[...])
    mirror = iota((BLK, BLK), 0) + iota((BLK, BLK), 1)
    flip = jnp.where(mirror == BLK - 1, 1.0, 0.0).astype(BF16)
    own_flip = jnp.dot(flip, own_side, preferred_element_type=F32).astype(BF16)
    m_stack = spread_rows(side(mixed))
    pair = lax.dot_general(
        own_flip, m_stack, (((1,), (1,)), ((), ())), preferred_element_type=F32
    )
    yield
    same = same_filter()
    tab_lb = tab_l.astype(BF16)
    s_first = jnp.dot(tab_r.astype(BF16), mixed[0:BLK], preferred_element_type=F32)
    s_first = jnp.where(same, s_first, 0.0)
    e_second = jnp.dot(tab_lb, d_long[BLK:ROWS], preferred_element_type=F32)
    e_second = jnp.where(same, e_second, 0.0).astype(BF16)
    seen = jnp.dot(tab_lb, own_side, preferred_element_type=F32)
    out_t = (res_row * jnp.exp(-dec_row * (sub_f + 1.0))).astype(BF16)
    in_t = (res_row * jnp.exp(-dec_row * (BLK - sub_f))).astype(BF16)
    y_next = jnp.dot(out_t, s_first.astype(BF16), preferred_element_type=F32)
    y_near = jnp.dot(in_t, e_second, preferred_element_type=F32)
    yield
    y_fwd = jnp.dot(t_fwd, m_stack, preferred_element_type=F32)
    yf[0:BLK, lanes] = y_fwd[:, 0:LANES]
    yf[BLK:ROWS, lanes] = y_fwd[:, LANES:] + y_next
    t_bwd = toeplitz(k_lag, upper)
    yield
    d_stack = spread_rows(side(d_long))
    y_bwd = jnp.dot(t_bwd, d_stack, preferred_element_type=F32)
    yb[0:BLK, lanes] = y_bwd[:, 0:LANES] + y_near
    yb[BLK:ROWS, lanes] = y_bwd[:, LANES:]

    yield
    lag_rows = []
    for f in range(PER):
        piece = jnp.where(mirror < BLK, pair[:, f * LANES : (f + 1) * LANES], 0.0)
        piece = pltpu.roll(piece, 0, 1, stride=1, stride_axis=0)
        lag_rows.append(jnp.broadcast_to(jnp.sum(piece, axis=0, keepdims=True), (POLES, LANES)))
    lag_sums = jnp.concatenate(lag_rows, axis=0)
    res_grad = lag_sums * tab_r + jnp.exp(-dec) * seen[:, LANES:] * s_first
    row = jnp.sum(jnp.transpose(res_grad), axis=0, keepdims=True)
    res_out[:, lanes] = jnp.broadcast_to(row, (HALO, LANES))
    rate = pick(dec)
    seen_out[:, lanes] = jnp.exp(-rate) * pick(seen[:, 0:LANES]) + jnp.exp(
        -rate * (BLK + 1.0)
    ) * pick(seen[:, LANES:])
    yield


def staggered(makers, stages, lag):
    for turn in range(stages + lag * (len(makers) - 1)):
        for k, maker in enumerate(makers):
            if 0 <= turn - lag * k < stages:
                next(maker)


def local_kernel(
    groups, shards, rounds, counts, every, m_ref, d_ref, param, states,
    yf, yb, res_out, seen_out, carries, masks, total, outbox, inbox, send, recv,
):
    step = pl.program_id(0)
    dp, me = lax.axis_index("dp"), lax.axis_index("ctx")
    chan = m_ref.shape[1]

    def peer(gap):
        return (dp, lax.rem(me + gap + shards, shards))

    def copy(j, way):
        gap = (1 << j) if way == 0 else -(1 << j)
        return pltpu.make_async_remote_copy(
            src_ref=outbox.at[j, way], dst_ref=inbox.at[j, way], send_sem=send.at[j, way],
            recv_sem=recv.at[j, way], device_id=peer(gap), device_id_type=MESH,
        )

    def sends(j, way):
        return me + (1 << j) < shards if way == 0 else me >= (1 << j)

    def start(j):
        for way in range(2):
            @pl.when(sends(j, way))
            def _(way=way):
                outbox[j, way] = total[way].astype(BF16)
                copy(j, way).start()

    def finish(j):
        for way in range(2):
            @pl.when(sends(j, 1 - way))
            def _(way=way):
                copy(j, way).wait_recv()

                gap = 1 << j
                low, high = (me - gap, me) if way == 0 else (me, me + gap)
                inner = jnp.zeros((1, chan), F32)
                for i in range(shards):
                    inside = (i > low) & (i < high)
                    inner = inner + jnp.where(inside, every[i, LOW_ROW : LOW_ROW + 1, :], 0.0)
                outer = inner + counts[0, 0].astype(F32)

                def piece(p, c):
                    lanes = pl.ds(pl.multiple_of(p * chan, LANES), chan)
                    rate = states[2, :, lanes]
                    there = inbox[j, way, :, lanes].astype(F32)
                    near = jnp.exp(-rate * inner) * there
                    carries[way, :, lanes] = carries[way, :, lanes] + near
                    if j < rounds - 1:
                        far = jnp.exp(-rate * outer) * there
                        total[way, :, lanes] = total[way, :, lanes] + far
                    return c

                lax.fori_loop(0, shards, piece, 0)

            @pl.when(sends(j, way))
            def _(way=way):
                copy(j, way).wait_send()

    @pl.when(step == 0)
    def _():
        barrier = pltpu.get_barrier_semaphore()
        greeted = 0
        for j in range(rounds):
            for way in range(2):
                there = sends(j, way)
                greeted = greeted + there.astype(jnp.int32)

                @pl.when(there)
                def _(j=j, way=way):
                    gap = (1 << j) if way == 0 else -(1 << j)
                    pl.semaphore_signal(
                        barrier, inc=1, device_id=peer(gap), device_id_type=MESH
                    )
        pl.semaphore_wait(barrier, greeted)
        masks[...] = row_mask((ROWS, LANES), 0, counts[0, 0])
        carries[...] = jnp.zeros_like(carries)
        total[...] = states[0:2]
        start(0)

    for j in range(1, rounds):
        @pl.when(step == (j * shards) // rounds)
        def _(j=j):
            finish(j - 1)
            start(j)

    makers = [
        local_group(k, m_ref, d_ref, param, masks, yf, yb, res_out, seen_out)
        for k in range(groups)
    ]
    staggered(makers, 6, 1)

    @pl.when(step == shards - 1)
    def _():
        finish(rounds - 1)


def final_kernel(
    groups, shards, counts, fq, fk, fv, q_ref, k_ref, v_ref, m_ref, g_ref, yf, yb, param,
    carries, rates, seen, res_in, skips, out, dfeat, dparam,
    own, dshort, prods, dwin, sems,
):
    count = counts[0, 0]
    step = pl.program_id(0)
    capacity = fq.shape[0]
    chan = fq.shape[1]
    slot = lax.rem(step, 2)

    def writes(at, place):
        made = []
        for m in range(3):
            lanes = pl.ds(pl.multiple_of((m * shards + at) * chan, LANES), chan)
            made.append(
                pltpu.make_async_copy(dwin.at[place, m], dfeat.at[:, lanes], sems.at[place, m])
            )
        return made

    @pl.when(step == 0)
    def _():
        own[...] = row_mask((ROWS, LANES), 0, count)
        dshort[:, ROWS:, :] = jnp.zeros((3, dshort.shape[1] - ROWS, LANES), F32)
        prods[...] = jnp.zeros_like(prods)

    @pl.when(step >= 2)
    def _():
        for copy in writes(step - 2, slot):
            copy.wait()

    dparam[GRAD_ROWS - 1 : GRAD_ROWS, :] = jnp.zeros((1, chan), F32)
    def group(k):
        lanes = slice(k * LANES, (k + 1) * LANES)
        res_row = param[0, RES_ROW : RES_ROW + 1, lanes]
        dec_row = param[0, DEC_ROW : DEC_ROW + 1, lanes]
        skip = param[0, SKIP_ROW : SKIP_ROW + 1, lanes]
        sub_f = iota((LANES, LANES), 0).astype(F32)
        out_t = (res_row * jnp.exp(-dec_row * (sub_f + 1.0))).astype(BF16)
        in_t = (res_row * jnp.exp(-dec_row * (BLK - 1.0 - sub_f))).astype(BF16)
        rate = rates[0, :, lanes]
        from_left = carries[0, :, lanes]
        from_right = carries[1, :, lanes]

        def pair(a, b):
            both = jnp.concatenate([a.astype(BF16), b.astype(BF16)], axis=1)
            return spread_rows(both)

        until = (count + (REACH + 1 - BLK)).astype(F32)
        y_left = jnp.dot(
            out_t, pair(from_left, from_left * jnp.exp(-rate * float(BLK))),
            preferred_element_type=F32,
        )
        y_right = jnp.dot(
            in_t,
            pair(from_right * jnp.exp(-rate * until), from_right * jnp.exp(-rate * (until - BLK))),
            preferred_element_type=F32,
        )
        crossed = seen[:, lanes] * from_left
        high = crossed.astype(BF16)
        low = (crossed - high.astype(F32)).astype(BF16)
        gather = (iota((LANES, LANES), 0) // GROUP) == (iota((LANES, LANES), 1) // GROUP)
        gather = jnp.where(gather, 1.0, 0.0).astype(BF16)
        sums = jnp.dot(high, gather, preferred_element_type=F32)
        sums = sums + jnp.dot(low, gather, preferred_element_type=F32)
        mine = iota((POLES, LANES), 0) == iota((POLES, LANES), 1) % POLES
        row = jnp.sum(jnp.where(mine, sums, 0.0), axis=0, keepdims=True)
        dparam[RES_ROW : RES_ROW + 1, lanes] = res_in[0:1, lanes] + row
        yield
        for r in range(0, ROWS, CHUNK):
            rows = slice(r, r + CHUNK)
            at = slice(r % BLK, r % BLK + CHUNK)
            cols = slice((r // BLK) * LANES, (r // BLK + 1) * LANES)
            kept = min(r + CHUNK, capacity) - r
            query = q_ref[rows, lanes].astype(F32)
            grad = g_ref[rows, lanes].astype(F32)
            mixed = m_ref[rows, lanes].astype(F32)
            long_out = yf[rows, lanes] + y_left[at, cols] + skip * mixed
            gated = (query * long_out).astype(BF16) * own[rows]
            out[r : r + kept, lanes] = gated[0:kept]
            dshort[0, rows, :] = grad * long_out
            d_mixed = yb[rows, lanes] + y_right[at, cols] + skip * (grad * query)
            dshort[1, rows, :] = d_mixed * v_ref[rows, lanes].astype(F32)
            dshort[2, rows, :] = d_mixed * k_ref[rows, lanes].astype(F32)

        yield
        for m, feat in enumerate((fq, fk, fv)):
            for r in range(0, ROWS, CHUNK):
                kept = min(r + CHUNK, capacity) - r
                rows = slice(r, r + kept)
                keep = own[rows]
                window = feat[rows, lanes] * keep
                total = None
                for tap in range(TAPS):
                    weight = param[0, TAPS * m + tap : TAPS * m + tap + 1, lanes]
                    shifted = dshort[m, r + tap : r + tap + kept, :]
                    term = weight * shifted
                    total = term if total is None else total + term
                    prods[rows, tap * LANES : (tap + 1) * LANES] = shifted.astype(BF16) * window
                dwin[slot, m, rows, lanes] = total.astype(BF16) * keep
            sums = jnp.dot(jnp.ones((HALO, ROWS), BF16), prods[...], preferred_element_type=F32)
            for tap in range(TAPS):
                dparam[TAPS * m + tap : TAPS * m + tap + 1, lanes] = sums[
                    0:1, tap * LANES : (tap + 1) * LANES
                ]

        dparam[SKIP_ROW : SKIP_ROW + 1, lanes] = skips[0:1, lanes]
        yield

    makers = [group(k) for k in range(groups)]
    next(makers[0])
    for k in range(groups):
        next(makers[k])
        if k + 1 < groups:
            next(makers[k + 1])
        next(makers[k])
    for copy in writes(step, slot):
        copy.start()

    @pl.when(step == shards - 1)
    def _():
        for copy in writes(step - 1, 1 - slot) + writes(step, slot):
            copy.wait()


def meet(peers):
    barrier = pltpu.get_barrier_semaphore()
    for peer in peers:
        pl.semaphore_signal(barrier, inc=1, device_id=peer, device_id_type=MESH)
    pl.semaphore_wait(barrier, len(peers))


def filter_lanes():
    return iota((PER, LANES), 1) // POLES == iota((PER, LANES), 0)


def pole_rows(square, table, chan):
    square[...] = jnp.zeros_like(square)
    square[0:POLES, 0 : chan // GROUP] = table
    turned = jnp.transpose(square[...])
    parts = []
    for g in range(chan // LANES):
        x = turned[g * PER : (g + 1) * PER]
        for gap in (POLES, 2 * POLES, 4 * POLES):
            x = x + pltpu.roll(x, gap, 1)
        parts.append(jnp.sum(jnp.where(filter_lanes(), x, 0.0), axis=0, keepdims=True))
    return jnp.concatenate(parts, axis=1)


def pole_table(square, row, chan):
    square[...] = jnp.zeros_like(square)
    for g in range(chan // LANES):
        x = jnp.broadcast_to(row[:, g * LANES : (g + 1) * LANES], (PER, LANES))
        x = jnp.where(filter_lanes(), x, 0.0)
        for gap in (POLES, 2 * POLES, 4 * POLES):
            x = x + pltpu.roll(x, gap, 1)
        square[g * PER : (g + 1) * PER, :] = x
    return jnp.transpose(square[...])[0:POLES, 0 : chan // GROUP]


def reduce_kernel(
    shards, replicas, part, out, packed, by_ctx, by_dp, send, recv, send_dp, recv_dp,
):
    dp, me = lax.axis_index("dp"), lax.axis_index("ctx")
    chan = out.shape[1]
    half = chan // 2
    peers = [(dp, lax.rem(me + d, shards)) for d in range(1, shards)]
    others = [(lax.rem(dp + d, replicas), me) for d in range(1, replicas)]

    def block(at):
        lanes = pl.ds(pl.multiple_of(at * chan, LANES), chan)
        return part[:, lanes]

    meet(peers + others)
    copies = []
    for n, peer in enumerate(peers):
        mine = block(peer[1])
        packed[n, :, 0:chan] = mine[0:POLES].astype(BF16)
        packed[n, :, chan:] = jnp.concatenate(
            [mine[POLES:, 0:half], mine[POLES:, half:]], axis=0
        ).astype(BF16)
        copies.append(
            pltpu.make_async_remote_copy(
                src_ref=packed.at[n], dst_ref=by_ctx.at[n], send_sem=send.at[n],
                recv_sem=recv.at[n], device_id=peer, device_id_type=MESH,
            )
        )
        copies[-1].start()
    total = block(me)
    top, rest = total[0:POLES], total[POLES:]
    rest = jnp.concatenate([rest[:, 0:half], rest[:, half:]], axis=0)
    for n, copy in enumerate(copies):
        copy.wait()
        top = top + by_ctx[n, :, 0:chan].astype(F32)
        rest = rest + by_ctx[n, :, chan:].astype(F32)
    mine = jnp.concatenate([top, rest], axis=1)
    by_dp[dp] = mine.astype(BF16)
    copies = []
    for n, peer in enumerate(others):
        copies.append(
            pltpu.make_async_remote_copy(
                src_ref=by_dp.at[dp], dst_ref=by_dp.at[dp], send_sem=send_dp.at[n],
                recv_sem=recv_dp.at[n], device_id=peer, device_id_type=MESH,
            )
        )
        copies[-1].start()
    for copy in copies:
        copy.wait()
    total = mine
    for n in range(1, replicas):
        total = total + by_dp[lax.rem(dp + n, replicas)].astype(F32)
    rest = total[:, chan:]
    low = POLES // 2
    rest = jnp.concatenate([rest[0:low], rest[low:]], axis=1)
    out[...] = jnp.concatenate([total[:, 0:chan], rest], axis=0)


def finish_kernel(rows, taps, res, skip, square):
    chan = rows.shape[1]
    for m in range(3):
        taps[m] = rows[TAPS * m : TAPS * (m + 1), :]
    skip[...] = rows[SKIP_ROW : SKIP_ROW + 1, :]
    res[...] = pole_table(square, rows[RES_ROW : RES_ROW + 1, :], chan)


def remote(ident):
    return pltpu.CompilerParams(
        collective_id=ident, has_side_effects=True, vmem_limit_bytes=VMEM_LIMIT
    )


def per_device(features, counts, short_taps, residue, decay_rate, skip_gain, cotangent):
    shards = lax.axis_size("ctx")
    capacity = features.shape[2]
    width = cotangent.shape[3]
    chan = short_taps.shape[2]
    groups = chan // LANES
    feats = features[0, 0]
    cot = cotangent[0, 0]
    count = counts[0, 0]

    tail = lax.dynamic_slice(feats, (count - HALO, 0), (HALO, 3 * width))
    anywhere = pl.BlockSpec(memory_space=pl.ANY)
    vmem = pl.BlockSpec(memory_space=pltpu.VMEM)
    smem = pl.BlockSpec(memory_space=pltpu.SMEM)
    rounds = (shards - 1).bit_length()

    def cols(rows, offset):
        return pl.BlockSpec((rows, chan), lambda g, *_: (0, offset * shards + g))

    def turn(g):
        return lax.rem(lax.axis_index("ctx") + g, shards)

    def turned(rows, offset):
        return pl.BlockSpec((rows, chan), lambda g: (0, offset * shards + turn(g)))

    def planes(lead, rows, first=0):
        return pl.BlockSpec((lead, rows, chan), lambda g, *_: (first, 0, g))

    def shape(*dims, dtype=F32):
        return jax.ShapeDtypeStruct(dims, dtype)

    plain = pltpu.CompilerParams(vmem_limit_bytes=VMEM_LIMIT)
    param_spec = pl.BlockSpec((1, FLAT_ROWS, chan), lambda g: (g, 0, 0))
    feat_specs = [cols(capacity, m) for m in range(3)]
    rows_spec = cols(ROWS, 0)
    rows_shape = shape(ROWS, width, dtype=BF16)
    query, key, value, mixed, grad, d_long, states, skips, flat = pl.pallas_call(
        functools.partial(front_kernel, groups, shards),
        grid=(shards,),
        in_specs=[smem] + [turned(capacity, m) for m in range(3)] + [turned(capacity, 0)]
        + [vmem] * 5
        + [pl.BlockSpec((2 * HALO, n * width), lambda g: (0, 0)) for n in (3, 1)],
        out_specs=[turned(ROWS, 0)] * 6
        + [pl.BlockSpec((3, POLES, chan), lambda g: (0, 0, turn(g))), turned(HALO, 0)]
        + [pl.BlockSpec((1, FLAT_ROWS, chan), lambda g: (turn(g), 0, 0))],
        out_shape=[rows_shape] * 6
        + [shape(3, POLES, width), shape(HALO, width), shape(shards, FLAT_ROWS, chan)],
        scratch_shapes=[
            pltpu.VMEM((4, HALO + ROWS, LANES), F32),
            pltpu.VMEM((4, 2 * ROWS + HALO, LANES), F32),
            pltpu.VMEM((3, ROWS, LANES), BF16),
            pltpu.VMEM((LOW_ROW, chan), F32),
            pltpu.VMEM((PARAM_ROWS, chan), BF16),
            pltpu.VMEM((LANES, LANES), F32),
            pltpu.VMEM((shards, PARAM_ROWS, chan), BF16),
            pltpu.VMEM((shards, HALO, 3 * chan), BF16),
            pltpu.VMEM((shards, HALO, 4 * chan), BF16),
            pltpu.VMEM((shards, HALO, 3 * chan), BF16),
            pltpu.VMEM((shards, HALO, 4 * chan), BF16),
            pltpu.SemaphoreType.DMA((3, shards)),
            pltpu.SemaphoreType.DMA((3, shards)),
        ],
        compiler_params=remote(0),
        name="front",
    )(
        counts, feats, feats, feats, cot, jnp.transpose(short_taps, (1, 0, 2)),
        skip_gain.reshape(1, chan), residue, decay_rate, tail, feats, cot,
    )

    whole = pl.BlockSpec((3, POLES, width), lambda g: (0, 0, 0))
    y_fwd, y_bwd, res_local, seen, carries = pl.pallas_call(
        functools.partial(local_kernel, groups, shards, rounds),
        grid=(shards,),
        in_specs=[smem, pl.BlockSpec((shards, FLAT_ROWS, chan), lambda g: (0, 0, 0)), rows_spec, rows_spec, param_spec, whole],
        out_specs=[rows_spec, rows_spec, cols(HALO, 0), cols(POLES, 0),
                   pl.BlockSpec((2, POLES, width), lambda g: (0, 0, 0))],
        out_shape=[shape(ROWS, width), shape(ROWS, width), shape(HALO, width),
                   shape(POLES, width), shape(2, POLES, width)],
        scratch_shapes=[
            pltpu.VMEM((ROWS, LANES), BF16),
            pltpu.VMEM((2, POLES, width), F32),
            pltpu.VMEM((rounds, 2, POLES, width), BF16),
            pltpu.VMEM((rounds, 2, POLES, width), BF16),
            pltpu.SemaphoreType.DMA((rounds, 2)),
            pltpu.SemaphoreType.DMA((rounds, 2)),
        ],
        compiler_params=remote(1),
        name="local",
    )(counts, flat, mixed, d_long, flat, states)

    out, dfeat, dparam = pl.pallas_call(
        functools.partial(final_kernel, groups, shards),
        grid=(shards,),
        in_specs=[smem] + feat_specs + [rows_spec] * 7
        + [param_spec, planes(2, POLES), planes(1, POLES, 2), cols(POLES, 0),
           cols(HALO, 0), cols(HALO, 0)],
        out_specs=[cols(capacity, 0), anywhere, cols(GRAD_ROWS, 0)],
        out_shape=[
            shape(capacity, width, dtype=BF16),
            shape(capacity, 3 * width, dtype=BF16),
            shape(GRAD_ROWS, width),
        ],
        scratch_shapes=[
            pltpu.VMEM((ROWS, LANES), BF16),
            pltpu.VMEM((3, ROWS + HALO, LANES), F32),
            pltpu.VMEM((ROWS, TAPS * LANES), BF16),
            pltpu.VMEM((2, 3, capacity, chan), BF16),
            pltpu.SemaphoreType.DMA((2, 3)),
        ],
        compiler_params=plain,
        name="final",
    )(counts, feats, feats, feats, query, key, value, mixed, grad, y_fwd, y_bwd, flat,
      carries, states, seen, res_local, skips)
    replicas = lax.axis_size("dp")
    rows = pl.pallas_call(
        functools.partial(reduce_kernel, shards, replicas),
        in_specs=[vmem],
        out_specs=vmem,
        out_shape=shape(GRAD_ROWS, chan),
        scratch_shapes=[
            pltpu.VMEM((shards - 1, POLES, chan + chan // 2), BF16),
            pltpu.VMEM((shards - 1, POLES, chan + chan // 2), BF16),
            pltpu.VMEM((replicas, POLES, chan + chan // 2), BF16),
            pltpu.SemaphoreType.DMA((shards - 1,)),
            pltpu.SemaphoreType.DMA((shards - 1,)),
            pltpu.SemaphoreType.DMA((replicas - 1,)),
            pltpu.SemaphoreType.DMA((replicas - 1,)),
        ],
        compiler_params=remote(2),
        name="reduce",
    )(dparam)
    taps, res, skip = pl.pallas_call(
        finish_kernel,
        in_specs=[vmem],
        out_specs=[vmem] * 3,
        out_shape=[shape(3, TAPS, chan), shape(POLES, chan // GROUP), shape(1, chan)],
        scratch_shapes=[pltpu.VMEM((LANES, LANES), F32)],
        name="finish",
    )(rows)
    return (
        out[None, None],
        dfeat[None, None],
        jnp.transpose(taps, (1, 0, 2)),
        res,
        skip.reshape(chan),
    )


def solution(mesh):
    in_specs = (
        P("dp", "ctx", None, None),
        P("dp", "ctx"),
        P(None, None, "ctx"),
        P(None, "ctx"),
        P(None, "ctx"),
        P("ctx"),
        P("dp", "ctx", None, None),
    )
    out_specs = (
        P("dp", "ctx", None, None),
        P("dp", "ctx", None, None),
        P(None, None, "ctx"),
        P(None, "ctx"),
        P("ctx"),
    )
    return jax.shard_map(
        per_device, mesh=mesh, in_specs=in_specs, out_specs=out_specs, check_vma=False
    )
```
